256 devices in a mesh: side: 2 (over y_hi), row: 8 (over z), col: 16 (over x, y_lo, core).
Axes of the slice: x: 4, y: 4 (y_hi: 2, y_lo: 2; y = y_hi * 2 + y_lo), z: 8, core: 2. Of those that a mesh axis runs over, the one named last changes fastest.
Arguments:
- queries: bfloat16 [512, 8192], P(('row', 'col')), may hold values from -4.5 to 16
- new_entries: bfloat16 [512, 2048], P(('row', 'col')), may hold values from -4.5 to 15.875
- cache_keys: bfloat16 [2, 512, 256, 1024], P('side', ('row', 'col')), may hold values from -4.5 to 16
- cache_values: bfloat16 [2, 512, 256, 1024], P('side', ('row', 'col')), may hold values from -6 to 6
- lengths: int32 [512], P(('row', 'col')), may hold values from 1 to 256, 32768 in all
- residual: bfloat16 [512, 8192], P(None, 'col'), may hold values from -16 to 16
- norm_gain: bfloat16 [8192], P('col'), may hold values from 0.099609375 to 1.8984375
- out_weight: bfloat16 [2, 8192, 8192], P('side', 'row', 'col'), may hold values from -0.125 to 0.125
- gate_weight: bfloat16 [2, 8192, 14336], P('side', 'col', 'row'), may hold values from -0.0625 to 0.0625
- up_weight: bfloat16 [2, 8192, 14336], P('side', 'col', 'row'), may hold values from -0.0625 to 0.0625
- down_weight: bfloat16 [2, 14336, 8192], P('side', 'row', 'col'), may hold values from -0.046875 to 0.046875
Outputs:
- layer_out: bfloat16 [512, 8192], P(('row', 'col'), 'side')
The draws below stay inside these ranges and needn't reach their ends.
All inputs are finite; a program needn't handle non-finite values. No bound on the sum of `lengths` on one device may be relied on, other than what follows from the above.
Results may differ from the reference program's by a relative error of at most 0.025.
Values may be sent and summed in bfloat16 or wider, within the bound.
No kernel may reach another device: no remote copies, remote signals or barrier semaphores. Data moves between devices by JAX's collectives and lax.ppermute only.
A program may use at most 64 MiB of HBM per device.

```python
import math
import jax
import jax.numpy as jnp
import numpy as np
from jax import lax

D = 8192
H = 64
KVH = 8
HD = 128
FF = 14336
CAP = 256
REQ_DEV = 4
REQS = 512
ORIG = 64
N_ROW = 8
N_COL = 16


def draw_queries(key, part):
    inner_key = jax.random.fold_in(key, 1)
    base = jnp.clip(jax.random.normal(inner_key, (REQS, H, HD), jnp.float32), -4.5, 4.5)
    return base.reshape(REQS, H * HD).astype(jnp.bfloat16)


def draw_new_entries(key, part):
    inner_key = jax.random.fold_in(key, 2)
    base = jnp.clip(jax.random.normal(inner_key, (REQS, 2, KVH, HD), jnp.float32), -4.5, 4.5)
    return base.reshape(REQS, 2 * KVH * HD).astype(jnp.bfloat16)


def draw_cache_keys(key, part):
    inner_key = jax.random.fold_in(key, 3)
    base = jnp.clip(jax.random.normal(inner_key, (2, REQS, CAP, KVH, HD), jnp.float32), -4.5, 4.5)
    return base.reshape(2, REQS, CAP, KVH * HD).astype(jnp.bfloat16)


def draw_residual(key, part):
    column = jnp.arange(D).astype(jnp.float32) / (D - 1)
    rise = jax.random.uniform(jax.random.fold_in(key, 41), (REQS, 1), jnp.float32, 0.0, 1.0)
    row_scale = 0.2 * 10.0 ** rise
    noise = jnp.clip(jax.random.normal(jax.random.fold_in(key, 4), (REQS, D), jnp.float32), -3.0, 3.0)
    col_scale = 0.2 * 10.0 ** column
    values = noise * row_scale * col_scale[None, :]
    return jnp.clip(values, -16.0, 16.0).astype(jnp.bfloat16)


def steps_of(stream_key, shape, cuts, least, high):
    level, own = 1.0, jax.random.fold_in(stream_key, 6)
    for axis_at, shards_of in cuts:
        steps = jnp.exp(jax.random.uniform(jax.random.fold_in(own, axis_at), (shards_of,), jnp.float32, least / len(cuts), high / len(cuts)))
        level = level * jnp.repeat(steps, shape[axis_at] // shards_of).reshape([-1 if axis == axis_at else 1 for axis in range(len(shape))])
    return level


def profile(number_of, total, reach, lean):
    loads = [(1 << 20) // math.isqrt(standing ** lean) + 1 for standing in range(2, number_of + 1)]
    spare, counts = total - reach - (number_of - 1), [1] * (number_of - 1)
    while spare > 0:
        free = [i for i in range(number_of - 1) if counts[i] < reach]
        whole, remaining = sum([loads[i] for i in free]), spare
        for i in free:
            more = min(reach - counts[i], max(1, remaining * loads[i] // whole), spare)
            counts[i] = counts[i] + more
            spare = spare - more
    return np.array([reach] + counts)


def uneven(stream_key, number_of, total, most, slope):
    if number_of == 2:
        one = jax.random.randint(stream_key, (), max(1, total - most), min(most, total - 1) + 1)
        return jnp.stack([one, total - one])
    sizes = jnp.asarray(profile(number_of, total, most, slope), jnp.int32)
    twos = (number_of - 1) // 2
    giver, taker = sizes[1:1 + 2 * twos:2], sizes[2:2 + 2 * twos:2]
    margin = jnp.minimum(giver - 1, most - taker)
    passed = jax.random.randint(jax.random.fold_in(stream_key, 1), (twos,), 0, 1 << 20) % (margin + 1)
    sizes = sizes.at[1:1 + 2 * twos:2].set(giver - passed).at[2:2 + 2 * twos:2].set(taker + passed)
    return sizes[jax.random.permutation(jax.random.fold_in(stream_key, 2), number_of)]


def centred(own_key, shape, scale, most, split=(), kind=jnp.bfloat16):
    factor_of = steps_of(own_key, shape, split, -0.22, 0.18) if split else 1.0
    values = jax.random.normal(own_key, shape, jnp.float32) * scale * factor_of
    return jnp.minimum(jnp.maximum(values, -most), most).astype(kind)


def setup_inputs(seed: int = 0) -> dict:
    seeds = jax.random.split(jax.random.key(seed), 12)
    queries = draw_queries(jax.random.fold_in(seeds[11], 71), 0)
    new_entries = draw_new_entries(jax.random.fold_in(seeds[11], 71), 0)
    cache_keys = draw_cache_keys(jax.random.fold_in(seeds[11], 71), 0)
    cache_values = centred(seeds[3], (2, REQS, CAP, KVH * HD), 1.0, 6.0, ((0, 2), (1, 128)))
    lengths = uneven(seeds[4], REQS, REQS * CAP // 4, CAP, 2).astype(jnp.int32)
    residual = draw_residual(jax.random.fold_in(seeds[11], 71), 0)
    norm_gain = jnp.clip(1.0 + 0.18 * jax.random.normal(seeds[6], (D,), jnp.float32), 0.099609375, 1.8984375).astype(jnp.bfloat16)
    out_weight = centred(seeds[7], (2, H * HD, D), (H * HD // 4) ** -0.5, 0.125, ((0, 2), (1, 8), (2, 16)))
    gate_weight = centred(seeds[8], (2, D, FF), D ** -0.5, 0.0625, ((0, 2), (1, 16), (2, 8)))
    up_weight = centred(seeds[9], (2, D, FF), D ** -0.5, 0.0625, ((0, 2), (1, 16), (2, 8)))
    down_weight = centred(seeds[10], (2, FF, D), FF ** -0.5, 0.046875, ((0, 2), (1, 8), (2, 16)))
    return dict(queries=queries, new_entries=new_entries, cache_keys=cache_keys, cache_values=cache_values, lengths=lengths, residual=residual, norm_gain=norm_gain, out_weight=out_weight, gate_weight=gate_weight, up_weight=up_weight, down_weight=down_weight)


rope_theta = 500000.0
stretch_factor = 8.0
eps = 1e-05

def frequencies(lengths):
    seq = lengths.astype(jnp.float32) + 1.0
    stretch = jnp.maximum(stretch_factor * seq / ORIG - (stretch_factor - 1.0), 1.0)
    log_base = jnp.log(jnp.float32(rope_theta)) + HD / (HD - 2.0) * jnp.log(stretch)
    expo = jnp.arange(HD // 2).astype(jnp.float32) * (2.0 / HD)
    return jnp.exp(-expo[None, :] * log_base[:, None])

def rotary(vec, angles):
    half = vec.shape[-1] // 2
    first = vec[..., :half]
    second = vec[..., half:]
    cosine = jnp.cos(angles)
    sine = jnp.sin(angles)
    return jnp.concatenate([first * cosine - second * sine, second * cosine + first * sine], axis=-1)

def attention(queries, new_entries, keys, values, lengths):
    slots = queries.shape[0]
    span = keys.shape[1]
    per_group = H // KVH
    freqs = frequencies(lengths)
    angle_new = lengths.astype(jnp.float32)[:, None] * freqs
    angle_cache = jnp.arange(span).astype(jnp.float32)[None, :, None] * freqs[:, None, :]
    query_rot = rotary(queries.astype(jnp.float32).reshape(slots, H, HD), angle_new[:, None, :])
    query_rot = lax.optimization_barrier(query_rot.astype(jnp.bfloat16)).astype(jnp.float32)
    query_rot = query_rot.reshape(slots, KVH, per_group, HD)
    key_fresh = new_entries[:, :KVH * HD].astype(jnp.float32).reshape(slots, KVH, HD)
    value_fresh = new_entries[:, KVH * HD:].astype(jnp.float32).reshape(slots, KVH, HD)
    key_new_rot = rotary(key_fresh, angle_new[:, None, :])
    key_new_rot = lax.optimization_barrier(key_new_rot.astype(jnp.bfloat16)).astype(jnp.float32)
    key_rot = rotary(keys.astype(jnp.float32).reshape(slots, span, KVH, HD), angle_cache[:, :, None, :])
    key_rot = lax.optimization_barrier(key_rot.astype(jnp.bfloat16)).astype(jnp.float32)
    scale = HD ** (-0.5)
    scores = jnp.einsum('sgqd,scgd->sgqc', query_rot, key_rot) * scale
    own_score = jnp.einsum('sgqd,sgd->sgq', query_rot, key_new_rot) * scale
    valid_mask = (jnp.arange(span)[None, :] < lengths[:, None])[:, None, None, :]
    highest = jnp.maximum(lax.optimization_barrier(jnp.max(jnp.where(valid_mask, scores, -1e+30), axis=-1)), own_score)
    weights = jnp.where(valid_mask, jnp.exp(scores - highest[..., None]), 0.0)
    own_weight = jnp.exp(own_score - highest)
    totals = lax.optimization_barrier(jnp.sum(weights, axis=-1)) + own_weight
    weights16 = lax.optimization_barrier(weights.astype(jnp.bfloat16)).astype(jnp.float32)
    cached_values = values.astype(jnp.float32).reshape(slots, span, KVH, HD)
    mixed = jnp.einsum('sgqc,scgd->sgqd', weights16, cached_values)
    mixed = mixed + own_weight[..., None] * value_fresh[:, :, None, :]
    return (mixed / totals[..., None]).reshape(slots, H * HD).astype(jnp.bfloat16)

def rounded(value):
    return lax.optimization_barrier(value.astype(jnp.bfloat16)).astype(jnp.float32)

def reference(queries, new_entries, cache_keys, cache_values, lengths, residual, norm_gain, out_weight, gate_weight, up_weight, down_weight):
    groups = REQS // REQ_DEV

    def one_block(pieces):
        return attention(pieces[0], pieces[1], pieces[2], pieces[3], pieces[4])
    attended = lax.map(one_block, (queries.reshape(groups, REQ_DEV, H * HD), new_entries.reshape(groups, REQ_DEV, 2 * KVH * HD), cache_keys[0].reshape(groups, REQ_DEV, CAP, KVH * HD), cache_values[0].reshape(groups, REQ_DEV, CAP, KVH * HD), lengths.reshape(groups, REQ_DEV)))
    attended = attended.reshape(REQS, H * HD)
    head_block = H * HD // N_ROW
    projected = jnp.zeros((REQS, D), jnp.float32)
    for block in range(N_ROW):
        lower = block * head_block
        term = jnp.dot(attended[:, lower:lower + head_block], out_weight[1, lower:lower + head_block, :], preferred_element_type=jnp.float32)
        projected = projected + rounded(term)
    stream = residual.astype(jnp.float32) + projected
    inv_rms = lax.rsqrt(lax.optimization_barrier(jnp.sum(stream * stream, axis=1)) / D + eps)
    normed = (stream * inv_rms[:, None] * norm_gain.astype(jnp.float32)[None, :]).astype(jnp.bfloat16)
    col_block = D // N_COL
    gate_sum = jnp.zeros((REQS, FF), jnp.float32)
    up_sum = jnp.zeros((REQS, FF), jnp.float32)
    for block in range(N_COL):
        lower = block * col_block
        rows_in = normed[:, lower:lower + col_block]
        gate_sum = gate_sum + rounded(jnp.dot(rows_in, gate_weight[1, lower:lower + col_block, :], preferred_element_type=jnp.float32))
        up_sum = up_sum + rounded(jnp.dot(rows_in, up_weight[1, lower:lower + col_block, :], preferred_element_type=jnp.float32))
    hidden = (jax.nn.silu(gate_sum) * up_sum).astype(jnp.bfloat16)
    unit_block = FF // N_ROW
    down_sum = jnp.zeros((REQS, D), jnp.float32)
    for block in range(N_ROW):
        lower = block * unit_block
        term = jnp.dot(hidden[:, lower:lower + unit_block], down_weight[1, lower:lower + unit_block, :], preferred_element_type=jnp.float32)
        down_sum = down_sum + rounded(term)
    return (stream + down_sum).astype(jnp.bfloat16)
```

```python
import functools
import math
import jax
import jax.numpy as jnp
from jax import lax
from jax.experimental import pallas as pl
from jax.experimental.pallas import tpu as pltpu
from jax.sharding import Mesh, PartitionSpec as P

D = 8192; H = 64; KVH = 8; HD = 128; ORIG = 64
rope_theta = 500000.0; stretch_factor = 8.0

def swap_halves(v):
    return jnp.concatenate([v[:, HD // 2:], v[:, : HD // 2]], axis=-1)

def attend_kernel(span, len_ref, q_ref, kn_ref, vn_ref, k_ref, v_ref, o_ref):
    slot = pl.program_id(0)
    length = len_ref[slot]
    lane = lax.broadcasted_iota(jnp.int32, (1, HD), 1)
    pair = jnp.where(lane < HD // 2, lane, lane - HD // 2).astype(jnp.float32)
    position = jnp.full((1, HD), length, jnp.int32).astype(jnp.float32)
    stretch = jnp.maximum(stretch_factor * (position + 1.0) / ORIG - (stretch_factor - 1.0), 1.0)
    log_base = math.log(rope_theta) + HD / (HD - 2.0) * jnp.log(stretch)
    freqs = jnp.exp(-(pair * (2.0 / HD)) * log_base)
    fine = lax.broadcasted_iota(jnp.int32, (16, HD), 0).astype(jnp.float32)
    steps = span // 16
    coarse = lax.broadcasted_iota(jnp.int32, (steps, HD), 0).astype(jnp.float32) * 16.0
    fine_cos, fine_sin = jnp.cos(fine * freqs), jnp.sin(fine * freqs)
    coarse_cos, coarse_sin = jnp.cos(coarse * freqs), jnp.sin(coarse * freqs)
    cos_parts, sin_parts = [], []
    for step in range(steps):
        cc, cs = coarse_cos[step:step + 1], coarse_sin[step:step + 1]
        cos_parts.append(cc * fine_cos - cs * fine_sin)
        sin_parts.append(cs * fine_cos + cc * fine_sin)
    cos_t = jnp.concatenate(cos_parts, axis=0)
    sin_t = jnp.concatenate(sin_parts, axis=0)
    sign = jnp.where(lane < HD // 2, -1.0, 1.0)
    cos_new = jnp.cos(position * freqs)
    sin_new = jnp.sin(position * freqs) * sign
    q = q_ref[0].astype(jnp.float32)
    q_rot = q * cos_new + swap_halves(q) * sin_new
    q_rot = q_rot.astype(jnp.bfloat16).astype(jnp.float32)
    q_both = jnp.concatenate([q_rot, swap_halves(q_rot) * -sign], axis=-1)
    k_new = kn_ref[0].astype(jnp.float32)
    k_new = k_new * cos_new + swap_halves(k_new) * sin_new
    k_new = k_new.astype(jnp.bfloat16).astype(jnp.float32)
    v_new = vn_ref[0].astype(jnp.float32)
    scale = HD ** (-0.5)
    per = H // KVH
    scores, own, fresh = [], [], []
    for g in range(KVH):
        kg = k_ref[0, 0, :, g * HD:(g + 1) * HD].astype(jnp.float32)
        kk = jnp.concatenate([(kg * cos_t).astype(jnp.bfloat16), (kg * sin_t).astype(jnp.bfloat16)], axis=-1)
        qg = q_both[g * per:(g + 1) * per].astype(jnp.bfloat16)
        scores.append(lax.dot_general(qg, kk, (((1,), (1,)), ((), ())), preferred_element_type=jnp.float32))
        own.append(jnp.sum(q_rot[g * per:(g + 1) * per] * k_new[g:g + 1], axis=-1, keepdims=True))
        fresh.append(jnp.broadcast_to(v_new[g:g + 1], (per, HD)))
    s = jnp.concatenate(scores, axis=0) * scale
    own_score = jnp.concatenate(own, axis=0) * scale
    valid = lax.broadcasted_iota(jnp.int32, (H, span), 1) < length
    s = jnp.where(valid, s, -1e30)
    top = jnp.maximum(jnp.max(s, axis=-1, keepdims=True), own_score)
    w = jnp.where(valid, jnp.exp(s - top), 0.0)
    own_w = jnp.exp(own_score - top)
    total = jnp.sum(w, axis=-1, keepdims=True) + own_w
    w16 = w.astype(jnp.bfloat16)
    mixed = []
    for p in range(KVH // 2):
        o = jnp.dot(w16[p * 2 * per:(p + 1) * 2 * per], v_ref[0, 0, :, p * 2 * HD:(p + 1) * 2 * HD], preferred_element_type=jnp.float32)
        mixed += [o[:per, :HD], o[per:, HD:]]
    out = (jnp.concatenate(mixed, axis=0) + own_w * jnp.concatenate(fresh, axis=0)) / total
    o_ref[0] = out.astype(jnp.bfloat16)

def attention(queries, new_entries, cache_keys, cache_values, lengths):
    slots = queries.shape[0]
    span = cache_keys.shape[2]
    q = queries.reshape(slots, H, HD)
    new = new_entries.reshape(slots, 2, KVH, HD)
    grid_spec = pltpu.PrefetchScalarGridSpec(
        num_scalar_prefetch=1, grid=(slots,),
        in_specs=[
            pl.BlockSpec((1, H, HD), lambda s, n: (s, 0, 0)),
            pl.BlockSpec((1, None, KVH, HD), lambda s, n: (s, 0, 0, 0)),
            pl.BlockSpec((1, None, KVH, HD), lambda s, n: (s, 1, 0, 0)),
            pl.BlockSpec((1, 1, span, KVH * HD), lambda s, n: (0, s, 0, 0)),
            pl.BlockSpec((1, 1, span, KVH * HD), lambda s, n: (0, s, 0, 0)),
        ],
        out_specs=pl.BlockSpec((1, H, HD), lambda s, n: (s, 0, 0)))
    return pl.pallas_call(
        functools.partial(attend_kernel, span), grid_spec=grid_spec,
        out_shape=jax.ShapeDtypeStruct((slots, H, HD), jnp.bfloat16),
        compiler_params=pltpu.CompilerParams(vmem_limit_bytes=32 << 20), name="attend",
    )(lengths, q, new, new, cache_keys, cache_values)

eps = 1e-05


def shift(value, axis, steps):
    count = lax.axis_size(axis)
    return lax.ppermute(value, axis, [(i, (i + steps) % count) for i in range(count)])


def from_behind(value, axis, steps):
    count = lax.axis_size(axis)
    first, last = (max(0, -steps), min(count, count - steps))
    return lax.ppermute(value, axis, [(source, source + steps) for source in range(first, last)])


def spread(value, axes):
    count = lax.axis_size(axes)
    copies = jnp.broadcast_to(value[None], (count,) + value.shape)
    return lax.all_to_all(copies, axes, split_axis=0, concat_axis=0, tiled=True)


def exchange(value, axes):
    return lax.all_to_all(value, axes, split_axis=0, concat_axis=0, tiled=True)


CHIPS = ("x", "yl")
COL = ("x", "yl", "core")


def local(queries, new_entries, cache_keys, cache_values, lengths, residual, norm_gain, out_weight, gate_weight, up_weight, down_weight):
    rows, chips = lax.axis_size("row"), lax.axis_size(CHIPS)
    row, core = lax.axis_index("row"), lax.axis_index("core")
    slots = queries.shape[0]
    head_block = H * HD // rows
    width = out_weight.shape[2]
    units = gate_weight.shape[2]
    half = units // 2
    total = rows * chips * 2 * slots
    group = total // rows

    def halves(weight, axis):
        mine = lax.dynamic_slice_in_dim(weight, core * half, half, axis)
        other = lax.dynamic_slice_in_dim(weight, (1 - core) * half, half, axis)
        return mine, other

    gate_mine, gate_other = halves(gate_weight[0], 1)
    up_mine, up_other = halves(up_weight[0], 1)
    down_mine, down_other = halves(down_weight[0], 0)
    gate_theirs = shift(gate_other, "core", 1)
    up_theirs = shift(up_other, "core", 1)
    gain_mine = norm_gain.astype(jnp.float32)
    gain_theirs = shift(norm_gain, "core", 1).astype(jnp.float32)

    attended = attention(queries, new_entries, cache_keys, cache_values, lengths)
    split_heads = attended.reshape(slots, rows, head_block).transpose(1, 0, 2)
    moved = from_behind(split_heads, "side", 1)
    blocks = exchange(moved, "row")
    near = spread(blocks, CHIPS)
    far = shift(near, "core", 1)
    both = jnp.where(core == 0, jnp.stack([near, far]), jnp.stack([far, near]))
    gathered = both.transpose(2, 1, 0, 3, 4).reshape(total, head_block)
    part = jnp.dot(gathered, out_weight[0], preferred_element_type=jnp.float32).astype(jnp.bfloat16)
    parts = exchange(part.reshape(rows, group, width), "row")
    own_residual = lax.dynamic_slice_in_dim(residual, row * group, group, 0)
    stream = own_residual.astype(jnp.float32) + jnp.sum(parts.astype(jnp.float32), axis=0)
    scaled = spread((stream * gain_mine[None, :]).astype(jnp.bfloat16), "row").reshape(total, width)
    scaled_theirs = shift(scaled, "core", 1)
    squares = jnp.sum(jnp.square(scaled.astype(jnp.float32) / gain_mine[None, :]), axis=1)
    squares = squares + jnp.sum(jnp.square(scaled_theirs.astype(jnp.float32) / gain_theirs[None, :]), axis=1)
    square_high = squares.astype(jnp.bfloat16)
    square_low = (squares - square_high.astype(jnp.float32)).astype(jnp.bfloat16)
    gate = jnp.dot(scaled, gate_mine, preferred_element_type=jnp.float32) + jnp.dot(scaled_theirs, gate_theirs, preferred_element_type=jnp.float32)
    up = jnp.dot(scaled, up_mine, preferred_element_type=jnp.float32) + jnp.dot(scaled_theirs, up_theirs, preferred_element_type=jnp.float32)
    pad = jnp.zeros((total, 126), jnp.bfloat16)
    sent = jnp.concatenate([gate.astype(jnp.bfloat16), up.astype(jnp.bfloat16), square_high[:, None], square_low[:, None], pad], axis=1)
    sums = jnp.sum(exchange(sent.reshape(chips, total // chips, 2 * half + 128), CHIPS).astype(jnp.float32), axis=0)
    inv_rms = lax.rsqrt((sums[:, 2 * half] + sums[:, 2 * half + 1]) / D + eps)
    gate_total = sums[:, :half] * inv_rms[:, None]
    up_total = sums[:, half:2 * half] * inv_rms[:, None]
    hidden_part = (jax.nn.silu(gate_total) * up_total).astype(jnp.bfloat16)
    hidden = spread(hidden_part, CHIPS).reshape(total, half)
    hidden_theirs = shift(hidden, "core", 1)
    down = jnp.dot(hidden, down_mine, preferred_element_type=jnp.float32) + jnp.dot(hidden_theirs, down_other, preferred_element_type=jnp.float32)
    downs = exchange(down.astype(jnp.bfloat16).reshape(rows, group, width), "row")
    final = (stream + jnp.sum(downs.astype(jnp.float32), axis=0)).astype(jnp.bfloat16)
    slot_rows = lax.all_to_all(final, COL, split_axis=0, concat_axis=1, tiled=True)
    half_width = slot_rows.shape[1] // 2
    returned = from_behind(slot_rows[:, :half_width], "side", -1)
    return jnp.where(lax.axis_index("side") == 0, returned, slot_rows[:, half_width:])


def solution(mesh):
    sizes = mesh.devices.shape
    inner = Mesh(mesh.devices.reshape(sizes[0], sizes[1], sizes[2] // 4, 2, 2), ("side", "row", "x", "yl", "core"))
    in_specs = (
        P(("row",) + COL, None),
        P(("row",) + COL, None),
        P("side", ("row",) + COL, None, None),
        P("side", ("row",) + COL, None, None),
        P(("row",) + COL),
        P(None, COL),
        P(COL),
        P("side", "row", COL),
        P("side", COL, "row"),
        P("side", COL, "row"),
        P("side", "row", COL),
    )
    out_specs = P(("row",) + COL, "side")
    return jax.shard_map(local, mesh=inner, in_specs=in_specs, out_specs=out_specs, check_vma=False)
```

```python
import functools
import math
import jax
import jax.numpy as jnp
from jax import lax
from jax.experimental import pallas as pl
from jax.experimental.pallas import tpu as pltpu
from jax.sharding import Mesh, PartitionSpec as P

D = 8192; H = 64; KVH = 8; HD = 128; ORIG = 64
rope_theta = 500000.0; stretch_factor = 8.0

def swap_halves(v):
    return jnp.concatenate([v[:, HD // 2:], v[:, : HD // 2]], axis=-1)

def attend_kernel(span, len_ref, q_ref, kn_ref, vn_ref, k_ref, v_ref, o_ref):
    slot = pl.program_id(0)
    length = len_ref[slot]
    lane = lax.broadcasted_iota(jnp.int32, (1, HD), 1)
    pair = jnp.where(lane < HD // 2, lane, lane - HD // 2).astype(jnp.float32)
    position = jnp.full((1, HD), length, jnp.int32).astype(jnp.float32)
    stretch = jnp.maximum(stretch_factor * (position + 1.0) / ORIG - (stretch_factor - 1.0), 1.0)
    log_base = math.log(rope_theta) + HD / (HD - 2.0) * jnp.log(stretch)
    freqs = jnp.exp(-(pair * (2.0 / HD)) * log_base)
    fine = lax.broadcasted_iota(jnp.int32, (16, HD), 0).astype(jnp.float32)
    steps = span // 16
    coarse = lax.broadcasted_iota(jnp.int32, (steps, HD), 0).astype(jnp.float32) * 16.0
    fine_cos, fine_sin = jnp.cos(fine * freqs), jnp.sin(fine * freqs)
    coarse_cos, coarse_sin = jnp.cos(coarse * freqs), jnp.sin(coarse * freqs)
    cos_parts, sin_parts = [], []
    for step in range(steps):
        cc, cs = coarse_cos[step:step + 1], coarse_sin[step:step + 1]
        cos_parts.append(cc * fine_cos - cs * fine_sin)
        sin_parts.append(cs * fine_cos + cc * fine_sin)
    cos_t = jnp.concatenate(cos_parts, axis=0)
    sin_t = jnp.concatenate(sin_parts, axis=0)
    sign = jnp.where(lane < HD // 2, -1.0, 1.0)
    cos_new = jnp.cos(position * freqs)
    sin_new = jnp.sin(position * freqs) * sign
    q = q_ref[0].astype(jnp.float32)
    q_rot = q * cos_new + swap_halves(q) * sin_new
    q_rot = q_rot.astype(jnp.bfloat16).astype(jnp.float32)
    q_both = jnp.concatenate([q_rot, swap_halves(q_rot) * -sign], axis=-1)
    k_new = kn_ref[0].astype(jnp.float32)
    k_new = k_new * cos_new + swap_halves(k_new) * sin_new
    k_new = k_new.astype(jnp.bfloat16).astype(jnp.float32)
    v_new = vn_ref[0].astype(jnp.float32)
    scale = HD ** (-0.5)
    per = H // KVH
    scores, own, fresh = [], [], []
    for g in range(KVH):
        kg = k_ref[0, 0, :, g * HD:(g + 1) * HD].astype(jnp.float32)
        kk = jnp.concatenate([(kg * cos_t).astype(jnp.bfloat16), (kg * sin_t).astype(jnp.bfloat16)], axis=-1)
        qg = q_both[g * per:(g + 1) * per].astype(jnp.bfloat16)
        scores.append(lax.dot_general(qg, kk, (((1,), (1,)), ((), ())), preferred_element_type=jnp.float32))
        own.append(jnp.sum(q_rot[g * per:(g + 1) * per] * k_new[g:g + 1], axis=-1, keepdims=True))
        fresh.append(jnp.broadcast_to(v_new[g:g + 1], (per, HD)))
    s = jnp.concatenate(scores, axis=0) * scale
    own_score = jnp.concatenate(own, axis=0) * scale
    valid = lax.broadcasted_iota(jnp.int32, (H, span), 1) < length
    s = jnp.where(valid, s, -1e30)
    top = jnp.maximum(jnp.max(s, axis=-1, keepdims=True), own_score)
    w = jnp.where(valid, jnp.exp(s - top), 0.0)
    own_w = jnp.exp(own_score - top)
    total = jnp.sum(w, axis=-1, keepdims=True) + own_w
    w16 = w.astype(jnp.bfloat16)
    mixed = []
    for p in range(KVH // 2):
        o = jnp.dot(w16[p * 2 * per:(p + 1) * 2 * per], v_ref[0, 0, :, p * 2 * HD:(p + 1) * 2 * HD], preferred_element_type=jnp.float32)
        mixed += [o[:per, :HD], o[per:, HD:]]
    out = (jnp.concatenate(mixed, axis=0) + own_w * jnp.concatenate(fresh, axis=0)) / total
    o_ref[0] = out.astype(jnp.bfloat16)

def attention(queries, new_entries, cache_keys, cache_values, lengths):
    slots = queries.shape[0]
    span = cache_keys.shape[2]
    q = queries.reshape(slots, H, HD)
    new = new_entries.reshape(slots, 2, KVH, HD)
    grid_spec = pltpu.PrefetchScalarGridSpec(
        num_scalar_prefetch=1, grid=(slots,),
        in_specs=[
            pl.BlockSpec((1, H, HD), lambda s, n: (s, 0, 0)),
            pl.BlockSpec((1, None, KVH, HD), lambda s, n: (s, 0, 0, 0)),
            pl.BlockSpec((1, None, KVH, HD), lambda s, n: (s, 1, 0, 0)),
            pl.BlockSpec((1, 1, span, KVH * HD), lambda s, n: (0, s, 0, 0)),
            pl.BlockSpec((1, 1, span, KVH * HD), lambda s, n: (0, s, 0, 0)),
        ],
        out_specs=pl.BlockSpec((1, H, HD), lambda s, n: (s, 0, 0)))
    return pl.pallas_call(
        functools.partial(attend_kernel, span), grid_spec=grid_spec,
        out_shape=jax.ShapeDtypeStruct((slots, H, HD), jnp.bfloat16),
        compiler_params=pltpu.CompilerParams(vmem_limit_bytes=60 << 20), name="attend",
    )(lengths, q, new, new, cache_keys, cache_values)

eps = 1e-05
CHIPS = ("x", "yl")
COL = ("x", "yl", "core")
ROW = ("rp", "rl")
HOME = ("rl", "rp")
WHOLE = pl.BlockSpec(memory_space=pltpu.VMEM)
SCALARS = pl.BlockSpec(memory_space=pltpu.SMEM)


def flip(value, axis):
    return lax.ppermute(value, axis, [(0, 1), (1, 0)])


def exchange(value, axes):
    return lax.all_to_all(value, axes, split_axis=0, concat_axis=0, tiled=True)


def matmul(left, right):
    return jnp.dot(left, right, preferred_element_type=jnp.float32)


def call(kernel, name, out_shape, **options):
    limit = options.pop("limit", 24)
    return pl.pallas_call(kernel, out_shape=out_shape, name=name, compiler_params=pltpu.CompilerParams(vmem_limit_bytes=limit << 20), **options)


def project_kernel(place_ref, near_ref, far_ref, own_ref, pair_ref, o_ref):
    core, low = place_ref[0], place_ref[1]
    rows, heads = near_ref.shape[0], own_ref.shape[1]
    homes = o_ref.shape[0]
    chips = rows // (homes * 4)
    to = lax.broadcasted_iota(jnp.int32, (rows, rows), 0)
    source = lax.broadcasted_iota(jnp.int32, (rows, rows), 1)
    wanted = ((to // 4) % chips) * (homes * 4) + (to // (chips * 4)) * 4 + to % 4
    order = (source == wanted).astype(jnp.bfloat16)
    for left_ref, place in ((near_ref, core), (far_ref, 1 - core)):
        part = matmul(left_ref[:, pl.ds(pl.multiple_of(low * heads, heads), heads)], own_ref[0])
        part = part + matmul(left_ref[:, pl.ds(pl.multiple_of((1 - low) * heads, heads), heads)], pair_ref[0])
        moved = matmul(order, part.astype(jnp.bfloat16)).astype(jnp.bfloat16)
        for home in range(homes):
            o_ref[home, place] = moved[home * chips * 4:(home + 1) * chips * 4]


def stream_kernel(parts_ref, residual_ref, gain_ref, stream_ref, copies_ref):
    stream = residual_ref[...].astype(jnp.float32)
    for i in range(parts_ref.shape[0]):
        stream = stream + parts_ref[i].astype(jnp.float32)
    stream_ref[...] = stream
    scaled = (stream * gain_ref[...].astype(jnp.float32)).astype(jnp.bfloat16)
    for i in range(copies_ref.shape[0]):
        copies_ref[i] = scaled


def gate_up_kernel(place_ref, mine_ref, theirs_ref, gain_ref, gain_theirs_ref, gate_ref, gate_theirs_ref, up_ref, up_theirs_ref, o_ref):
    half = gate_theirs_ref.shape[1]
    at = pl.ds(pl.multiple_of(place_ref[0] * half, half), half)
    mine, theirs = mine_ref[...], theirs_ref[...]
    o_ref[:, :half] = (matmul(mine, gate_ref[0, :, at]) + matmul(theirs, gate_theirs_ref[...])).astype(jnp.bfloat16)
    o_ref[:, half:2 * half] = (matmul(mine, up_ref[0, :, at]) + matmul(theirs, up_theirs_ref[...])).astype(jnp.bfloat16)
    one = mine.astype(jnp.float32) / gain_ref[...].astype(jnp.float32)
    two = theirs.astype(jnp.float32) / gain_theirs_ref[...].astype(jnp.float32)
    squares = jnp.sum(one * one + two * two, axis=1, keepdims=True)
    high = squares.astype(jnp.bfloat16).astype(jnp.float32)
    lane = lax.broadcasted_iota(jnp.int32, (mine.shape[0], 128), 1)
    o_ref[:, 2 * half:] = jnp.where(lane == 0, high, jnp.where(lane == 1, squares - high, 0.0)).astype(jnp.bfloat16)


def hidden_kernel(parts_ref, copies_ref):
    half = copies_ref.shape[2]
    sums = parts_ref[0].astype(jnp.float32)
    for i in range(1, parts_ref.shape[0]):
        sums = sums + parts_ref[i].astype(jnp.float32)
    squares = sums[:, 2 * half:2 * half + 1] + sums[:, 2 * half + 1:2 * half + 2]
    inv_rms = lax.rsqrt(squares / D + eps)
    gate = sums[:, :half] * inv_rms
    up = sums[:, half:2 * half] * inv_rms
    hidden = (gate / (1.0 + jnp.exp(-gate)) * up).astype(jnp.bfloat16)
    for i in range(copies_ref.shape[0]):
        copies_ref[i] = hidden


def down_kernel(place_ref, mine_ref, theirs_ref, weight_ref, o_ref):
    half = mine_ref.shape[1]
    core = place_ref[0]
    part = matmul(mine_ref[...], weight_ref[0, pl.ds(pl.multiple_of(core * half, half), half), :])
    part = part + matmul(theirs_ref[...], weight_ref[0, pl.ds(pl.multiple_of((1 - core) * half, half), half), :])
    o_ref[...] = part.astype(jnp.bfloat16)


def final_kernel(parts_ref, stream_ref, copies_ref):
    total = parts_ref[0].astype(jnp.float32)
    for i in range(1, parts_ref.shape[0]):
        total = total + parts_ref[i].astype(jnp.float32)
    final = (stream_ref[...] + total).astype(jnp.bfloat16)
    for i in range(copies_ref.shape[0]):
        copies_ref[i] = final


def local(queries, new_entries, cache_keys, cache_values, lengths, residual, norm_gain, out_weight, gate_weight, up_weight, down_weight):
    bf16 = jnp.bfloat16
    rows, pairs, chips = lax.axis_size(ROW), lax.axis_size("rp"), lax.axis_size(CHIPS)
    row, core, side = lax.axis_index(ROW), lax.axis_index("core"), lax.axis_index("side")
    slots, width = queries.shape[0], out_weight.shape[2]
    units = gate_weight.shape[2]
    half = units // 2
    group = chips * 2 * slots
    total = rows * group
    place = jnp.stack([core, lax.axis_index("rl")]).astype(jnp.int32)

    out_pair = flip(out_weight, "rl")
    gate_theirs = flip(lax.dynamic_slice_in_dim(gate_weight[0], (1 - core) * half, half, 1), "core")
    up_theirs = flip(lax.dynamic_slice_in_dim(up_weight[0], (1 - core) * half, half, 1), "core")
    gain = norm_gain[None, :]
    gain_theirs = flip(gain, "core")

    attended = attention(queries, new_entries, cache_keys, cache_values, lengths)
    by_pair = attended.reshape(slots, pairs, H * HD // pairs).transpose(1, 0, 2)
    by_pair = jnp.broadcast_to(by_pair[None], (2,) + by_pair.shape).reshape(2 * pairs, slots, H * HD // pairs)
    mine = exchange(by_pair, ("side", "rp"))[:pairs].reshape(pairs * slots, H * HD // pairs)
    near = exchange(jnp.broadcast_to(mine[None], (chips,) + mine.shape), CHIPS).reshape(chips * pairs * slots, H * HD // pairs)
    far = flip(near, "core")
    part = call(project_kernel, "project", jax.ShapeDtypeStruct((pairs, 2, group // 2, width), bf16), in_specs=[SCALARS, WHOLE, WHOLE, WHOLE, WHOLE], out_specs=WHOLE)(place, near, far, out_weight, out_pair)
    parts = exchange(part.reshape(pairs, group, width), "rp")
    own_residual = lax.dynamic_index_in_dim(residual.reshape(rows, chips, 2, slots, width), row, 0, False).transpose(1, 0, 2, 3).reshape(group, width)
    stream, copies = call(stream_kernel, "stream", (jax.ShapeDtypeStruct((group, width), jnp.float32), jax.ShapeDtypeStruct((rows, group, width), bf16)), in_specs=[WHOLE] * 3, out_specs=(WHOLE, WHOLE))(parts, own_residual, gain)
    scaled = exchange(copies, HOME).reshape(total, width)
    scaled_theirs = flip(scaled, "core")
    block = total // 4
    fixed = lambda shape: pl.BlockSpec(shape, lambda i: (0,) * len(shape))
    sent = call(gate_up_kernel, "gate_up", jax.ShapeDtypeStruct((total, units + 128), bf16), grid=(4,),
        in_specs=[SCALARS, pl.BlockSpec((block, width), lambda i: (i, 0)), pl.BlockSpec((block, width), lambda i: (i, 0)), fixed((1, width)), fixed((1, width)),
            fixed((1, width, units)), fixed((width, half)), fixed((1, width, units)), fixed((width, half))],
        out_specs=pl.BlockSpec((block, units + 128), lambda i: (i, 0)))(place, scaled, scaled_theirs, gain, gain_theirs, gate_weight, gate_theirs, up_weight, up_theirs)
    sums = exchange(sent.reshape(chips, group, units + 128), CHIPS)
    step = group // 4
    hidden = call(hidden_kernel, "hidden", jax.ShapeDtypeStruct((chips, group, half), bf16), grid=(4,),
        in_specs=[pl.BlockSpec((chips, step, units + 128), lambda i: (0, i, 0))], out_specs=pl.BlockSpec((chips, step, half), lambda i: (0, i, 0)))(sums)
    hidden = exchange(hidden, CHIPS).reshape(total, half)
    hidden_theirs = flip(hidden, "core")
    down = call(down_kernel, "down", jax.ShapeDtypeStruct((total, width), bf16), grid=(4,),
        in_specs=[SCALARS, pl.BlockSpec((block, half), lambda i: (i, 0)), pl.BlockSpec((block, half), lambda i: (i, 0)), fixed((1, units, width))],
        out_specs=pl.BlockSpec((block, width), lambda i: (i, 0)))(place, hidden, hidden_theirs, down_weight)
    downs = exchange(down.reshape(rows, group, width), HOME)
    final = call(final_kernel, "final", jax.ShapeDtypeStruct((2, group, width), bf16), in_specs=[WHOLE] * 2, out_specs=WHOLE)(downs, stream)
    back = exchange(final.reshape(2 * 2 * chips, slots, width), ("side", "core") + CHIPS)
    back = back.reshape(2, 2, lax.axis_size("x"), lax.axis_size("yl"), slots, width)[1]
    back = lax.dynamic_slice_in_dim(back, side * (lax.axis_size("x") // 2), lax.axis_size("x") // 2, 1)
    return back.transpose(3, 1, 2, 0, 4).reshape(slots, width * chips)


def solution(mesh):
    sides, rows, cols = mesh.devices.shape
    inner = Mesh(mesh.devices.reshape(sides, rows // 2, 2, cols // 4, 2, 2), ("side",) + ROW + COL)
    in_specs = (
        P(ROW + COL, None),
        P(ROW + COL, None),
        P("side", ROW + COL, None, None),
        P("side", ROW + COL, None, None),
        P(ROW + COL),
        P(None, COL),
        P(COL),
        P("side", ROW, COL),
        P("side", COL, ROW),
        P("side", COL, ROW),
        P("side", ROW, COL),
    )
    return jax.shard_map(local, mesh=inner, in_specs=in_specs, out_specs=P(ROW + COL, "side"), check_vma=False)
```

```python
import functools
import math
import jax
import jax.numpy as jnp
from jax import lax
from jax.experimental import pallas as pl
from jax.experimental.pallas import tpu as pltpu
from jax.sharding import Mesh, PartitionSpec as P

D = 8192
H = 64
KVH = 8
HD = 128
ORIG = 64
PER = H // KVH

rope_theta = 500000.0
stretch_factor = 8.0
eps = 1e-05

CHIPS = ("x", "yl")
COL = ("x", "yl", "core")
ROW = ("rp", "rl")
HOME = ("side", "rl", "rp")
WHOLE = pl.BlockSpec(memory_space=pltpu.VMEM)
SCALARS = pl.BlockSpec(memory_space=pltpu.SMEM)


def swap_halves(v):
    return jnp.concatenate([v[:, HD // 2:], v[:, : HD // 2]], axis=-1)


def attend_kernel(len_ref, q_ref, new_ref, k_lo_ref, k_hi_ref, v_lo_ref, v_hi_ref, o_ref, q_all, new_all, s_all, acc, out_all):
    slot = pl.program_id(0)
    slots = q_ref.shape[0]
    length = len_ref[slot]
    half = k_lo_ref.shape[2]
    span = 2 * half

    @pl.when(slot == 0)
    def _():
        for h in range(H):
            q_all[:, h, :] = q_ref[:, h * HD:(h + 1) * HD].astype(jnp.float32)
        for h in range(2 * KVH):
            new_all[:, h, :] = new_ref[:, h * HD:(h + 1) * HD].astype(jnp.float32)

    lane = lax.broadcasted_iota(jnp.int32, (1, HD), 1)
    pair = jnp.where(lane < HD // 2, lane, lane - HD // 2).astype(jnp.float32)
    position = jnp.full((1, HD), length, jnp.int32).astype(jnp.float32)
    stretch = jnp.maximum(stretch_factor * (position + 1.0) / ORIG - (stretch_factor - 1.0), 1.0)
    log_base = math.log(rope_theta) + HD / (HD - 2.0) * jnp.log(stretch)
    freqs = jnp.exp(-(pair * (2.0 / HD)) * log_base)
    steps = span // 16
    fine = lax.broadcasted_iota(jnp.int32, (16, HD), 0).astype(jnp.float32)
    coarse = lax.broadcasted_iota(jnp.int32, (steps, HD), 0).astype(jnp.float32) * 16.0
    fine_cos, fine_sin = jnp.cos(fine * freqs), jnp.sin(fine * freqs)
    coarse_cos, coarse_sin = jnp.cos(coarse * freqs), jnp.sin(coarse * freqs)

    def tables(first):
        cos_parts, sin_parts = [], []
        for step in range(first, first + steps // 2):
            cc, cs = coarse_cos[step:step + 1], coarse_sin[step:step + 1]
            cos_parts.append(cc * fine_cos - cs * fine_sin)
            sin_parts.append(cs * fine_cos + cc * fine_sin)
        return jnp.concatenate(cos_parts, axis=0), jnp.concatenate(sin_parts, axis=0)

    sign = jnp.where(lane < HD // 2, -1.0, 1.0)
    cos_new = jnp.cos(position * freqs)
    sin_new = jnp.sin(position * freqs) * sign
    q = q_all[slot]
    q_rot = q * cos_new + swap_halves(q) * sin_new
    q_rot = q_rot.astype(jnp.bfloat16).astype(jnp.float32)
    q_both = jnp.concatenate([q_rot, swap_halves(q_rot) * -sign], axis=-1)
    k_new = new_all[slot, :KVH]
    k_new = k_new * cos_new + swap_halves(k_new) * sin_new
    k_new = k_new.astype(jnp.bfloat16).astype(jnp.float32)
    v_new = new_all[slot, KVH:]
    scale = HD ** (-0.5)

    def score(k_ref, first):
        cos_t, sin_t = tables(first)
        for g in range(KVH):
            kg = k_ref[0, 0, :, g * HD:(g + 1) * HD].astype(jnp.float32)
            kk = jnp.concatenate([(kg * cos_t).astype(jnp.bfloat16), (kg * sin_t).astype(jnp.bfloat16)], axis=-1)
            qg = q_both[g * PER:(g + 1) * PER].astype(jnp.bfloat16)
            s_all[g * PER:(g + 1) * PER, first * 16:first * 16 + half] = lax.dot_general(qg, kk, (((1,), (1,)), ((), ())), preferred_element_type=jnp.float32)

    score(k_lo_ref, 0)

    @pl.when(length > half)
    def _():
        score(k_hi_ref, steps // 2)

    @pl.when(length <= half)
    def _():
        s_all[:, half:] = jnp.zeros((H, half), jnp.float32)

    own, fresh = [], []
    for g in range(KVH):
        own.append(jnp.sum(q_rot[g * PER:(g + 1) * PER] * k_new[g:g + 1], axis=-1, keepdims=True))
        fresh.append(jnp.broadcast_to(v_new[g:g + 1], (PER, HD)))
    own_score = jnp.concatenate(own, axis=0) * scale
    valid = lax.broadcasted_iota(jnp.int32, (H, span), 1) < length
    s = jnp.where(valid, s_all[...] * scale, -1e30)
    top = jnp.maximum(jnp.max(s, axis=-1, keepdims=True), own_score)
    w = jnp.where(valid, jnp.exp(s - top), 0.0)
    own_w = jnp.exp(own_score - top)
    total = jnp.sum(w, axis=-1, keepdims=True) + own_w
    w16 = w.astype(jnp.bfloat16)

    def mix(v_ref, weights):
        parts = []
        for p in range(KVH // 2):
            o = jnp.dot(weights[p * 2 * PER:(p + 1) * 2 * PER], v_ref[0, 0, :, p * 2 * HD:(p + 1) * 2 * HD], preferred_element_type=jnp.float32)
            parts += [o[:PER, :HD], o[PER:, HD:]]
        return jnp.concatenate(parts, axis=0)

    acc[...] = mix(v_lo_ref, w16[:, :half]) + own_w * jnp.concatenate(fresh, axis=0)

    @pl.when(length > half)
    def _():
        acc[...] += mix(v_hi_ref, w16[:, half:])

    out = acc[...] / total
    sides = 2
    pairs = o_ref.shape[0] // sides
    heads = H // (pairs * 2 * sides)
    for h in range(H):
        block, q_at = h // heads, h % heads
        side, low, home = block % sides, (block // sides) % 2, block // (2 * sides)
        at = (low * heads + q_at) * HD
        out_all[slot, side * pairs + home:side * pairs + home + 1, at:at + HD] = out[h:h + 1]

    @pl.when(slot == slots - 1)
    def _():
        for d in range(o_ref.shape[0]):
            o_ref[d] = jnp.concatenate([out_all[j, d:d + 1] for j in range(slots)], axis=0).astype(jnp.bfloat16)


def attention(queries, new_entries, cache_keys, cache_values, lengths, pairs):
    slots = queries.shape[0]
    half = cache_keys.shape[2] // 2
    width = KVH * HD
    low = pl.BlockSpec((1, 1, half, width), lambda s, n: (0, s, 0, 0))

    def last_long(s, n):
        at = 0
        for j in range(1, slots):
            at = jnp.where((s >= j) & (n[j] > half), j, at)
        return (0, at, 1, 0)

    high = pl.BlockSpec((1, 1, half, width), last_long)
    heads = H * HD // (2 * pairs)
    grid_spec = pltpu.PrefetchScalarGridSpec(
        num_scalar_prefetch=1, grid=(slots,),
        in_specs=[pl.BlockSpec((slots, H * HD), lambda s, n: (0, 0)), pl.BlockSpec((slots, 2 * width), lambda s, n: (0, 0)), low, high, low, high],
        out_specs=pl.BlockSpec((2 * pairs, slots, heads), lambda s, n: (0, 0, 0)),
        scratch_shapes=[
            pltpu.VMEM((slots, H, HD), jnp.float32), pltpu.VMEM((slots, 2 * KVH, HD), jnp.float32),
            pltpu.VMEM((H, 2 * half), jnp.float32), pltpu.VMEM((H, HD), jnp.float32), pltpu.VMEM((slots, 2 * pairs, heads), jnp.float32)])
    return pl.pallas_call(
        attend_kernel, grid_spec=grid_spec,
        out_shape=jax.ShapeDtypeStruct((2 * pairs, slots, heads), jnp.bfloat16),
        compiler_params=pltpu.CompilerParams(vmem_limit_bytes=60 << 20), name="attend",
    )(lengths, queries, new_entries, cache_keys, cache_keys, cache_values, cache_values)


def flip(value, axis):
    return lax.ppermute(value, axis, [(0, 1), (1, 0)])


def from_ffn(value):
    return lax.ppermute(value, "side", [(1, 0)])


def exchange(value, axes):
    return lax.all_to_all(value, axes, split_axis=0, concat_axis=0, tiled=True)


def matmul(left, right):
    return jnp.dot(left, right, preferred_element_type=jnp.float32)


def call(kernel, name, out_shape, **options):
    return pl.pallas_call(kernel, out_shape=out_shape, name=name, compiler_params=pltpu.CompilerParams(vmem_limit_bytes=24 << 20), **options)


def project_kernel(place_ref, near_ref, far_ref, own_ref, pair_ref, o_ref):
    core, low = place_ref[0], place_ref[1]
    rows, heads = near_ref.shape[0], own_ref.shape[0]
    homes = o_ref.shape[1]
    chips = rows // (homes * 4)
    to = lax.broadcasted_iota(jnp.int32, (rows, rows), 0)
    source = lax.broadcasted_iota(jnp.int32, (rows, rows), 1)
    wanted = ((to // 4) % chips) * (homes * 4) + (to // (chips * 4)) * 4 + to % 4
    order = (source == wanted).astype(jnp.bfloat16)
    for left_ref, place in ((near_ref, core), (far_ref, 1 - core)):
        part = matmul(left_ref[:, pl.ds(pl.multiple_of(low * heads, heads), heads)], own_ref[...])
        part = part + matmul(left_ref[:, pl.ds(pl.multiple_of((1 - low) * heads, heads), heads)], pair_ref[...])
        moved = matmul(order, part.astype(jnp.bfloat16)).astype(jnp.bfloat16)
        for home in range(homes):
            o_ref[place, home] = moved[home * chips * 4:(home + 1) * chips * 4]


def stream_kernel(parts_ref, residual_ref, gain_ref, stream_ref, copies_ref):
    stream = residual_ref[...].astype(jnp.float32)
    for i in range(parts_ref.shape[0]):
        stream = stream + parts_ref[i].astype(jnp.float32)
    stream_ref[...] = stream
    scaled = (stream * gain_ref[...].astype(jnp.float32)).astype(jnp.bfloat16)
    for i in range(copies_ref.shape[0]):
        copies_ref[i] = scaled


def gate_up_kernel(merge, place_ref, x_ref, gain_ref, gate_in_ref, up_in_ref, gate_ref, up_ref, *rest):
    other_ref, o_ref = rest if merge else (None, rest[0])
    side = place_ref[2]
    units = gate_in_ref.shape[1]
    x = x_ref[...]

    def fill(gate_weight, up_weight):
        gate, up = matmul(x, gate_weight), matmul(x, up_weight)
        if merge:
            gate = gate + other_ref[:, :units].astype(jnp.float32)
            up = up + other_ref[:, units:2 * units].astype(jnp.float32)
        o_ref[:, :units] = gate.astype(jnp.bfloat16)
        o_ref[:, units:2 * units] = up.astype(jnp.bfloat16)

    @pl.when(side == 0)
    def _():
        fill(gate_in_ref[...], up_in_ref[...])

    @pl.when(side != 0)
    def _():
        fill(gate_ref[0, :, units:], up_ref[0, :, units:])

    one = x.astype(jnp.float32) / gain_ref[...].astype(jnp.float32)
    squares = jnp.sum(one * one, axis=1, keepdims=True)
    if merge:
        tail = other_ref[:, 2 * units:].astype(jnp.float32)
        squares = squares + tail[:, 0:1] + tail[:, 1:2]
    high = squares.astype(jnp.bfloat16).astype(jnp.float32)
    lane = lax.broadcasted_iota(jnp.int32, (x.shape[0], 128), 1)
    o_ref[:, 2 * units:] = jnp.where(lane == 0, high, jnp.where(lane == 1, squares - high, 0.0)).astype(jnp.bfloat16)


def hidden_kernel(parts_ref, copies_ref):
    units = copies_ref.shape[2]
    sums = parts_ref[0].astype(jnp.float32)
    for i in range(1, parts_ref.shape[0]):
        sums = sums + parts_ref[i].astype(jnp.float32)
    squares = sums[:, 2 * units:2 * units + 1] + sums[:, 2 * units + 1:2 * units + 2]
    inv_rms = lax.rsqrt(squares / D + eps)
    gate = sums[:, :units] * inv_rms
    up = sums[:, units:2 * units] * inv_rms
    hidden = (gate / (1.0 + jnp.exp(-gate)) * up).astype(jnp.bfloat16)
    for i in range(copies_ref.shape[0]):
        copies_ref[i] = hidden


def down_kernel(place_ref, mine_ref, theirs_ref, weight_in_ref, weight_ref, o_ref):
    core, side = place_ref[0], place_ref[2]
    units = weight_in_ref.shape[0]

    def fill(weight):
        o_ref[core] = matmul(mine_ref[...], weight).astype(jnp.bfloat16)
        o_ref[1 - core] = matmul(theirs_ref[...], weight).astype(jnp.bfloat16)

    @pl.when(side == 0)
    def _():
        fill(weight_in_ref[...])

    @pl.when(side != 0)
    def _():
        fill(weight_ref[0, units:, :])


def final_kernel(parts_ref, stream_ref, copies_ref):
    total = parts_ref[0].astype(jnp.float32)
    for i in range(1, parts_ref.shape[0]):
        total = total + parts_ref[i].astype(jnp.float32)
    final = (stream_ref[...] + total).astype(jnp.bfloat16)
    for i in range(copies_ref.shape[0]):
        copies_ref[i] = final


def local(queries, new_entries, cache_keys, cache_values, lengths, residual, norm_gain, out_weight, gate_weight, up_weight, down_weight):
    bf16 = jnp.bfloat16
    rows, pairs, chips = lax.axis_size(ROW), lax.axis_size("rp"), lax.axis_size(CHIPS)
    row, core, side = lax.axis_index(ROW), lax.axis_index("core"), lax.axis_index("side")
    slots, width = queries.shape[0], out_weight.shape[2]
    head_part = out_weight.shape[1] // 2
    units = gate_weight.shape[2] // 2
    group = chips * slots
    total = rows * 2 * group
    place = jnp.stack([core, lax.axis_index("rl"), side]).astype(jnp.int32)

    out_own = jnp.where(side == 0, from_ffn(out_weight[0, :head_part]), out_weight[0, head_part:])
    out_pair = flip(out_own, "rl")
    gain = norm_gain[None, :]

    by_pair = attention(queries, new_entries, cache_keys, cache_values, lengths, pairs)
    by_pair, gate_late, up_late, down_late = lax.optimization_barrier((by_pair, gate_weight, up_weight, down_weight))
    gate_in = from_ffn(gate_late[0, :, :units])
    up_in = from_ffn(up_late[0, :, :units])
    down_in = from_ffn(down_late[0, :units])
    mine = exchange(by_pair, ("side", "rp"))[:pairs].reshape(pairs * slots, 2 * head_part)
    near = exchange(jnp.broadcast_to(mine[None], (chips,) + mine.shape), CHIPS).reshape(chips * pairs * slots, 2 * head_part)
    far = flip(near, "core")
    part = call(project_kernel, "project", jax.ShapeDtypeStruct((2, pairs, group, width), bf16), in_specs=[SCALARS, WHOLE, WHOLE, WHOLE, WHOLE], out_specs=WHOLE)(place, near, far, out_own, out_pair)
    parts = exchange(part.reshape(2 * pairs, group, width), ("side", "rp"))
    own_residual = lax.dynamic_slice(residual.reshape(rows, chips, 2, slots, width), (row, 0, side, 0, 0), (1, chips, 1, slots, width)).reshape(group, width)
    stream, copies = call(stream_kernel, "stream", (jax.ShapeDtypeStruct((group, width), jnp.float32), jax.ShapeDtypeStruct((2 * rows, group, width), bf16)), in_specs=[WHOLE] * 3, out_specs=(WHOLE, WHOLE))(parts, own_residual, gain)
    scaled = exchange(copies, HOME).reshape(total, width)

    steps = 2
    block = total // (2 * steps)
    wide = 2 * units + 128

    def gate_up(which, name, *other):
        fixed = lambda shape: pl.BlockSpec(shape, lambda i, p: (0,) * len(shape))
        piece = pl.BlockSpec((block, wide), lambda i, p: (i, 0))
        grid_spec = pltpu.PrefetchScalarGridSpec(
            num_scalar_prefetch=1, grid=(steps,),
            in_specs=[pl.BlockSpec((block, width), lambda i, p: (which(p[0]) * steps + i, 0)), fixed((1, width)), fixed((width, units)), fixed((width, units)),
                fixed((1, width, 2 * units)), fixed((1, width, 2 * units))] + [piece] * len(other),
            out_specs=piece)
        return call(functools.partial(gate_up_kernel, bool(other)), name, jax.ShapeDtypeStruct((total // 2, wide), bf16), grid_spec=grid_spec)(
            place, scaled, gain, gate_in, up_in, gate_weight, up_weight, *other)

    far_part = gate_up(lambda c: 1 - c, "gate_up_far")
    sent = gate_up(lambda c: c, "gate_up_near", flip(far_part, "core"))
    share = total // (2 * chips)
    sums = exchange(sent.reshape(chips, share, wide), CHIPS)
    hidden = call(hidden_kernel, "hidden", jax.ShapeDtypeStruct((chips, share, units), bf16), grid=(2,),
        in_specs=[pl.BlockSpec((chips, share // 2, wide), lambda i: (0, i, 0))], out_specs=pl.BlockSpec((chips, share // 2, units), lambda i: (0, i, 0)))(sums)
    hidden = exchange(hidden, CHIPS).reshape(total // 2, units)
    down = call(down_kernel, "down", jax.ShapeDtypeStruct((2, total // 2, width), bf16), in_specs=[SCALARS] + [WHOLE] * 4, out_specs=WHOLE)(
        place, hidden, flip(hidden, "core"), down_in, down_weight)
    downs = exchange(down.reshape(2 * rows, group, width), HOME)
    final = call(final_kernel, "final", jax.ShapeDtypeStruct((4, group, width), bf16), in_specs=[WHOLE] * 2, out_specs=WHOLE)(downs, stream)
    back = exchange(final.reshape(4 * chips, slots, width), ("side", "core") + CHIPS)
    back = back.reshape(2, 2, lax.axis_size("x"), lax.axis_size("yl"), slots, width)
    half = lax.axis_size("x") // 2
    back = lax.dynamic_slice(back, (core, 0, side * half, 0, 0, 0), (1, 2, half, lax.axis_size("yl"), slots, width))[0]
    return back.transpose(3, 1, 2, 0, 4).reshape(slots, width * chips)


def solution(mesh):
    sides, rows, cols = mesh.devices.shape
    inner = Mesh(mesh.devices.reshape(sides, rows // 2, 2, cols // 4, 2, 2), ("side",) + ROW + COL)
    in_specs = (
        P(ROW + COL, None),
        P(ROW + COL, None),
        P("side", ROW + COL, None, None),
        P("side", ROW + COL, None, None),
        P(ROW + COL),
        P(None, COL),
        P(COL),
        P("side", ROW, COL),
        P("side", COL, ROW),
        P("side", COL, ROW),
        P("side", ROW, COL),
    )
    return jax.shard_map(local, mesh=inner, in_specs=in_specs, out_specs=P(ROW + COL, "side"), check_vma=False)
```

```python
import functools
import math
import jax
import jax.numpy as jnp
from jax import lax
from jax.experimental import pallas as pl
from jax.experimental.pallas import tpu as pltpu
from jax.sharding import Mesh, PartitionSpec as P

D = 8192
H = 64
KVH = 8
HD = 128
ORIG = 64
PER = H // KVH

rope_theta = 500000.0
stretch_factor = 8.0
eps = 1e-05

CHIPS = ("x", "yl")
COL = ("x", "yl", "core")
ROW = ("rp", "rl")
HOME = ("side", "rl", "rp")
WHOLE = pl.BlockSpec(memory_space=pltpu.VMEM)
HELD = pl.BlockSpec(memory_space=pl.ANY)
SCALARS = pl.BlockSpec(memory_space=pltpu.SMEM)


def swap_halves(v):
    return jnp.concatenate([v[:, HD // 2:], v[:, : HD // 2]], axis=-1)


def attend_kernel(len_ref, q_ref, new_ref, k_lo_ref, k_hi_ref, v_lo_ref, v_hi_ref, o_ref, q_all, new_all, s_all, acc, out_all):
    slot = pl.program_id(0)
    slots = q_ref.shape[0]
    length = len_ref[slot]
    half = k_lo_ref.shape[2]
    span = 2 * half

    @pl.when(slot == 0)
    def _():
        for h in range(H):
            q_all[:, h, :] = q_ref[:, h * HD:(h + 1) * HD].astype(jnp.float32)
        for h in range(2 * KVH):
            new_all[:, h, :] = new_ref[:, h * HD:(h + 1) * HD].astype(jnp.float32)

    lane = lax.broadcasted_iota(jnp.int32, (1, HD), 1)
    pair = jnp.where(lane < HD // 2, lane, lane - HD // 2).astype(jnp.float32)
    position = jnp.full((1, HD), length, jnp.int32).astype(jnp.float32)
    stretch = jnp.maximum(stretch_factor * (position + 1.0) / ORIG - (stretch_factor - 1.0), 1.0)
    log_base = math.log(rope_theta) + HD / (HD - 2.0) * jnp.log(stretch)
    freqs = jnp.exp(-(pair * (2.0 / HD)) * log_base)
    steps = span // 16
    fine = lax.broadcasted_iota(jnp.int32, (16, HD), 0).astype(jnp.float32)
    coarse = lax.broadcasted_iota(jnp.int32, (steps, HD), 0).astype(jnp.float32) * 16.0
    fine_cos, fine_sin = jnp.cos(fine * freqs), jnp.sin(fine * freqs)
    coarse_cos, coarse_sin = jnp.cos(coarse * freqs), jnp.sin(coarse * freqs)

    def tables(first):
        cos_parts, sin_parts = [], []
        for step in range(first, first + steps // 2):
            cc, cs = coarse_cos[step:step + 1], coarse_sin[step:step + 1]
            cos_parts.append(cc * fine_cos - cs * fine_sin)
            sin_parts.append(cs * fine_cos + cc * fine_sin)
        return jnp.concatenate(cos_parts, axis=0), jnp.concatenate(sin_parts, axis=0)

    sign = jnp.where(lane < HD // 2, -1.0, 1.0)
    cos_new = jnp.cos(position * freqs)
    sin_new = jnp.sin(position * freqs) * sign
    q = q_all[slot]
    q_rot = q * cos_new + swap_halves(q) * sin_new
    q_rot = q_rot.astype(jnp.bfloat16).astype(jnp.float32)
    q_both = jnp.concatenate([q_rot, swap_halves(q_rot) * -sign], axis=-1)
    k_new = new_all[slot, :KVH]
    k_new = k_new * cos_new + swap_halves(k_new) * sin_new
    k_new = k_new.astype(jnp.bfloat16).astype(jnp.float32)
    v_new = new_all[slot, KVH:]
    scale = HD ** (-0.5)

    def score(k_ref, first):
        cos_t, sin_t = tables(first)
        for g in range(KVH):
            kg = k_ref[0, 0, :, g * HD:(g + 1) * HD].astype(jnp.float32)
            kk = jnp.concatenate([(kg * cos_t).astype(jnp.bfloat16), (kg * sin_t).astype(jnp.bfloat16)], axis=-1)
            qg = q_both[g * PER:(g + 1) * PER].astype(jnp.bfloat16)
            s_all[g * PER:(g + 1) * PER, first * 16:first * 16 + half] = lax.dot_general(qg, kk, (((1,), (1,)), ((), ())), preferred_element_type=jnp.float32)

    score(k_lo_ref, 0)

    @pl.when(length > half)
    def _():
        score(k_hi_ref, steps // 2)

    @pl.when(length <= half)
    def _():
        s_all[:, half:] = jnp.zeros((H, half), jnp.float32)

    own, fresh = [], []
    for g in range(KVH):
        own.append(jnp.sum(q_rot[g * PER:(g + 1) * PER] * k_new[g:g + 1], axis=-1, keepdims=True))
        fresh.append(jnp.broadcast_to(v_new[g:g + 1], (PER, HD)))
    own_score = jnp.concatenate(own, axis=0) * scale
    valid = lax.broadcasted_iota(jnp.int32, (H, span), 1) < length
    s = jnp.where(valid, s_all[...] * scale, -1e30)
    top = jnp.maximum(jnp.max(s, axis=-1, keepdims=True), own_score)
    w = jnp.where(valid, jnp.exp(s - top), 0.0)
    own_w = jnp.exp(own_score - top)
    total = jnp.sum(w, axis=-1, keepdims=True) + own_w
    w16 = w.astype(jnp.bfloat16)

    def mix(v_ref, weights):
        parts = []
        for p in range(KVH // 2):
            o = jnp.dot(weights[p * 2 * PER:(p + 1) * 2 * PER], v_ref[0, 0, :, p * 2 * HD:(p + 1) * 2 * HD], preferred_element_type=jnp.float32)
            parts += [o[:PER, :HD], o[PER:, HD:]]
        return jnp.concatenate(parts, axis=0)

    acc[...] = mix(v_lo_ref, w16[:, :half]) + own_w * jnp.concatenate(fresh, axis=0)

    @pl.when(length > half)
    def _():
        acc[...] += mix(v_hi_ref, w16[:, half:])

    out = acc[...] / total
    sides = 2
    pairs = o_ref.shape[0] // sides
    heads = H // (pairs * 2 * sides)
    for h in range(H):
        block, q_at = h // heads, h % heads
        side, low, home = block % sides, (block // sides) % 2, block // (2 * sides)
        at = (side * pairs + home) * 2 + low
        out_all[slot, at:at + 1, q_at * HD:(q_at + 1) * HD] = out[h:h + 1]

    @pl.when(slot == slots - 1)
    def _():
        for d in range(o_ref.shape[0]):
            o_ref[d] = jnp.concatenate([out_all[j, 2 * d:2 * d + 2] for j in range(slots)], axis=0).astype(jnp.bfloat16)


def attention(queries, new_entries, cache_keys, cache_values, lengths, pairs):
    slots = queries.shape[0]
    half = cache_keys.shape[2] // 2
    width = KVH * HD
    low = pl.BlockSpec((1, 1, half, width), lambda s, n: (0, s, 0, 0))

    def last_long(s, n):
        at = 0
        for j in range(1, slots):
            at = jnp.where((s >= j) & (n[j] > half), j, at)
        return (0, at, 1, 0)

    high = pl.BlockSpec((1, 1, half, width), last_long)
    heads = H * HD // (4 * pairs)
    grid_spec = pltpu.PrefetchScalarGridSpec(
        num_scalar_prefetch=1, grid=(slots,),
        in_specs=[pl.BlockSpec((slots, H * HD), lambda s, n: (0, 0)), pl.BlockSpec((slots, 2 * width), lambda s, n: (0, 0)), low, high, low, high],
        out_specs=pl.BlockSpec((2 * pairs, 2 * slots, heads), lambda s, n: (0, 0, 0)),
        scratch_shapes=[
            pltpu.VMEM((slots, H, HD), jnp.float32), pltpu.VMEM((slots, 2 * KVH, HD), jnp.float32),
            pltpu.VMEM((H, 2 * half), jnp.float32), pltpu.VMEM((H, HD), jnp.float32), pltpu.VMEM((slots, 4 * pairs, heads), jnp.float32)])
    return pl.pallas_call(
        attend_kernel, grid_spec=grid_spec,
        out_shape=jax.ShapeDtypeStruct((2 * pairs, 2 * slots, heads), jnp.bfloat16),
        compiler_params=pltpu.CompilerParams(vmem_limit_bytes=60 << 20), name="attend",
    )(lengths, queries, new_entries, cache_keys, cache_keys, cache_values, cache_values)


def flip(value, axis):
    return lax.ppermute(value, axis, [(0, 1), (1, 0)])


def from_ffn(value):
    return lax.ppermute(value, "side", [(1, 0)])


def exchange(value, axes):
    return lax.all_to_all(value, axes, split_axis=0, concat_axis=0, tiled=True)


def matmul(left, right):
    return jnp.dot(left, right, preferred_element_type=jnp.float32)


def call(kernel, name, out_shape, **options):
    return pl.pallas_call(kernel, out_shape=out_shape, name=name, compiler_params=pltpu.CompilerParams(vmem_limit_bytes=24 << 20), **options)


def project_kernel(place_ref, near_ref, far_ref, own_ref, pair_ref, held_ref, o_ref):
    core, low = place_ref[0], place_ref[1]
    homes, group = o_ref.shape[1], o_ref.shape[2]
    rows = homes * group
    to = lax.broadcasted_iota(jnp.int32, (rows, 2 * rows), 0)
    source = lax.broadcasted_iota(jnp.int32, (rows, 2 * rows), 1)
    pick_own = (source == 2 * to + low).astype(jnp.bfloat16)
    pick_pair = (source == 2 * to + 1 - low).astype(jnp.bfloat16)
    for left_ref, place in ((near_ref, core), (far_ref, 1 - core)):
        part = matmul(matmul(pick_own, left_ref[...]).astype(jnp.bfloat16), own_ref[...])
        part = part + matmul(matmul(pick_pair, left_ref[...]).astype(jnp.bfloat16), pair_ref[...])
        for home in range(homes):
            o_ref[place, home] = part[home * group:(home + 1) * group].astype(jnp.bfloat16)


def stream_kernel(parts_ref, residual_ref, gain_ref, held_ref, stream_ref, copies_ref):
    stream = residual_ref[...].astype(jnp.float32)
    for i in range(parts_ref.shape[0]):
        stream = stream + parts_ref[i].astype(jnp.float32)
    stream_ref[...] = stream
    scaled = (stream * gain_ref[...].astype(jnp.float32)).astype(jnp.bfloat16)
    for i in range(copies_ref.shape[0]):
        copies_ref[i] = scaled


def gate_up_kernel(merge, place_ref, x_ref, gain_ref, gate_in_ref, up_in_ref, gate_ref, up_ref, *rest):
    other_ref, o_ref = rest[0], rest[1]
    side = place_ref[2]
    units = gate_in_ref.shape[1]
    x = x_ref[...]

    def fill(gate_weight, up_weight):
        gate, up = matmul(x, gate_weight), matmul(x, up_weight)
        if merge:
            gate = gate + other_ref[:, :units].astype(jnp.float32)
            up = up + other_ref[:, units:2 * units].astype(jnp.float32)
        o_ref[:, :units] = gate.astype(jnp.bfloat16)
        o_ref[:, units:2 * units] = up.astype(jnp.bfloat16)

    @pl.when(side == 0)
    def _():
        fill(gate_in_ref[...], up_in_ref[...])

    @pl.when(side != 0)
    def _():
        fill(gate_ref[0, :, units:], up_ref[0, :, units:])

    one = x.astype(jnp.float32) / gain_ref[...].astype(jnp.float32)
    squares = jnp.sum(one * one, axis=1, keepdims=True)
    if merge:
        tail = other_ref[:, 2 * units:].astype(jnp.float32)
        squares = squares + tail[:, 0:1] + tail[:, 1:2]
    high = squares.astype(jnp.bfloat16).astype(jnp.float32)
    lane = lax.broadcasted_iota(jnp.int32, (x.shape[0], 128), 1)
    o_ref[:, 2 * units:] = jnp.where(lane == 0, high, jnp.where(lane == 1, squares - high, 0.0)).astype(jnp.bfloat16)


def hidden_kernel(parts_ref, held_ref, copies_ref):
    units = copies_ref.shape[2]
    sums = parts_ref[0].astype(jnp.float32)
    for i in range(1, parts_ref.shape[0]):
        sums = sums + parts_ref[i].astype(jnp.float32)
    squares = sums[:, 2 * units:2 * units + 1] + sums[:, 2 * units + 1:2 * units + 2]
    inv_rms = lax.rsqrt(squares / D + eps)
    gate = sums[:, :units] * inv_rms
    up = sums[:, units:2 * units] * inv_rms
    hidden = (gate / (1.0 + jnp.exp(-gate)) * up).astype(jnp.bfloat16)
    for i in range(copies_ref.shape[0]):
        copies_ref[i] = hidden


def down_kernel(place_ref, mine_ref, theirs_ref, first_ref, rest_ref, weight_ref, o_ref):
    core, side = place_ref[0], place_ref[2]
    cut = first_ref.shape[0]
    units = cut + rest_ref.shape[0]

    def fill(first, rest):
        for left_ref, place in ((mine_ref, core), (theirs_ref, 1 - core)):
            part = (matmul(left_ref[:, :cut], first) + matmul(left_ref[:, cut:], rest)).astype(jnp.bfloat16)
            group = o_ref.shape[2]
            for row in range(o_ref.shape[0]):
                o_ref[row, place] = part[row * group:(row + 1) * group]

    @pl.when(side == 0)
    def _():
        fill(first_ref[...], rest_ref[...])

    @pl.when(side != 0)
    def _():
        fill(weight_ref[0, units:units + cut, :], weight_ref[0, units + cut:, :])


def final_kernel(place_ref, parts_ref, stream_ref, copies_ref):
    core_half = stream_ref.shape[0]
    total = parts_ref[0].astype(jnp.float32)
    for i in range(1, parts_ref.shape[0]):
        total = total + parts_ref[i].astype(jnp.float32)
    for half in range(2):
        rows = slice(half * core_half, (half + 1) * core_half)
        final = total[rows] + jnp.where(place_ref[2] == half, stream_ref[...], 0.0)
        for i in range(copies_ref.shape[0]):
            copies_ref[i, rows] = final.astype(jnp.bfloat16)


def local(queries, new_entries, cache_keys, cache_values, lengths, residual, norm_gain, out_weight, gate_weight, up_weight, down_weight):
    bf16 = jnp.bfloat16
    rows, pairs, chips = lax.axis_size(ROW), lax.axis_size("rp"), lax.axis_size(CHIPS)
    row, core, side = lax.axis_index(ROW), lax.axis_index("core"), lax.axis_index("side")
    slots, width = queries.shape[0], out_weight.shape[2]
    head_part = out_weight.shape[1] // 2
    units = gate_weight.shape[2] // 2
    group = chips * slots
    total = rows * 2 * group
    place = jnp.stack([core, lax.axis_index("rl"), side]).astype(jnp.int32)

    out_own = jnp.where(side == 0, from_ffn(out_weight[0, :head_part]), out_weight[0, head_part:])
    out_pair = flip(out_own, "rl")
    gain = norm_gain[None, :]

    by_pair = attention(queries, new_entries, cache_keys, cache_values, lengths, pairs)
    by_pair, gate_late, up_late, down_late = lax.optimization_barrier((by_pair, gate_weight, up_weight, down_weight))
    gate_in = from_ffn(gate_late[0, :, :units])
    up_in = from_ffn(up_late[0, :, :units])
    cut = units // 2 // 256 * 256 + 256
    down_first = from_ffn(down_late[0, :cut])
    down_rest = from_ffn(down_late[0, cut:units])
    arrived = lax.ppermute(by_pair[pairs:], "side", [(0, 1)])
    mine = jnp.where(side == 0, by_pair[:pairs], arrived)
    near = exchange(jnp.broadcast_to(mine[:, None], (pairs, chips) + mine.shape[1:]).reshape((pairs * chips,) + mine.shape[1:]), ("rp",) + CHIPS).reshape(pairs * chips * 2 * slots, head_part)
    far = flip(near, "core")
    part = call(project_kernel, "project", jax.ShapeDtypeStruct((2, pairs, group, width), bf16), in_specs=[SCALARS, WHOLE, WHOLE, WHOLE, WHOLE, HELD], out_specs=WHOLE)(place, near, far, out_own, out_pair, gate_in)
    parts = exchange(part.reshape(2 * pairs, group, width), ("side", "rp"))
    own_residual = lax.dynamic_slice(residual.reshape(rows, chips, 2, slots, width), (row, 0, side, 0, 0), (1, chips, 1, slots, width)).reshape(group, width)
    stream, copies = call(stream_kernel, "stream", (jax.ShapeDtypeStruct((group, width), jnp.float32), jax.ShapeDtypeStruct((2 * rows, group, width), bf16)), in_specs=[WHOLE] * 3 + [HELD], out_specs=(WHOLE, WHOLE))(parts, own_residual, gain, up_in)
    scaled = exchange(copies, HOME).reshape(total, width)

    steps = 2
    block = total // (2 * steps)
    wide = 2 * units + 128

    def gate_up(which, name, extra, other):
        fixed = lambda shape: pl.BlockSpec(shape, lambda i, p: (0,) * len(shape))
        piece = pl.BlockSpec((block, wide), lambda i, p: (i, 0))
        grid_spec = pltpu.PrefetchScalarGridSpec(
            num_scalar_prefetch=1, grid=(steps,),
            in_specs=[pl.BlockSpec((block, width), lambda i, p: (which(p[0]) * steps + i, 0)), fixed((1, width)), fixed((width, units)), fixed((width, units)),
                fixed((1, width, 2 * units)), fixed((1, width, 2 * units))] + [piece if other else HELD],
            out_specs=piece)
        return call(functools.partial(gate_up_kernel, other), name, jax.ShapeDtypeStruct((total // 2, wide), bf16), grid_spec=grid_spec)(
            place, scaled, gain, gate_in, up_in, gate_weight, up_weight, extra)

    far_part = gate_up(lambda c: 1 - c, "gate_up_far", down_first, False)
    sent = gate_up(lambda c: c, "gate_up_near", flip(far_part, "core"), True)
    share = total // (2 * chips)
    sums = exchange(sent.reshape(chips, share, wide), CHIPS)
    hidden = call(hidden_kernel, "hidden", jax.ShapeDtypeStruct((chips, share, units), bf16), grid=(2,),
        in_specs=[pl.BlockSpec((chips, share // 2, wide), lambda i: (0, i, 0)), HELD], out_specs=pl.BlockSpec((chips, share // 2, units), lambda i: (0, i, 0)))(sums, down_rest)
    hidden = exchange(hidden, CHIPS).reshape(total // 2, units)
    down = call(down_kernel, "down", jax.ShapeDtypeStruct((rows, 2, group, width), bf16), in_specs=[SCALARS] + [WHOLE] * 5, out_specs=WHOLE)(
        place, hidden, flip(hidden, "core"), down_first, down_rest, down_weight)
    downs = exchange(down.reshape(rows, 2 * group, width), ("rl", "rp"))
    final = call(final_kernel, "final", jax.ShapeDtypeStruct((2, 2 * group, width), bf16), in_specs=[SCALARS] + [WHOLE] * 2, out_specs=WHOLE)(place, downs, stream)
    back = exchange(final.reshape(4 * chips, slots, width), ("side", "core") + CHIPS)
    back = back.reshape(2, 2, lax.axis_size("x"), lax.axis_size("yl"), slots, width)
    half = lax.axis_size("x") // 2
    back = lax.dynamic_slice_in_dim(back, side * half, half, 2).astype(jnp.float32)
    back = (back[0] + back[1]).astype(bf16)
    return back.transpose(3, 1, 2, 0, 4).reshape(slots, width * chips)


def solution(mesh):
    sides, rows, cols = mesh.devices.shape
    inner = Mesh(mesh.devices.reshape(sides, rows // 2, 2, cols // 4, 2, 2), ("side",) + ROW + COL)
    in_specs = (
        P(ROW + COL, None),
        P(ROW + COL, None),
        P("side", ROW + COL, None, None),
        P("side", ROW + COL, None, None),
        P(ROW + COL),
        P(None, COL),
        P(COL),
        P("side", ROW, COL),
        P("side", COL, ROW),
        P("side", COL, ROW),
        P("side", ROW, COL),
    )
    return jax.shard_map(local, mesh=inner, in_specs=in_specs, out_specs=P(ROW + COL, "side"), check_vma=False)
```

```python
import functools
import math
import jax
import jax.numpy as jnp
from jax import lax
from jax.experimental import pallas as pl
from jax.experimental.pallas import tpu as pltpu
from jax.sharding import Mesh, PartitionSpec as P

D = 8192
H = 64
KVH = 8
HD = 128
ORIG = 64
PER = H // KVH

rope_theta = 500000.0
stretch_factor = 8.0
eps = 1e-05

CHIPS = ("x", "yl")
COL = ("x", "yl", "core")
ROW = ("rp", "rl")
HOME = ("rl", "rp")
WHOLE = pl.BlockSpec(memory_space=pltpu.VMEM)
HELD = pl.BlockSpec(memory_space=pl.ANY)
SCALARS = pl.BlockSpec(memory_space=pltpu.SMEM)


def swap_halves(v):
    return jnp.concatenate([v[:, HD // 2:], v[:, : HD // 2]], axis=-1)


def attend_kernel(len_ref, place_ref, q_ref, new_ref, k_lo_ref, k_hi_ref, v_lo_ref, v_hi_ref, *rest):
    o_refs, (q_all, new_all, s_all, acc, out_all) = rest[:-5], rest[-5:]
    slot = pl.program_id(0)
    slots = q_ref.shape[0]
    length = len_ref[slot]
    half = k_lo_ref.shape[2]
    span = 2 * half

    @pl.when(slot == 0)
    def _():
        for h in range(H):
            q_all[:, h, :] = q_ref[:, h * HD:(h + 1) * HD].astype(jnp.float32)
        for h in range(2 * KVH):
            new_all[:, h, :] = new_ref[:, h * HD:(h + 1) * HD].astype(jnp.float32)

    lane = lax.broadcasted_iota(jnp.int32, (1, HD), 1)
    pair = jnp.where(lane < HD // 2, lane, lane - HD // 2).astype(jnp.float32)
    position = jnp.full((1, HD), length, jnp.int32).astype(jnp.float32)
    stretch = jnp.maximum(stretch_factor * (position + 1.0) / ORIG - (stretch_factor - 1.0), 1.0)
    log_base = math.log(rope_theta) + HD / (HD - 2.0) * jnp.log(stretch)
    freqs = jnp.exp(-(pair * (2.0 / HD)) * log_base)
    steps = span // 16
    fine = lax.broadcasted_iota(jnp.int32, (16, HD), 0).astype(jnp.float32)
    coarse = lax.broadcasted_iota(jnp.int32, (steps, HD), 0).astype(jnp.float32) * 16.0
    fine_cos, fine_sin = jnp.cos(fine * freqs), jnp.sin(fine * freqs)
    coarse_cos, coarse_sin = jnp.cos(coarse * freqs), jnp.sin(coarse * freqs)

    def tables(first):
        cos_parts, sin_parts = [], []
        for step in range(first, first + steps // 2):
            cc, cs = coarse_cos[step:step + 1], coarse_sin[step:step + 1]
            cos_parts.append(cc * fine_cos - cs * fine_sin)
            sin_parts.append(cs * fine_cos + cc * fine_sin)
        return jnp.concatenate(cos_parts, axis=0), jnp.concatenate(sin_parts, axis=0)

    sign = jnp.where(lane < HD // 2, -1.0, 1.0)
    cos_new = jnp.cos(position * freqs)
    sin_new = jnp.sin(position * freqs) * sign
    q = q_all[slot]
    q_rot = q * cos_new + swap_halves(q) * sin_new
    q_rot = q_rot.astype(jnp.bfloat16).astype(jnp.float32)
    q_both = jnp.concatenate([q_rot, swap_halves(q_rot) * -sign], axis=-1)
    k_new = new_all[slot, :KVH]
    k_new = k_new * cos_new + swap_halves(k_new) * sin_new
    k_new = k_new.astype(jnp.bfloat16).astype(jnp.float32)
    v_new = new_all[slot, KVH:]
    scale = HD ** (-0.5)

    def score(k_ref, first):
        cos_t, sin_t = tables(first)
        for g in range(KVH):
            kg = k_ref[0, 0, :, g * HD:(g + 1) * HD].astype(jnp.float32)
            kk = jnp.concatenate([(kg * cos_t).astype(jnp.bfloat16), (kg * sin_t).astype(jnp.bfloat16)], axis=-1)
            qg = q_both[g * PER:(g + 1) * PER].astype(jnp.bfloat16)
            s_all[g * PER:(g + 1) * PER, first * 16:first * 16 + half] = lax.dot_general(qg, kk, (((1,), (1,)), ((), ())), preferred_element_type=jnp.float32)

    score(k_lo_ref, 0)

    @pl.when(length > half)
    def _():
        score(k_hi_ref, steps // 2)

    @pl.when(length <= half)
    def _():
        s_all[:, half:] = jnp.zeros((H, half), jnp.float32)

    own, fresh = [], []
    for g in range(KVH):
        own.append(jnp.sum(q_rot[g * PER:(g + 1) * PER] * k_new[g:g + 1], axis=-1, keepdims=True))
        fresh.append(jnp.broadcast_to(v_new[g:g + 1], (PER, HD)))
    own_score = jnp.concatenate(own, axis=0) * scale
    valid = lax.broadcasted_iota(jnp.int32, (H, span), 1) < length
    s = jnp.where(valid, s_all[...] * scale, -1e30)
    top = jnp.maximum(jnp.max(s, axis=-1, keepdims=True), own_score)
    w = jnp.where(valid, jnp.exp(s - top), 0.0)
    own_w = jnp.exp(own_score - top)
    total = jnp.sum(w, axis=-1, keepdims=True) + own_w
    w16 = w.astype(jnp.bfloat16)

    def mix(v_ref, weights):
        parts = []
        for p in range(KVH // 2):
            o = jnp.dot(weights[p * 2 * PER:(p + 1) * 2 * PER], v_ref[0, 0, :, p * 2 * HD:(p + 1) * 2 * HD], preferred_element_type=jnp.float32)
            parts += [o[:PER, :HD], o[PER:, HD:]]
        return jnp.concatenate(parts, axis=0)

    acc[...] = mix(v_lo_ref, w16[:, :half]) + own_w * jnp.concatenate(fresh, axis=0)

    @pl.when(length > half)
    def _():
        acc[...] += mix(v_hi_ref, w16[:, half:])

    out = acc[...] / total
    pairs = len(o_refs)
    per_row = H // (2 * pairs)
    for h in range(H):
        at, q_at = h // per_row, h % per_row
        out_all[at // 2, slot, at % 2:at % 2 + 1, q_at * HD:(q_at + 1) * HD] = out[h:h + 1]

    @pl.when(slot == slots - 1)
    def _():
        for k in range(pairs):
            home = lax.rem(place_ref[2] + k, pairs)
            o_refs[k][...] = jnp.concatenate([out_all[home, j] for j in range(slots)], axis=0).astype(jnp.bfloat16)


def attention(place, queries, new_entries, cache_keys, cache_values, lengths, pairs):
    slots = queries.shape[0]
    half = cache_keys.shape[2] // 2
    width = KVH * HD
    low = pl.BlockSpec((1, 1, half, width), lambda s, n, p: (0, s, 0, 0))

    def last_long(s, n, p):
        at = 0
        for j in range(1, slots):
            at = jnp.where((s >= j) & (n[j] > half), j, at)
        return (0, at, 1, 0)

    high = pl.BlockSpec((1, 1, half, width), last_long)
    heads = H * HD // (2 * pairs)
    grid_spec = pltpu.PrefetchScalarGridSpec(
        num_scalar_prefetch=2, grid=(slots,),
        in_specs=[pl.BlockSpec((slots, H * HD), lambda s, n, p: (0, 0)), pl.BlockSpec((slots, 2 * width), lambda s, n, p: (0, 0)), low, high, low, high],
        out_specs=[pl.BlockSpec((2 * slots, heads), lambda s, n, p: (0, 0))] * pairs,
        scratch_shapes=[
            pltpu.VMEM((slots, H, HD), jnp.float32), pltpu.VMEM((slots, 2 * KVH, HD), jnp.float32),
            pltpu.VMEM((H, 2 * half), jnp.float32), pltpu.VMEM((H, HD), jnp.float32), pltpu.VMEM((pairs, slots, 2, heads), jnp.float32)])
    return pl.pallas_call(
        attend_kernel, grid_spec=grid_spec,
        out_shape=[jax.ShapeDtypeStruct((2 * slots, heads), jnp.bfloat16)] * pairs,
        compiler_params=pltpu.CompilerParams(vmem_limit_bytes=60 << 20), name="attend",
    )(lengths, place, queries, new_entries, cache_keys, cache_keys, cache_values, cache_values)


def flip(value, axis):
    return lax.ppermute(value, axis, [(0, 1), (1, 0)])


def turn(value, steps):
    count = lax.axis_size("rp")
    return lax.ppermute(value, "rp", [(i, (i + steps) % count) for i in range(count)])


def to_ffn(value, steps):
    count = lax.axis_size("rp")
    return lax.ppermute(value, ("side", "rp"), [(i, count + (i + steps) % count) for i in range(count)])


def exchange(value, axes):
    return lax.all_to_all(value, axes, split_axis=0, concat_axis=0, tiled=True)


def matmul(left, right):
    return jnp.dot(left, right, preferred_element_type=jnp.float32)


def call(kernel, name, out_shape, **options):
    return pl.pallas_call(kernel, out_shape=out_shape, name=name, compiler_params=pltpu.CompilerParams(vmem_limit_bytes=24 << 20), **options)


def fan_kernel(*refs):
    blocks, o_ref = refs[:-2], refs[-1]
    rows = blocks[0].shape[0]
    for i in range(o_ref.shape[0]):
        for k, block in enumerate(blocks):
            o_ref[i, k * rows:(k + 1) * rows] = block[...]


def project_kernel(place_ref, near_ref, far_ref, own_ref, pair_a_ref, pair_b_ref, held_ref, *o_refs):
    core, low = place_ref[0], place_ref[1]
    pairs, group = len(o_refs), o_refs[0].shape[1]
    slots = near_ref.shape[0] // (2 * pairs * (group // 4))
    rows = pairs * group
    to = lax.broadcasted_iota(jnp.int32, (rows, 2 * rows), 0)
    source = lax.broadcasted_iota(jnp.int32, (rows, 2 * rows), 1)
    block = (pairs - to // group) % pairs
    first = ((to % group) // slots) * (2 * slots * pairs) + block * (2 * slots) + (to % slots) * 2
    pick_own = (source == first + low).astype(jnp.bfloat16)
    pick_pair = (source == first + 1 - low).astype(jnp.bfloat16)
    cut = pair_a_ref.shape[0]
    for left_ref, place in ((near_ref, core), (far_ref, 1 - core)):
        part = matmul(matmul(pick_own, left_ref[...]).astype(jnp.bfloat16), own_ref[0])
        theirs = matmul(pick_pair, left_ref[...]).astype(jnp.bfloat16)
        part = part + matmul(theirs[:, :cut], pair_a_ref[...]) + matmul(theirs[:, cut:], pair_b_ref[...])
        for k in range(pairs):
            o_refs[k][place] = part[k * group:(k + 1) * group].astype(jnp.bfloat16)


def stream_kernel(*refs):
    parts, (residual_ref, gain_ref, held_ref, stream_ref, copies_ref) = refs[:-5], refs[-5:]
    stream = residual_ref[...].astype(jnp.float32)
    for part_ref in parts:
        stream = stream + part_ref[...].astype(jnp.float32)
    stream_ref[...] = stream
    scaled = (stream * gain_ref[...].astype(jnp.float32)).astype(jnp.bfloat16)
    for i in range(copies_ref.shape[0]):
        copies_ref[i] = scaled


def gate_up_kernel(mine_ref, theirs_ref, gain_ref, gain_theirs_ref, gate_ref, gate_theirs_ref, up_ref, up_theirs_ref, o_ref):
    half = gate_ref.shape[1]
    mine, theirs = mine_ref[...], theirs_ref[...]
    o_ref[:, :half] = (matmul(mine, gate_ref[...]) + matmul(theirs, gate_theirs_ref[...])).astype(jnp.bfloat16)
    o_ref[:, half:2 * half] = (matmul(mine, up_ref[...]) + matmul(theirs, up_theirs_ref[...])).astype(jnp.bfloat16)
    one = mine.astype(jnp.float32) * (1.0 / gain_ref[...].astype(jnp.float32))
    two = theirs.astype(jnp.float32) * (1.0 / gain_theirs_ref[...].astype(jnp.float32))
    squares = jnp.sum(one * one + two * two, axis=1, keepdims=True)
    high = squares.astype(jnp.bfloat16).astype(jnp.float32)
    lane = lax.broadcasted_iota(jnp.int32, (mine.shape[0], 128), 1)
    o_ref[:, 2 * half:] = jnp.where(lane == 0, high, jnp.where(lane == 1, squares - high, 0.0)).astype(jnp.bfloat16)


def hidden_kernel(parts_ref, copies_ref):
    half = copies_ref.shape[2]
    sums = parts_ref[0].astype(jnp.float32)
    for i in range(1, parts_ref.shape[0]):
        sums = sums + parts_ref[i].astype(jnp.float32)
    squares = sums[:, 2 * half:2 * half + 1] + sums[:, 2 * half + 1:2 * half + 2]
    inv_rms = lax.rsqrt(squares / D + eps)
    gate = sums[:, :half] * inv_rms
    up = sums[:, half:2 * half] * inv_rms
    hidden = (gate / (1.0 + jnp.exp(-gate)) * up).astype(jnp.bfloat16)
    for i in range(copies_ref.shape[0]):
        copies_ref[i] = hidden


def down_kernel(place_ref, mine_ref, theirs_ref, weight_ref, o_ref):
    half = mine_ref.shape[1]
    core = place_ref[0]
    part = matmul(mine_ref[...], weight_ref[0, pl.ds(pl.multiple_of(core * half, half), half), :])
    part = part + matmul(theirs_ref[...], weight_ref[0, pl.ds(pl.multiple_of((1 - core) * half, half), half), :])
    o_ref[...] = part.astype(jnp.bfloat16)


def final_kernel(parts_ref, stream_ref, copies_ref):
    total = parts_ref[0].astype(jnp.float32)
    for i in range(1, parts_ref.shape[0]):
        total = total + parts_ref[i].astype(jnp.float32)
    final = (stream_ref[...] + total).astype(jnp.bfloat16)
    for i in range(copies_ref.shape[0]):
        copies_ref[i] = final


def local(queries, new_entries, cache_keys, cache_values, lengths, residual, norm_gain, out_weight, gate_weight, up_weight, down_weight):
    bf16 = jnp.bfloat16
    rows, pairs, chips = lax.axis_size(ROW), lax.axis_size("rp"), lax.axis_size(CHIPS)
    row, core, side = lax.axis_index(ROW), lax.axis_index("core"), lax.axis_index("side")
    slots, width = queries.shape[0], out_weight.shape[2]
    heads = out_weight.shape[1]
    half = gate_weight.shape[2] // 2
    group = chips * 2 * slots
    total = rows * group
    place = jnp.stack([core, lax.axis_index("rl"), lax.axis_index("rp")]).astype(jnp.int32)

    pair_a = flip(out_weight[0, :heads // 2], "rl")
    pair_b = flip(out_weight[0, heads // 2:], "rl")
    gain = norm_gain[None, :]
    gain_theirs = flip(gain, "core")
    gate_theirs = flip(lax.dynamic_slice_in_dim(gate_weight[0], (1 - core) * half, half, 1), "core")
    up_theirs = flip(lax.dynamic_slice_in_dim(up_weight[0], (1 - core) * half, half, 1), "core")
    gate_mine = lax.dynamic_slice_in_dim(gate_weight[0], core * half, half, 1)
    up_mine = lax.dynamic_slice_in_dim(up_weight[0], core * half, half, 1)

    blocks = attention(place, queries, new_entries, cache_keys, cache_values, lengths, pairs)
    blocks = [to_ffn(block, k) for k, block in enumerate(blocks)]
    fanned = call(fan_kernel, "fan", jax.ShapeDtypeStruct((chips, pairs * 2 * slots, heads), bf16), in_specs=[WHOLE] * pairs + [HELD], out_specs=WHOLE)(*blocks, pair_a)
    near = exchange(fanned, CHIPS).reshape(chips * pairs * 2 * slots, heads)
    far = flip(near, "core")
    own, *parts = call(project_kernel, "project", [jax.ShapeDtypeStruct((2, group // 2, width), bf16)] * pairs, in_specs=[SCALARS] + [WHOLE] * 5 + [HELD], out_specs=[WHOLE] * pairs)(
        place, near, far, out_weight, pair_a, pair_b, gain_theirs)
    parts = [own] + [turn(part, k + 1) for k, part in enumerate(parts)]
    parts = [part.reshape(group, width) for part in parts]
    own_residual = lax.dynamic_index_in_dim(residual.reshape(rows, chips, 2, slots, width), row, 0, False).transpose(1, 0, 2, 3).reshape(group, width)
    stream, copies = call(stream_kernel, "stream", (jax.ShapeDtypeStruct((group, width), jnp.float32), jax.ShapeDtypeStruct((rows, group, width), bf16)), in_specs=[WHOLE] * (pairs + 2) + [HELD], out_specs=(WHOLE, WHOLE))(
        *parts, own_residual, gain, gain_theirs)
    scaled = exchange(copies, HOME).reshape(total, width)
    scaled_theirs = flip(scaled, "core")
    block = total // 4
    fixed = lambda shape: pl.BlockSpec(shape, lambda i: (0,) * len(shape))
    sent = call(gate_up_kernel, "gate_up", jax.ShapeDtypeStruct((total, 2 * half + 128), bf16), grid=(4,),
        in_specs=[pl.BlockSpec((block, width), lambda i: (i, 0))] * 2 + [fixed((1, width))] * 2 + [fixed((width, half))] * 4,
        out_specs=pl.BlockSpec((block, 2 * half + 128), lambda i: (i, 0)))(scaled, scaled_theirs, gain, gain_theirs, gate_mine, gate_theirs, up_mine, up_theirs)
    sums = exchange(sent.reshape(chips, group, 2 * half + 128), CHIPS)
    step = group // 4
    hidden = call(hidden_kernel, "hidden", jax.ShapeDtypeStruct((chips, group, half), bf16), grid=(4,),
        in_specs=[pl.BlockSpec((chips, step, 2 * half + 128), lambda i: (0, i, 0))], out_specs=pl.BlockSpec((chips, step, half), lambda i: (0, i, 0)))(sums)
    hidden = exchange(hidden, CHIPS).reshape(total, half)
    down = call(down_kernel, "down", jax.ShapeDtypeStruct((total, width), bf16), in_specs=[SCALARS] + [WHOLE] * 3, out_specs=WHOLE)(place, hidden, flip(hidden, "core"), down_weight)
    downs = exchange(down.reshape(rows, group, width), HOME)
    final = call(final_kernel, "final", jax.ShapeDtypeStruct((2, group, width), bf16), in_specs=[WHOLE] * 2, out_specs=WHOLE)(downs, stream)
    back = exchange(final.reshape(4 * chips, slots, width), ("side", "core") + CHIPS)
    back = back.reshape(2, 2, lax.axis_size("x"), lax.axis_size("yl"), slots, width)[1]
    part = lax.axis_size("x") // 2
    back = lax.dynamic_slice_in_dim(back, side * part, part, 1)
    return back.transpose(3, 1, 2, 0, 4).reshape(slots, width * chips)


def solution(mesh):
    sides, rows, cols = mesh.devices.shape
    inner = Mesh(mesh.devices.reshape(sides, rows // 2, 2, cols // 4, 2, 2), ("side",) + ROW + COL)
    in_specs = (
        P(ROW + COL, None),
        P(ROW + COL, None),
        P("side", ROW + COL, None, None),
        P("side", ROW + COL, None, None),
        P(ROW + COL),
        P(None, COL),
        P(COL),
        P("side", ROW, COL),
        P("side", COL, ROW),
        P("side", COL, ROW),
        P("side", ROW, COL),
    )
    return jax.shard_map(local, mesh=inner, in_specs=in_specs, out_specs=P(ROW + COL, "side"), check_vma=False)
```

```python
import functools
import math
import jax
import jax.numpy as jnp
from jax import lax
from jax.experimental import pallas as pl
from jax.experimental.pallas import tpu as pltpu
from jax.sharding import Mesh, PartitionSpec as P

D = 8192
H = 64
KVH = 8
HD = 128
ORIG = 64
PER = H // KVH

rope_theta = 500000.0
stretch_factor = 8.0
eps = 1e-05

CHIPS = ("x", "yl")
COL = ("x", "yl", "core")
ROW = ("rp", "rl")
HOME = ("rl", "rp")
WHOLE = pl.BlockSpec(memory_space=pltpu.VMEM)
HELD = pl.BlockSpec(memory_space=pl.ANY)
SCALARS = pl.BlockSpec(memory_space=pltpu.SMEM)


def swap_halves(v):
    return jnp.concatenate([v[:, HD // 2:], v[:, : HD // 2]], axis=-1)


def attend_kernel(len_ref, q_ref, new_ref, k_lo_ref, k_hi_ref, v_lo_ref, v_hi_ref, *rest):
    o_refs, (q_all, new_all, s_all, acc, out_all, fine_all, coarse_all, at_all) = rest[:-8], rest[-8:]
    slot = pl.program_id(0)
    slots = q_ref.shape[0]
    length = len_ref[slot]
    half = k_lo_ref.shape[2]
    span = 2 * half

    @pl.when(slot == 0)
    def _():
        for h in range(H):
            q_all[:, h, :] = q_ref[:, h * HD:(h + 1) * HD].astype(jnp.float32)
        for h in range(2 * KVH):
            new_all[:, h, :] = new_ref[:, h * HD:(h + 1) * HD].astype(jnp.float32)

    steps = span // 16
    lane = lax.broadcasted_iota(jnp.int32, (1, HD), 1)
    sign = jnp.where(lane < HD // 2, -1.0, 1.0)

    @pl.when(slot == 0)
    def _():
        pair = jnp.where(lane < HD // 2, lane, lane - HD // 2).astype(jnp.float32)
        positions = jnp.concatenate([jnp.full((8, HD), len_ref[j], jnp.int32) for j in range(slots)], axis=0).astype(jnp.float32)
        stretch = jnp.maximum(stretch_factor * (positions + 1.0) / ORIG - (stretch_factor - 1.0), 1.0)
        log_base = math.log(rope_theta) + HD / (HD - 2.0) * jnp.log(stretch)
        freqs = jnp.exp(-(pair * (2.0 / HD)) * log_base)
        low = lax.broadcasted_iota(jnp.int32, (16, HD), 0).astype(jnp.float32)
        high = lax.broadcasted_iota(jnp.int32, (steps, HD), 0).astype(jnp.float32) * 16.0
        each = [freqs[8 * j:8 * j + 1] for j in range(slots)]
        angles = jnp.concatenate([low * f for f in each] + [high * f for f in each] + [positions * freqs], axis=0)
        cosine, sine = jnp.cos(angles), jnp.sin(angles)
        for j in range(slots):
            fine_all[j, 0] = cosine[16 * j:16 * j + 16]
            fine_all[j, 1] = sine[16 * j:16 * j + 16]
            at = 16 * slots + steps * j
            coarse_all[j, 0] = cosine[at:at + steps]
            coarse_all[j, 1] = sine[at:at + steps]
            at = (16 + steps) * slots + 8 * j
            at_all[j, 0] = cosine[at:at + 8]
            at_all[j, 1] = sine[at:at + 8]

    fine_cos, fine_sin = fine_all[slot, 0], fine_all[slot, 1]
    coarse_cos, coarse_sin = coarse_all[slot, 0], coarse_all[slot, 1]

    def tables(first):
        cos_parts, sin_parts = [], []
        for step in range(first, first + steps // 2):
            cc, cs = coarse_cos[step:step + 1], coarse_sin[step:step + 1]
            cos_parts.append(cc * fine_cos - cs * fine_sin)
            sin_parts.append(cs * fine_cos + cc * fine_sin)
        return jnp.concatenate(cos_parts, axis=0), jnp.concatenate(sin_parts, axis=0)

    cos_new = at_all[slot, 0, :1]
    sin_new = at_all[slot, 1, :1] * sign
    q = q_all[slot]
    q_rot = q * cos_new + swap_halves(q) * sin_new
    q_rot = q_rot.astype(jnp.bfloat16).astype(jnp.float32)
    q_both = jnp.concatenate([q_rot, swap_halves(q_rot) * -sign], axis=-1)
    k_new = new_all[slot, :KVH]
    k_new = k_new * cos_new + swap_halves(k_new) * sin_new
    k_new = k_new.astype(jnp.bfloat16).astype(jnp.float32)
    v_new = new_all[slot, KVH:]
    scale = HD ** (-0.5)

    def score(k_ref, first):
        cos_t, sin_t = tables(first)
        for g in range(KVH):
            kg = k_ref[0, 0, :, g * HD:(g + 1) * HD].astype(jnp.float32)
            kk = jnp.concatenate([(kg * cos_t).astype(jnp.bfloat16), (kg * sin_t).astype(jnp.bfloat16)], axis=-1)
            qg = q_both[g * PER:(g + 1) * PER].astype(jnp.bfloat16)
            s_all[g * PER:(g + 1) * PER, first * 16:first * 16 + half] = lax.dot_general(qg, kk, (((1,), (1,)), ((), ())), preferred_element_type=jnp.float32)

    score(k_lo_ref, 0)

    @pl.when(length > half)
    def _():
        score(k_hi_ref, steps // 2)

    @pl.when(length <= half)
    def _():
        s_all[:, half:] = jnp.zeros((H, half), jnp.float32)

    own, fresh = [], []
    for g in range(KVH):
        own.append(jnp.sum(q_rot[g * PER:(g + 1) * PER] * k_new[g:g + 1], axis=-1, keepdims=True))
        fresh.append(jnp.broadcast_to(v_new[g:g + 1], (PER, HD)))
    own_score = jnp.concatenate(own, axis=0) * scale
    valid = lax.broadcasted_iota(jnp.int32, (H, span), 1) < length
    s = jnp.where(valid, s_all[...] * scale, -1e30)
    top = jnp.maximum(jnp.max(s, axis=-1, keepdims=True), own_score)
    w = jnp.where(valid, jnp.exp(s - top), 0.0)
    own_w = jnp.exp(own_score - top)
    total = jnp.sum(w, axis=-1, keepdims=True) + own_w
    w16 = w.astype(jnp.bfloat16)

    def mix(v_ref, weights):
        parts = []
        for p in range(KVH // 2):
            o = jnp.dot(weights[p * 2 * PER:(p + 1) * 2 * PER], v_ref[0, 0, :, p * 2 * HD:(p + 1) * 2 * HD], preferred_element_type=jnp.float32)
            parts += [o[:PER, :HD], o[PER:, HD:]]
        return jnp.concatenate(parts, axis=0)

    acc[...] = mix(v_lo_ref, w16[:, :half]) + own_w * jnp.concatenate(fresh, axis=0)

    @pl.when(length > half)
    def _():
        acc[...] += mix(v_hi_ref, w16[:, half:])

    out = acc[...] / total
    pairs = len(o_refs)
    per_row = H // (2 * pairs)
    for h in range(H):
        at, q_at = h // per_row, h % per_row
        out_all[at // 2, slot, at % 2:at % 2 + 1, q_at * HD:(q_at + 1) * HD] = out[h:h + 1]

    @pl.when(slot == slots - 1)
    def _():
        for k in range(pairs):
            home = lax.rem(lax.axis_index("rp") + k, pairs)
            o_refs[k][...] = jnp.concatenate([out_all[home, j] for j in range(slots)], axis=0).astype(jnp.bfloat16)


def attention(queries, new_entries, cache_keys, cache_values, lengths, pairs):
    slots = queries.shape[0]
    half = cache_keys.shape[2] // 2
    width = KVH * HD
    low = pl.BlockSpec((1, 1, half, width), lambda s, n: (0, s, 0, 0))

    def last_long(s, n):
        at = 0
        for j in range(1, slots):
            at = jnp.where((s >= j) & (n[j] > half), j, at)
        return (0, at, 1, 0)

    high = pl.BlockSpec((1, 1, half, width), last_long)
    heads = H * HD // (2 * pairs)
    grid_spec = pltpu.PrefetchScalarGridSpec(
        num_scalar_prefetch=1, grid=(slots,),
        in_specs=[pl.BlockSpec((slots, H * HD), lambda s, n: (0, 0)), pl.BlockSpec((slots, 2 * width), lambda s, n: (0, 0)), low, high, low, high],
        out_specs=[pl.BlockSpec((2 * slots, heads), lambda s, n: (0, 0))] * pairs,
        scratch_shapes=[
            pltpu.VMEM((slots, H, HD), jnp.float32), pltpu.VMEM((slots, 2 * KVH, HD), jnp.float32),
            pltpu.VMEM((H, 2 * half), jnp.float32), pltpu.VMEM((H, HD), jnp.float32), pltpu.VMEM((pairs, slots, 2, heads), jnp.float32),
            pltpu.VMEM((slots, 2, 16, HD), jnp.float32), pltpu.VMEM((slots, 2, 2 * half // 16, HD), jnp.float32), pltpu.VMEM((slots, 2, 8, HD), jnp.float32)])
    return pl.pallas_call(
        attend_kernel, grid_spec=grid_spec,
        out_shape=[jax.ShapeDtypeStruct((2 * slots, heads), jnp.bfloat16)] * pairs,
        compiler_params=pltpu.CompilerParams(vmem_limit_bytes=60 << 20), name="attend",
    )(lengths, queries, new_entries, cache_keys, cache_keys, cache_values, cache_values)


def flip(value, axis):
    return lax.ppermute(value, axis, [(0, 1), (1, 0)])


def turn(value, steps):
    count = lax.axis_size("rp")
    return lax.ppermute(value, "rp", [(i, (i + steps) % count) for i in range(count)])


def to_ffn(value, steps):
    count = lax.axis_size("rp")
    return lax.ppermute(value, ("side", "rp"), [(i, count + (i + steps) % count) for i in range(count)])


def exchange(value, axes):
    return lax.all_to_all(value, axes, split_axis=0, concat_axis=0, tiled=True)


def matmul(left, right):
    return jnp.dot(left, right, preferred_element_type=jnp.float32)


def call(kernel, name, out_shape, **options):
    limit = options.pop("limit", 24)
    return pl.pallas_call(kernel, out_shape=out_shape, name=name, compiler_params=pltpu.CompilerParams(vmem_limit_bytes=limit << 20), **options)


def fan_kernel(*refs):
    blocks, o_ref = refs[:-2], refs[-1]
    rows = blocks[0].shape[0]
    for i in range(o_ref.shape[0]):
        for k, block in enumerate(blocks):
            o_ref[i, k * rows:(k + 1) * rows] = block[...]


def project_kernel(near_ref, far_ref, own_ref, pair_ref, *o_refs):
    core, low = lax.axis_index("core"), lax.axis_index("rl")
    pairs, group = len(o_refs), o_refs[0].shape[1]
    slots = near_ref.shape[0] // (2 * pairs * (group // 4))
    rows = pairs * group
    to = lax.broadcasted_iota(jnp.int32, (rows, 2 * rows), 0)
    source = lax.broadcasted_iota(jnp.int32, (rows, 2 * rows), 1)
    block = (pairs - to // group) % pairs
    first = ((to % group) // slots) * (2 * slots * pairs) + block * (2 * slots) + (to % slots) * 2
    pick_own = (source == first + low).astype(jnp.bfloat16)
    pick_pair = (source == first + 1 - low).astype(jnp.bfloat16)
    for left_ref, place in ((near_ref, core), (far_ref, 1 - core)):
        part = matmul(matmul(pick_own, left_ref[...]).astype(jnp.bfloat16), own_ref[0])
        part = part + matmul(matmul(pick_pair, left_ref[...]).astype(jnp.bfloat16), pair_ref[0])
        for k in range(pairs):
            o_refs[k][place] = part[k * group:(k + 1) * group].astype(jnp.bfloat16)


def stream_kernel(*refs):
    parts, (residual_ref, gain_ref, stream_ref, copies_ref) = refs[:-4], refs[-4:]
    group = stream_ref.shape[0]
    chips = group // 8
    row = lax.axis_index("rp") * 2 + lax.axis_index("rl")
    to = lax.broadcasted_iota(jnp.int32, (group, group), 0)
    source = lax.broadcasted_iota(jnp.int32, (group, group), 1)
    order = (source == (to // 4 % chips) * 8 + (to // (4 * chips)) * 4 + to % 4).astype(jnp.bfloat16)
    stream = matmul(order, residual_ref[pl.ds(pl.multiple_of(row * group, group), group), :])
    for part_ref in parts:
        stream = stream + part_ref[...].astype(jnp.float32)
    stream_ref[...] = stream
    scaled = (stream * gain_ref[...].astype(jnp.float32)).astype(jnp.bfloat16)
    for i in range(copies_ref.shape[0]):
        copies_ref[i] = scaled


def gate_up_kernel(mine_ref, theirs_ref, gate_ref, gate_theirs_ref, up_ref, up_theirs_ref, o_ref):
    both = jnp.concatenate([gate_ref[...], up_ref[...]], axis=1)
    both_theirs = jnp.concatenate([gate_theirs_ref[...], up_theirs_ref[...]], axis=1)
    o_ref[...] = (matmul(mine_ref[...], both) + matmul(theirs_ref[...], both_theirs)).astype(jnp.bfloat16)


def squares_kernel(mine_ref, theirs_ref, gain_ref, gain_theirs_ref, o_ref):
    one = mine_ref[...].astype(jnp.float32) * (1.0 / gain_ref[...].astype(jnp.float32))
    two = theirs_ref[...].astype(jnp.float32) * (1.0 / gain_theirs_ref[...].astype(jnp.float32))
    squares = jnp.sum(one * one + two * two, axis=1, keepdims=True)
    at = lax.broadcasted_iota(jnp.int32, (128, 128), 0) == lax.broadcasted_iota(jnp.int32, (128, 128), 1)
    for i in range(o_ref.shape[0]):
        o_ref[i:i + 1] = jnp.sum(jnp.where(at, squares[i * 128:(i + 1) * 128], 0.0), axis=0, keepdims=True)


def hidden_kernel(parts_ref, squares_ref, copies_ref):
    group = parts_ref.shape[1]
    chip = lax.axis_index("x") * 2 + lax.axis_index("yl")
    sums = parts_ref[0].astype(jnp.float32)
    for i in range(1, parts_ref.shape[0]):
        sums = sums + parts_ref[i].astype(jnp.float32)
    to = lax.broadcasted_iota(jnp.int32, (group, 128), 0) + lax.rem(chip, 128 // group) * group
    lane = lax.broadcasted_iota(jnp.int32, (group, 128), 1)
    line = lax.broadcasted_iota(jnp.int32, squares_ref.shape, 0) == chip // (128 // group)
    wanted = jnp.sum(jnp.where(line, squares_ref[...], 0.0), axis=0, keepdims=True)
    squares = jnp.sum(jnp.where(to == lane, wanted, 0.0), axis=1, keepdims=True)
    inv_rms = lax.rsqrt(squares / D + eps)
    for i in range(copies_ref.shape[2] // 128):
        gate = sums[:, i * 256:i * 256 + 128] * inv_rms
        up = sums[:, i * 256 + 128:i * 256 + 256] * inv_rms
        hidden = (gate / (1.0 + jnp.exp(-gate)) * up).astype(jnp.bfloat16)
        for j in range(copies_ref.shape[0]):
            copies_ref[j, :, i * 128:(i + 1) * 128] = hidden


def down_kernel(mine_ref, theirs_ref, weight_ref, o_ref):
    half = mine_ref.shape[1]
    core = lax.axis_index("core")
    part = matmul(mine_ref[...], weight_ref[0, pl.ds(pl.multiple_of(core * half, half), half), :])
    part = part + matmul(theirs_ref[...], weight_ref[0, pl.ds(pl.multiple_of((1 - core) * half, half), half), :])
    o_ref[...] = part.astype(jnp.bfloat16)


def final_kernel(parts_ref, stream_ref, copies_ref):
    total = parts_ref[0].astype(jnp.float32)
    for i in range(1, parts_ref.shape[0]):
        total = total + parts_ref[i].astype(jnp.float32)
    final = stream_ref[...] + total
    count, slots = copies_ref.shape[0] // 2, copies_ref.shape[1]
    for i in range(count):
        block = final[i * slots:(i + 1) * slots].astype(jnp.bfloat16)
        copies_ref[i] = block
        copies_ref[count + i] = block


def output_kernel(back_ref, o_ref):
    width = back_ref.shape[2]
    chips = back_ref.shape[0] // 4
    half = chips // 2
    side = lax.axis_index("side")
    for chip in range(half):
        for core in range(2):
            at = (2 * chip + core) * width
            o_ref[:, at:at + width] = back_ref[(2 + core) * chips + side * half + chip]


def local(queries, new_entries, cache_keys, cache_values, lengths, residual, norm_gain, out_weight, gate_weight, up_weight, down_weight):
    bf16 = jnp.bfloat16
    rows, pairs, chips = lax.axis_size(ROW), lax.axis_size("rp"), lax.axis_size(CHIPS)
    core = lax.axis_index("core")
    slots, width = queries.shape[0], out_weight.shape[2]
    heads = out_weight.shape[1]
    half = gate_weight.shape[2] // 2
    group = chips * 2 * slots
    total = rows * group
    pair = flip(out_weight, "rl")
    gain = norm_gain[None, :]
    gain_theirs = flip(gain, "core")
    gate_theirs = flip(lax.dynamic_slice_in_dim(gate_weight[0], (1 - core) * half, half, 1), "core")
    up_theirs = flip(lax.dynamic_slice_in_dim(up_weight[0], (1 - core) * half, half, 1), "core")

    gate_mine = lax.dynamic_slice_in_dim(gate_weight[0], core * half, half, 1)
    up_mine = lax.dynamic_slice_in_dim(up_weight[0], core * half, half, 1)
    blocks = attention(queries, new_entries, cache_keys, cache_values, lengths, pairs)
    blocks = [to_ffn(block, k) for k, block in enumerate(blocks)]
    fanned = call(fan_kernel, "fan", jax.ShapeDtypeStruct((chips, pairs * 2 * slots, heads), bf16), in_specs=[WHOLE] * pairs + [HELD], out_specs=WHOLE)(*blocks, pair)
    near = exchange(fanned, CHIPS).reshape(chips * pairs * 2 * slots, heads)
    far = flip(near, "core")
    own, *parts = call(project_kernel, "project", [jax.ShapeDtypeStruct((2, group // 2, width), bf16)] * pairs, in_specs=[WHOLE] * 4, out_specs=[WHOLE] * pairs)(near, far, out_weight, pair)
    parts = [own] + [turn(part, k + 1) for k, part in enumerate(parts)]
    parts = [part.reshape(group, width) for part in parts]
    stream, copies = call(stream_kernel, "stream", (jax.ShapeDtypeStruct((group, width), jnp.float32), jax.ShapeDtypeStruct((rows, group, width), bf16)), in_specs=[WHOLE] * (pairs + 2), out_specs=(WHOLE, WHOLE))(
        *parts, residual, gain)
    scaled = exchange(copies, HOME).reshape(total, width)
    scaled_theirs = flip(scaled, "core")
    steps = half // 128
    fixed = pl.BlockSpec((total, width), lambda i: (0, 0))
    piece = pl.BlockSpec((width, 128), lambda i: (0, i))
    grid_spec = pltpu.PrefetchScalarGridSpec(num_scalar_prefetch=0, grid=(steps,), in_specs=[fixed, fixed] + [piece] * 4, out_specs=pl.BlockSpec((total, 256), lambda i: (0, i)))
    sent = call(gate_up_kernel, "gate_up", pltpu.HBM((total, 2 * half), bf16), grid_spec=grid_spec)(scaled, scaled_theirs, gate_mine, gate_theirs, up_mine, up_theirs)
    squares = call(squares_kernel, "squares", jax.ShapeDtypeStruct((total // 128, 128), jnp.float32), in_specs=[WHOLE] * 4, out_specs=WHOLE)(scaled, scaled_theirs, gain, gain_theirs)
    squares = squares + flip(squares, "yl")
    for distance in (1, 2):
        squares = squares + lax.ppermute(squares, "x", [(i, i ^ distance) for i in range(lax.axis_size("x"))])
    sums = exchange(sent.reshape(chips, group, 2 * half), CHIPS)
    hidden = call(hidden_kernel, "hidden", jax.ShapeDtypeStruct((chips, group, half), bf16), in_specs=[WHOLE] * 2, out_specs=WHOLE)(sums, squares)
    hidden = exchange(hidden, CHIPS).reshape(total, half)
    down = call(down_kernel, "down", jax.ShapeDtypeStruct((total, width), bf16), in_specs=[WHOLE] * 3, out_specs=WHOLE)(hidden, flip(hidden, "core"), down_weight)
    downs = exchange(down.reshape(rows, group, width), HOME)
    final = call(final_kernel, "final", jax.ShapeDtypeStruct((4 * chips, slots, width), bf16), in_specs=[WHOLE] * 2, out_specs=WHOLE)(downs, stream)
    back = exchange(final, ("side", "core") + CHIPS)
    return call(output_kernel, "output", jax.ShapeDtypeStruct((slots, width * chips), bf16), in_specs=[WHOLE], out_specs=WHOLE)(back)


def solution(mesh):
    sides, rows, cols = mesh.devices.shape
    inner = Mesh(mesh.devices.reshape(sides, rows // 2, 2, cols // 4, 2, 2), ("side",) + ROW + COL)
    in_specs = (
        P(ROW + COL, None),
        P(ROW + COL, None),
        P("side", ROW + COL, None, None),
        P("side", ROW + COL, None, None),
        P(ROW + COL),
        P(None, COL),
        P(COL),
        P("side", ROW, COL),
        P("side", COL, ROW),
        P("side", COL, ROW),
        P("side", ROW, COL),
    )
    return jax.shard_map(local, mesh=inner, in_specs=in_specs, out_specs=P(ROW + COL, "side"), check_vma=False)
```

```python
import functools
import math
import jax
import jax.numpy as jnp
from jax import lax
from jax.experimental import pallas as pl
from jax.experimental.pallas import tpu as pltpu
from jax.sharding import Mesh, PartitionSpec as P

D = 8192
H = 64
KVH = 8
HD = 128
ORIG = 64
PER = H // KVH

rope_theta = 500000.0
stretch_factor = 8.0
eps = 1e-05

CHIPS = ("x", "yl")
COL = ("x", "yl", "core")
ROW = ("rp", "rl")
HOME = ("rl", "rp")
WHOLE = pl.BlockSpec(memory_space=pltpu.VMEM)
HELD = pl.BlockSpec(memory_space=pl.ANY)
SCALARS = pl.BlockSpec(memory_space=pltpu.SMEM)


def swap_halves(v):
    return jnp.concatenate([v[:, HD // 2:], v[:, : HD // 2]], axis=-1)


def attend_kernel(len_ref, q_ref, new_ref, k_lo_ref, k_hi_ref, v_lo_ref, v_hi_ref, *rest):
    o_refs, (q_all, new_all, s_all, acc, out_all, fine_all, coarse_all, at_all) = rest[:-8], rest[-8:]
    slot = pl.program_id(0)
    slots = q_ref.shape[0]
    length = len_ref[slot]
    half = k_lo_ref.shape[2]
    span = 2 * half

    @pl.when(slot == 0)
    def _():
        for h in range(H):
            q_all[:, h, :] = q_ref[:, h * HD:(h + 1) * HD].astype(jnp.float32)
        for h in range(2 * KVH):
            new_all[:, h, :] = new_ref[:, h * HD:(h + 1) * HD].astype(jnp.float32)

    steps = span // 16
    lane = lax.broadcasted_iota(jnp.int32, (1, HD), 1)
    sign = jnp.where(lane < HD // 2, -1.0, 1.0)

    @pl.when(slot == 0)
    def _():
        pair = jnp.where(lane < HD // 2, lane, lane - HD // 2).astype(jnp.float32)
        positions = jnp.concatenate([jnp.full((8, HD), len_ref[j], jnp.int32) for j in range(slots)], axis=0).astype(jnp.float32)
        stretch = jnp.maximum(stretch_factor * (positions + 1.0) / ORIG - (stretch_factor - 1.0), 1.0)
        log_base = math.log(rope_theta) + HD / (HD - 2.0) * jnp.log(stretch)
        freqs = jnp.exp(-(pair * (2.0 / HD)) * log_base)
        low = lax.broadcasted_iota(jnp.int32, (16, HD), 0).astype(jnp.float32)
        high = lax.broadcasted_iota(jnp.int32, (steps, HD), 0).astype(jnp.float32) * 16.0
        each = [freqs[8 * j:8 * j + 1] for j in range(slots)]
        angles = jnp.concatenate([low * f for f in each] + [high * f for f in each] + [positions * freqs], axis=0)
        cosine, sine = jnp.cos(angles), jnp.sin(angles)
        for j in range(slots):
            fine_all[j, 0] = cosine[16 * j:16 * j + 16]
            fine_all[j, 1] = sine[16 * j:16 * j + 16]
            at = 16 * slots + steps * j
            coarse_all[j, 0] = cosine[at:at + steps]
            coarse_all[j, 1] = sine[at:at + steps]
            at = (16 + steps) * slots + 8 * j
            at_all[j, 0] = cosine[at:at + 8]
            at_all[j, 1] = sine[at:at + 8]

    fine_cos, fine_sin = fine_all[slot, 0], fine_all[slot, 1]
    coarse_cos, coarse_sin = coarse_all[slot, 0], coarse_all[slot, 1]

    def tables(first):
        cos_parts, sin_parts = [], []
        for step in range(first, first + steps // 2):
            cc, cs = coarse_cos[step:step + 1], coarse_sin[step:step + 1]
            cos_parts.append(cc * fine_cos - cs * fine_sin)
            sin_parts.append(cs * fine_cos + cc * fine_sin)
        return jnp.concatenate(cos_parts, axis=0), jnp.concatenate(sin_parts, axis=0)

    cos_new = at_all[slot, 0, :1]
    sin_new = at_all[slot, 1, :1] * sign
    q = q_all[slot]
    q_rot = q * cos_new + swap_halves(q) * sin_new
    q_rot = q_rot.astype(jnp.bfloat16).astype(jnp.float32)
    q_both = jnp.concatenate([q_rot, swap_halves(q_rot) * -sign], axis=-1)
    k_new = new_all[slot, :KVH]
    k_new = k_new * cos_new + swap_halves(k_new) * sin_new
    k_new = k_new.astype(jnp.bfloat16).astype(jnp.float32)
    v_new = new_all[slot, KVH:]
    scale = HD ** (-0.5)

    def score(k_ref, first):
        cos_t, sin_t = tables(first)
        for g in range(KVH):
            kg = k_ref[0, 0, :, g * HD:(g + 1) * HD].astype(jnp.float32)
            kk = jnp.concatenate([(kg * cos_t).astype(jnp.bfloat16), (kg * sin_t).astype(jnp.bfloat16)], axis=-1)
            qg = q_both[g * PER:(g + 1) * PER].astype(jnp.bfloat16)
            s_all[g * PER:(g + 1) * PER, first * 16:first * 16 + half] = lax.dot_general(qg, kk, (((1,), (1,)), ((), ())), preferred_element_type=jnp.float32)

    score(k_lo_ref, 0)

    @pl.when(length > half)
    def _():
        score(k_hi_ref, steps // 2)

    @pl.when(length <= half)
    def _():
        s_all[:, half:] = jnp.zeros((H, half), jnp.float32)

    own, fresh = [], []
    for g in range(KVH):
        own.append(jnp.sum(q_rot[g * PER:(g + 1) * PER] * k_new[g:g + 1], axis=-1, keepdims=True))
        fresh.append(jnp.broadcast_to(v_new[g:g + 1], (PER, HD)))
    own_score = jnp.concatenate(own, axis=0) * scale
    valid = lax.broadcasted_iota(jnp.int32, (H, span), 1) < length
    s = jnp.where(valid, s_all[...] * scale, -1e30)
    top = jnp.maximum(jnp.max(s, axis=-1, keepdims=True), own_score)
    w = jnp.where(valid, jnp.exp(s - top), 0.0)
    own_w = jnp.exp(own_score - top)
    total = jnp.sum(w, axis=-1, keepdims=True) + own_w
    w16 = w.astype(jnp.bfloat16)

    def mix(v_ref, weights):
        parts = []
        for p in range(KVH // 2):
            o = jnp.dot(weights[p * 2 * PER:(p + 1) * 2 * PER], v_ref[0, 0, :, p * 2 * HD:(p + 1) * 2 * HD], preferred_element_type=jnp.float32)
            parts += [o[:PER, :HD], o[PER:, HD:]]
        return jnp.concatenate(parts, axis=0)

    acc[...] = mix(v_lo_ref, w16[:, :half]) + own_w * jnp.concatenate(fresh, axis=0)

    @pl.when(length > half)
    def _():
        acc[...] += mix(v_hi_ref, w16[:, half:])

    out = acc[...] / total
    pairs = len(o_refs)
    per_row = H // (2 * pairs)
    for h in range(H):
        at, q_at = h // per_row, h % per_row
        out_all[at // 2, slot, at % 2:at % 2 + 1, q_at * HD:(q_at + 1) * HD] = out[h:h + 1]

    @pl.when(slot == slots - 1)
    def _():
        for k in range(pairs):
            home = lax.rem(lax.axis_index("rp") + k, pairs)
            o_refs[k][...] = jnp.concatenate([out_all[home, j] for j in range(slots)], axis=0).astype(jnp.bfloat16)


def attention(queries, new_entries, cache_keys, cache_values, lengths, pairs):
    slots = queries.shape[0]
    half = cache_keys.shape[2] // 2
    width = KVH * HD
    low = pl.BlockSpec((1, 1, half, width), lambda s, n: (0, s, 0, 0))

    def last_long(s, n):
        at = 0
        for j in range(1, slots):
            at = jnp.where((s >= j) & (n[j] > half), j, at)
        return (0, at, 1, 0)

    high = pl.BlockSpec((1, 1, half, width), last_long)
    heads = H * HD // (2 * pairs)
    grid_spec = pltpu.PrefetchScalarGridSpec(
        num_scalar_prefetch=1, grid=(slots,),
        in_specs=[pl.BlockSpec((slots, H * HD), lambda s, n: (0, 0)), pl.BlockSpec((slots, 2 * width), lambda s, n: (0, 0)), low, high, low, high],
        out_specs=[pl.BlockSpec((2 * slots, heads), lambda s, n: (0, 0))] * pairs,
        scratch_shapes=[
            pltpu.VMEM((slots, H, HD), jnp.float32), pltpu.VMEM((slots, 2 * KVH, HD), jnp.float32),
            pltpu.VMEM((H, 2 * half), jnp.float32), pltpu.VMEM((H, HD), jnp.float32), pltpu.VMEM((pairs, slots, 2, heads), jnp.float32),
            pltpu.VMEM((slots, 2, 16, HD), jnp.float32), pltpu.VMEM((slots, 2, 2 * half // 16, HD), jnp.float32), pltpu.VMEM((slots, 2, 8, HD), jnp.float32)])
    return pl.pallas_call(
        attend_kernel, grid_spec=grid_spec,
        out_shape=[jax.ShapeDtypeStruct((2 * slots, heads), jnp.bfloat16)] * pairs,
        compiler_params=pltpu.CompilerParams(vmem_limit_bytes=60 << 20), name="attend",
    )(lengths, queries, new_entries, cache_keys, cache_keys, cache_values, cache_values)


def flip(value, axis):
    return lax.ppermute(value, axis, [(0, 1), (1, 0)])


def turn(value, steps):
    count = lax.axis_size("rp")
    return lax.ppermute(value, "rp", [(i, (i + steps) % count) for i in range(count)])


def to_ffn(value, steps):
    count = lax.axis_size("rp")
    return lax.ppermute(value, ("side", "rp"), [(i, count + (i + steps) % count) for i in range(count)])


def exchange(value, axes):
    return lax.all_to_all(value, axes, split_axis=0, concat_axis=0, tiled=True)


def matmul(left, right):
    return jnp.dot(left, right, preferred_element_type=jnp.float32)


def call(kernel, name, out_shape, **options):
    limit = options.pop("limit", 24)
    return pl.pallas_call(kernel, out_shape=out_shape, name=name, compiler_params=pltpu.CompilerParams(vmem_limit_bytes=limit << 20), **options)


def fan_kernel(*refs):
    blocks, o_ref = refs[:-2], refs[-1]
    rows = blocks[0].shape[0]
    for i in range(o_ref.shape[0]):
        for k, block in enumerate(blocks):
            o_ref[i, k * rows:(k + 1) * rows] = block[...]


def project_kernel(near_ref, far_ref, own_ref, pair_a_ref, pair_b_ref, held_ref, *o_refs):
    core, low = lax.axis_index("core"), lax.axis_index("rl")
    pairs, group = len(o_refs), o_refs[0].shape[1]
    slots = near_ref.shape[0] // (2 * pairs * (group // 4))
    rows = pairs * group
    cut = pair_a_ref.shape[0]
    to = lax.broadcasted_iota(jnp.int32, (rows, 2 * rows), 0)
    source = lax.broadcasted_iota(jnp.int32, (rows, 2 * rows), 1)
    block = (pairs - to // group) % pairs
    first = ((to % group) // slots) * (2 * slots * pairs) + block * (2 * slots) + (to % slots) * 2
    pick_own = (source == first + low).astype(jnp.bfloat16)
    pick_pair = (source == first + 1 - low).astype(jnp.bfloat16)
    for left_ref, place in ((near_ref, core), (far_ref, 1 - core)):
        part = matmul(matmul(pick_own, left_ref[...]).astype(jnp.bfloat16), own_ref[0])
        theirs = matmul(pick_pair, left_ref[...]).astype(jnp.bfloat16)
        part = part + matmul(theirs[:, :cut], pair_a_ref[...]) + matmul(theirs[:, cut:], pair_b_ref[...])
        for k in range(pairs):
            o_refs[k][place] = part[k * group:(k + 1) * group].astype(jnp.bfloat16)


def stream_kernel(*refs):
    parts, (residual_ref, gain_ref, stream_ref, copies_ref) = refs[:-4], refs[-4:]
    group = stream_ref.shape[0]
    chips = group // 8
    row = lax.axis_index("rp") * 2 + lax.axis_index("rl")
    to = lax.broadcasted_iota(jnp.int32, (group, group), 0)
    source = lax.broadcasted_iota(jnp.int32, (group, group), 1)
    order = (source == (to // 4 % chips) * 8 + (to // (4 * chips)) * 4 + to % 4).astype(jnp.bfloat16)
    stream = matmul(order, residual_ref[pl.ds(pl.multiple_of(row * group, group), group), :])
    for part_ref in parts:
        stream = stream + part_ref[...].astype(jnp.float32)
    stream_ref[...] = stream
    scaled = (stream * gain_ref[...].astype(jnp.float32)).astype(jnp.bfloat16)
    for i in range(copies_ref.shape[0]):
        copies_ref[i] = scaled


def gate_up_kernel(mine_ref, theirs_ref, gain_ref, gain_theirs_ref, gate_ref, gate_theirs_ref, up_ref, up_theirs_ref, o_ref):
    half = gate_ref.shape[1]
    mine, theirs = mine_ref[...], theirs_ref[...]
    o_ref[:, :half] = (matmul(mine, gate_ref[...]) + matmul(theirs, gate_theirs_ref[...])).astype(jnp.bfloat16)
    o_ref[:, half:2 * half] = (matmul(mine, up_ref[...]) + matmul(theirs, up_theirs_ref[...])).astype(jnp.bfloat16)
    one = mine.astype(jnp.float32) * (1.0 / gain_ref[...].astype(jnp.float32))
    two = theirs.astype(jnp.float32) * (1.0 / gain_theirs_ref[...].astype(jnp.float32))
    squares = jnp.sum(one * one + two * two, axis=1, keepdims=True)
    high = squares.astype(jnp.bfloat16).astype(jnp.float32)
    lane = lax.broadcasted_iota(jnp.int32, (mine.shape[0], 128), 1)
    o_ref[:, 2 * half:] = jnp.where(lane == 0, high, jnp.where(lane == 1, squares - high, 0.0)).astype(jnp.bfloat16)


def hidden_kernel(parts_ref, copies_ref):
    half = copies_ref.shape[2]
    sums = parts_ref[0].astype(jnp.float32)
    for i in range(1, parts_ref.shape[0]):
        sums = sums + parts_ref[i].astype(jnp.float32)
    squares = sums[:, 2 * half:2 * half + 1] + sums[:, 2 * half + 1:2 * half + 2]
    inv_rms = lax.rsqrt(squares / D + eps)
    gate = sums[:, :half] * inv_rms
    up = sums[:, half:2 * half] * inv_rms
    hidden = (gate / (1.0 + jnp.exp(-gate)) * up).astype(jnp.bfloat16)
    for i in range(copies_ref.shape[0]):
        copies_ref[i] = hidden


def down_kernel(mine_ref, theirs_ref, weight_ref, o_ref):
    half = mine_ref.shape[1]
    core = lax.axis_index("core")
    part = matmul(mine_ref[...], weight_ref[0, pl.ds(pl.multiple_of(core * half, half), half), :])
    part = part + matmul(theirs_ref[...], weight_ref[0, pl.ds(pl.multiple_of((1 - core) * half, half), half), :])
    o_ref[...] = part.astype(jnp.bfloat16)


def final_kernel(parts_ref, stream_ref, copies_ref):
    total = parts_ref[0].astype(jnp.float32)
    for i in range(1, parts_ref.shape[0]):
        total = total + parts_ref[i].astype(jnp.float32)
    final = stream_ref[...] + total
    count, slots = copies_ref.shape[0] // 2, copies_ref.shape[1]
    for i in range(count):
        block = final[i * slots:(i + 1) * slots].astype(jnp.bfloat16)
        copies_ref[i] = block
        copies_ref[count + i] = block


def output_kernel(back_ref, o_ref):
    width = back_ref.shape[2]
    chips = back_ref.shape[0] // 4
    half = chips // 2
    side = lax.axis_index("side")
    for chip in range(half):
        for core in range(2):
            at = (2 * chip + core) * width
            o_ref[:, at:at + width] = back_ref[(2 + core) * chips + side * half + chip]


def local(queries, new_entries, cache_keys, cache_values, lengths, residual, norm_gain, out_weight, gate_weight, up_weight, down_weight):
    bf16 = jnp.bfloat16
    rows, pairs, chips = lax.axis_size(ROW), lax.axis_size("rp"), lax.axis_size(CHIPS)
    core = lax.axis_index("core")
    slots, width = queries.shape[0], out_weight.shape[2]
    heads = out_weight.shape[1]
    half = gate_weight.shape[2] // 2
    group = chips * 2 * slots
    total = rows * group
    cut = heads // 8 * 3
    pair_a = flip(out_weight[0, :cut], "rl")
    pair_b = flip(out_weight[0, cut:], "rl")
    gain = norm_gain[None, :]
    gain_theirs = flip(gain, "core")
    gate_theirs = flip(lax.dynamic_slice_in_dim(gate_weight[0], (1 - core) * half, half, 1), "core")
    up_theirs = flip(lax.dynamic_slice_in_dim(up_weight[0], (1 - core) * half, half, 1), "core")

    gate_mine = lax.dynamic_slice_in_dim(gate_weight[0], core * half, half, 1)
    up_mine = lax.dynamic_slice_in_dim(up_weight[0], core * half, half, 1)
    blocks = attention(queries, new_entries, cache_keys, cache_values, lengths, pairs)
    blocks = [to_ffn(block, k) for k, block in enumerate(blocks)]
    fanned = call(fan_kernel, "fan", jax.ShapeDtypeStruct((chips, pairs * 2 * slots, heads), bf16), in_specs=[WHOLE] * pairs + [HELD], out_specs=WHOLE)(*blocks, pair_a)
    near = exchange(fanned, CHIPS).reshape(chips * pairs * 2 * slots, heads)
    far = flip(near, "core")
    own, *parts = call(project_kernel, "project", [jax.ShapeDtypeStruct((2, group // 2, width), bf16)] * pairs, in_specs=[WHOLE] * 5 + [HELD], out_specs=[WHOLE] * pairs)(near, far, out_weight, pair_a, pair_b, gain_theirs)
    parts = [own] + [turn(part, k + 1) for k, part in enumerate(parts)]
    parts = [part.reshape(group, width) for part in parts]
    stream, copies = call(stream_kernel, "stream", (jax.ShapeDtypeStruct((group, width), jnp.float32), jax.ShapeDtypeStruct((rows, group, width), bf16)), in_specs=[WHOLE] * (pairs + 2), out_specs=(WHOLE, WHOLE))(
        *parts, residual, gain)
    scaled = exchange(copies, HOME).reshape(total, width)
    scaled_theirs = flip(scaled, "core")
    sent = call(gate_up_kernel, "gate_up", jax.ShapeDtypeStruct((total, 2 * half + 128), bf16), in_specs=[WHOLE] * 8, out_specs=WHOLE)(
        scaled, scaled_theirs, gain, gain_theirs, gate_mine, gate_theirs, up_mine, up_theirs)
    sums = exchange(sent.reshape(chips, group, 2 * half + 128), CHIPS)
    hidden = call(hidden_kernel, "hidden", jax.ShapeDtypeStruct((chips, group, half), bf16), in_specs=[WHOLE], out_specs=WHOLE)(sums)
    hidden = exchange(hidden, CHIPS).reshape(total, half)
    down = call(down_kernel, "down", jax.ShapeDtypeStruct((total, width), bf16), in_specs=[WHOLE] * 3, out_specs=WHOLE)(hidden, flip(hidden, "core"), down_weight)
    downs = exchange(down.reshape(rows, group, width), HOME)
    final = call(final_kernel, "final", jax.ShapeDtypeStruct((4 * chips, slots, width), bf16), in_specs=[WHOLE] * 2, out_specs=WHOLE)(downs, stream)
    back = exchange(final, ("side", "core") + CHIPS)
    return call(output_kernel, "output", jax.ShapeDtypeStruct((slots, width * chips), bf16), in_specs=[WHOLE], out_specs=WHOLE)(back)


def solution(mesh):
    sides, rows, cols = mesh.devices.shape
    inner = Mesh(mesh.devices.reshape(sides, rows // 2, 2, cols // 4, 2, 2), ("side",) + ROW + COL)
    in_specs = (
        P(ROW + COL, None),
        P(ROW + COL, None),
        P("side", ROW + COL, None, None),
        P("side", ROW + COL, None, None),
        P(ROW + COL),
        P(None, COL),
        P(COL),
        P("side", ROW, COL),
        P("side", COL, ROW),
        P("side", COL, ROW),
        P("side", ROW, COL),
    )
    return jax.shard_map(local, mesh=inner, in_specs=in_specs, out_specs=P(ROW + COL, "side"), check_vma=False)
```

```python
import functools
import math
import jax
import jax.numpy as jnp
from jax import lax
from jax.experimental import pallas as pl
from jax.experimental.pallas import tpu as pltpu
from jax.sharding import Mesh, PartitionSpec as P

D = 8192
H = 64
KVH = 8
HD = 128
ORIG = 64
PER = H // KVH

rope_theta = 500000.0
stretch_factor = 8.0
eps = 1e-05

CHIPS = ("x", "yl")
COL = ("x", "yl", "core")
ROW = ("rp", "rl")
HOME = ("rl", "rp")
WHOLE = pl.BlockSpec(memory_space=pltpu.VMEM)
HELD = pl.BlockSpec(memory_space=pl.ANY)
SCALARS = pl.BlockSpec(memory_space=pltpu.SMEM)


def swap_halves(v):
    return jnp.concatenate([v[:, HD // 2:], v[:, : HD // 2]], axis=-1)


def attend_kernel(len_ref, q_ref, new_ref, k_lo_ref, k_hi_ref, v_lo_ref, v_hi_ref, *rest):
    o_refs, (q_all, new_all, s_all, acc, out_all, fine_all, coarse_all, at_all) = rest[:-8], rest[-8:]
    slot = pl.program_id(0)
    slots = q_ref.shape[0]
    length = len_ref[slot]
    half = k_lo_ref.shape[2]
    span = 2 * half

    @pl.when(slot == 0)
    def _():
        for h in range(H):
            q_all[:, h, :] = q_ref[:, h * HD:(h + 1) * HD].astype(jnp.float32)
        for h in range(2 * KVH):
            new_all[:, h, :] = new_ref[:, h * HD:(h + 1) * HD].astype(jnp.float32)

    steps = span // 16
    lane = lax.broadcasted_iota(jnp.int32, (1, HD), 1)
    sign = jnp.where(lane < HD // 2, -1.0, 1.0)

    @pl.when(slot == 0)
    def _():
        pair = jnp.where(lane < HD // 2, lane, lane - HD // 2).astype(jnp.float32)
        positions = jnp.concatenate([jnp.full((8, HD), len_ref[j], jnp.int32) for j in range(slots)], axis=0).astype(jnp.float32)
        stretch = jnp.maximum(stretch_factor * (positions + 1.0) / ORIG - (stretch_factor - 1.0), 1.0)
        log_base = math.log(rope_theta) + HD / (HD - 2.0) * jnp.log(stretch)
        freqs = jnp.exp(-(pair * (2.0 / HD)) * log_base)
        low = lax.broadcasted_iota(jnp.int32, (16, HD), 0).astype(jnp.float32)
        high = lax.broadcasted_iota(jnp.int32, (steps, HD), 0).astype(jnp.float32) * 16.0
        each = [freqs[8 * j:8 * j + 1] for j in range(slots)]
        angles = jnp.concatenate([low * f for f in each] + [high * f for f in each] + [positions * freqs], axis=0)
        cosine, sine = jnp.cos(angles), jnp.sin(angles)
        for j in range(slots):
            fine_all[j, 0] = cosine[16 * j:16 * j + 16]
            fine_all[j, 1] = sine[16 * j:16 * j + 16]
            at = 16 * slots + steps * j
            coarse_all[j, 0] = cosine[at:at + steps]
            coarse_all[j, 1] = sine[at:at + steps]
            at = (16 + steps) * slots + 8 * j
            at_all[j, 0] = cosine[at:at + 8]
            at_all[j, 1] = sine[at:at + 8]

    fine_cos, fine_sin = fine_all[slot, 0], fine_all[slot, 1]
    coarse_cos, coarse_sin = coarse_all[slot, 0], coarse_all[slot, 1]

    def tables(first):
        cos_parts, sin_parts = [], []
        for step in range(first, first + steps // 2):
            cc, cs = coarse_cos[step:step + 1], coarse_sin[step:step + 1]
            cos_parts.append(cc * fine_cos - cs * fine_sin)
            sin_parts.append(cs * fine_cos + cc * fine_sin)
        return jnp.concatenate(cos_parts, axis=0), jnp.concatenate(sin_parts, axis=0)

    cos_new = at_all[slot, 0, :1]
    sin_new = at_all[slot, 1, :1] * sign
    q = q_all[slot]
    q_rot = q * cos_new + swap_halves(q) * sin_new
    q_rot = q_rot.astype(jnp.bfloat16).astype(jnp.float32)
    q_both = jnp.concatenate([q_rot, swap_halves(q_rot) * -sign], axis=-1)
    k_new = new_all[slot, :KVH]
    k_new = k_new * cos_new + swap_halves(k_new) * sin_new
    k_new = k_new.astype(jnp.bfloat16).astype(jnp.float32)
    v_new = new_all[slot, KVH:]
    scale = HD ** (-0.5)

    def score(k_ref, first):
        cos_t, sin_t = tables(first)
        for g in range(KVH):
            kg = k_ref[0, 0, :, g * HD:(g + 1) * HD].astype(jnp.float32)
            kk = jnp.concatenate([(kg * cos_t).astype(jnp.bfloat16), (kg * sin_t).astype(jnp.bfloat16)], axis=-1)
            qg = q_both[g * PER:(g + 1) * PER].astype(jnp.bfloat16)
            s_all[g * PER:(g + 1) * PER, first * 16:first * 16 + half] = lax.dot_general(qg, kk, (((1,), (1,)), ((), ())), preferred_element_type=jnp.float32)

    score(k_lo_ref, 0)

    @pl.when(length > half)
    def _():
        score(k_hi_ref, steps // 2)

    @pl.when(length <= half)
    def _():
        s_all[:, half:] = jnp.zeros((H, half), jnp.float32)

    own, fresh = [], []
    for g in range(KVH):
        own.append(jnp.sum(q_rot[g * PER:(g + 1) * PER] * k_new[g:g + 1], axis=-1, keepdims=True))
        fresh.append(jnp.broadcast_to(v_new[g:g + 1], (PER, HD)))
    own_score = jnp.concatenate(own, axis=0) * scale
    valid = lax.broadcasted_iota(jnp.int32, (H, span), 1) < length
    s = jnp.where(valid, s_all[...] * scale, -1e30)
    top = jnp.maximum(jnp.max(s, axis=-1, keepdims=True), own_score)
    w = jnp.where(valid, jnp.exp(s - top), 0.0)
    own_w = jnp.exp(own_score - top)
    total = jnp.sum(w, axis=-1, keepdims=True) + own_w
    w16 = w.astype(jnp.bfloat16)

    def mix(v_ref, weights):
        parts = []
        for p in range(KVH // 2):
            o = jnp.dot(weights[p * 2 * PER:(p + 1) * 2 * PER], v_ref[0, 0, :, p * 2 * HD:(p + 1) * 2 * HD], preferred_element_type=jnp.float32)
            parts += [o[:PER, :HD], o[PER:, HD:]]
        return jnp.concatenate(parts, axis=0)

    acc[...] = mix(v_lo_ref, w16[:, :half]) + own_w * jnp.concatenate(fresh, axis=0)

    @pl.when(length > half)
    def _():
        acc[...] += mix(v_hi_ref, w16[:, half:])

    out = acc[...] / total
    pairs = len(o_refs)
    per_row = H // (2 * pairs)
    for h in range(H):
        at, q_at = h // per_row, h % per_row
        out_all[at // 2, slot, at % 2:at % 2 + 1, q_at * HD:(q_at + 1) * HD] = out[h:h + 1]

    @pl.when(slot == slots - 1)
    def _():
        for k in range(pairs):
            home = lax.rem(lax.axis_index("rp") + k, pairs)
            o_refs[k][...] = jnp.concatenate([out_all[home, j] for j in range(slots)], axis=0).astype(jnp.bfloat16)


def attention(queries, new_entries, cache_keys, cache_values, lengths, pairs):
    slots = queries.shape[0]
    half = cache_keys.shape[2] // 2
    width = KVH * HD
    low = pl.BlockSpec((1, 1, half, width), lambda s, n: (0, s, 0, 0))

    def last_long(s, n):
        at = 0
        for j in range(1, slots):
            at = jnp.where((s >= j) & (n[j] > half), j, at)
        return (0, at, 1, 0)

    high = pl.BlockSpec((1, 1, half, width), last_long)
    heads = H * HD // (2 * pairs)
    grid_spec = pltpu.PrefetchScalarGridSpec(
        num_scalar_prefetch=1, grid=(slots,),
        in_specs=[pl.BlockSpec((slots, H * HD), lambda s, n: (0, 0)), pl.BlockSpec((slots, 2 * width), lambda s, n: (0, 0)), low, high, low, high],
        out_specs=[pl.BlockSpec((2 * slots, heads), lambda s, n: (0, 0))] * pairs,
        scratch_shapes=[
            pltpu.VMEM((slots, H, HD), jnp.float32), pltpu.VMEM((slots, 2 * KVH, HD), jnp.float32),
            pltpu.VMEM((H, 2 * half), jnp.float32), pltpu.VMEM((H, HD), jnp.float32), pltpu.VMEM((pairs, slots, 2, heads), jnp.float32),
            pltpu.VMEM((slots, 2, 16, HD), jnp.float32), pltpu.VMEM((slots, 2, 2 * half // 16, HD), jnp.float32), pltpu.VMEM((slots, 2, 8, HD), jnp.float32)])
    return pl.pallas_call(
        attend_kernel, grid_spec=grid_spec,
        out_shape=[jax.ShapeDtypeStruct((2 * slots, heads), jnp.bfloat16)] * pairs,
        compiler_params=pltpu.CompilerParams(vmem_limit_bytes=60 << 20), name="attend",
    )(lengths, queries, new_entries, cache_keys, cache_keys, cache_values, cache_values)


def flip(value, axis):
    return lax.ppermute(value, axis, [(0, 1), (1, 0)])


def turn(value, steps):
    count = lax.axis_size("rp")
    return lax.ppermute(value, "rp", [(i, (i + steps) % count) for i in range(count)])


def to_ffn(value, steps):
    count = lax.axis_size("rp")
    return lax.ppermute(value, ("side", "rp"), [(i, count + (i + steps) % count) for i in range(count)])


def exchange(value, axes):
    return lax.all_to_all(value, axes, split_axis=0, concat_axis=0, tiled=True)


def matmul(left, right):
    return jnp.dot(left, right, preferred_element_type=jnp.float32)


def call(kernel, name, out_shape, **options):
    limit = options.pop("limit", 24)
    return pl.pallas_call(kernel, out_shape=out_shape, name=name, compiler_params=pltpu.CompilerParams(vmem_limit_bytes=limit << 20), **options)


def fan_kernel(*refs):
    blocks, o_ref = refs[:-3], refs[-1]
    rows = blocks[0].shape[0]
    for i in range(o_ref.shape[0]):
        for k, block in enumerate(blocks):
            o_ref[i, k * rows:(k + 1) * rows] = block[...]


def project_kernel(near_ref, far_ref, own_ref, pair_ref, *o_refs):
    core, low = lax.axis_index("core"), lax.axis_index("rl")
    pairs, group = len(o_refs), o_refs[0].shape[1]
    slots = near_ref.shape[0] // (2 * pairs * (group // 4))
    rows = pairs * group
    to = lax.broadcasted_iota(jnp.int32, (rows, 2 * rows), 0)
    source = lax.broadcasted_iota(jnp.int32, (rows, 2 * rows), 1)
    block = (pairs - to // group) % pairs
    first = ((to % group) // slots) * (2 * slots * pairs) + block * (2 * slots) + (to % slots) * 2
    pick_own = (source == first + low).astype(jnp.bfloat16)
    pick_pair = (source == first + 1 - low).astype(jnp.bfloat16)
    for left_ref, place in ((near_ref, core), (far_ref, 1 - core)):
        part = matmul(matmul(pick_own, left_ref[...]).astype(jnp.bfloat16), own_ref[0])
        part = part + matmul(matmul(pick_pair, left_ref[...]).astype(jnp.bfloat16), pair_ref[0])
        for k in range(pairs):
            o_refs[k][place] = part[k * group:(k + 1) * group].astype(jnp.bfloat16)


def stream_kernel(*refs):
    parts, (residual_ref, gain_ref, stream_ref, copies_ref) = refs[:-4], refs[-4:]
    group = stream_ref.shape[0]
    chips = group // 8
    row = lax.axis_index("rp") * 2 + lax.axis_index("rl")
    to = lax.broadcasted_iota(jnp.int32, (group, group), 0)
    source = lax.broadcasted_iota(jnp.int32, (group, group), 1)
    order = (source == (to // 4 % chips) * 8 + (to // (4 * chips)) * 4 + to % 4).astype(jnp.bfloat16)
    stream = matmul(order, residual_ref[pl.ds(pl.multiple_of(row * group, group), group), :])
    for part_ref in parts:
        stream = stream + part_ref[...].astype(jnp.float32)
    stream_ref[...] = stream
    scaled = (stream * gain_ref[...].astype(jnp.float32)).astype(jnp.bfloat16)
    for i in range(copies_ref.shape[0]):
        copies_ref[i] = scaled


def gate_up_kernel(mine_ref, theirs_ref, gain_ref, gain_theirs_ref, gate_ref, gate_theirs_ref, up_ref, up_theirs_ref, o_ref):
    half = gate_ref.shape[1]
    mine, theirs = mine_ref[...], theirs_ref[...]
    o_ref[:, :half] = (matmul(mine, gate_ref[...]) + matmul(theirs, gate_theirs_ref[...])).astype(jnp.bfloat16)
    o_ref[:, half:2 * half] = (matmul(mine, up_ref[...]) + matmul(theirs, up_theirs_ref[...])).astype(jnp.bfloat16)
    one = mine.astype(jnp.float32) * (1.0 / gain_ref[...].astype(jnp.float32))
    two = theirs.astype(jnp.float32) * (1.0 / gain_theirs_ref[...].astype(jnp.float32))
    squares = jnp.sum(one * one + two * two, axis=1, keepdims=True)
    high = squares.astype(jnp.bfloat16).astype(jnp.float32)
    lane = lax.broadcasted_iota(jnp.int32, (mine.shape[0], 128), 1)
    o_ref[:, 2 * half:] = jnp.where(lane == 0, high, jnp.where(lane == 1, squares - high, 0.0)).astype(jnp.bfloat16)


def hidden_kernel(parts_ref, copies_ref):
    half = copies_ref.shape[2]
    sums = parts_ref[0].astype(jnp.float32)
    for i in range(1, parts_ref.shape[0]):
        sums = sums + parts_ref[i].astype(jnp.float32)
    squares = sums[:, 2 * half:2 * half + 1] + sums[:, 2 * half + 1:2 * half + 2]
    inv_rms = lax.rsqrt(squares / D + eps)
    gate = sums[:, :half] * inv_rms
    up = sums[:, half:2 * half] * inv_rms
    hidden = (gate / (1.0 + jnp.exp(-gate)) * up).astype(jnp.bfloat16)
    for i in range(copies_ref.shape[0]):
        copies_ref[i] = hidden


def down_kernel(mine_ref, theirs_ref, weight_ref, o_ref):
    half = mine_ref.shape[1]
    core = lax.axis_index("core")
    part = matmul(mine_ref[...], weight_ref[0, pl.ds(pl.multiple_of(core * half, half), half), :])
    part = part + matmul(theirs_ref[...], weight_ref[0, pl.ds(pl.multiple_of((1 - core) * half, half), half), :])
    o_ref[...] = part.astype(jnp.bfloat16)


def final_kernel(parts_ref, stream_ref, copies_ref):
    total = parts_ref[0].astype(jnp.float32)
    for i in range(1, parts_ref.shape[0]):
        total = total + parts_ref[i].astype(jnp.float32)
    final = stream_ref[...] + total
    count, slots = copies_ref.shape[0] // 2, copies_ref.shape[1]
    for i in range(count):
        block = final[i * slots:(i + 1) * slots].astype(jnp.bfloat16)
        copies_ref[i] = block
        copies_ref[count + i] = block


def output_kernel(back_ref, o_ref):
    width = back_ref.shape[2]
    chips = back_ref.shape[0] // 4
    half = chips // 2
    side = lax.axis_index("side")
    for chip in range(half):
        for core in range(2):
            at = (2 * chip + core) * width
            o_ref[:, at:at + width] = back_ref[(2 + core) * chips + side * half + chip]


def local(queries, new_entries, cache_keys, cache_values, lengths, residual, norm_gain, out_weight, gate_weight, up_weight, down_weight):
    bf16 = jnp.bfloat16
    rows, pairs, chips = lax.axis_size(ROW), lax.axis_size("rp"), lax.axis_size(CHIPS)
    core = lax.axis_index("core")
    slots, width = queries.shape[0], out_weight.shape[2]
    heads = out_weight.shape[1]
    half = gate_weight.shape[2] // 2
    group = chips * 2 * slots
    total = rows * group
    pair = flip(out_weight, "rl")
    gain = norm_gain[None, :]
    gain_theirs = flip(gain, "core")
    gate_theirs = flip(lax.dynamic_slice_in_dim(gate_weight[0], (1 - core) * half, half, 1), "core")
    up_theirs = flip(lax.dynamic_slice_in_dim(up_weight[0], (1 - core) * half, half, 1), "core")

    gate_mine = lax.dynamic_slice_in_dim(gate_weight[0], core * half, half, 1)
    up_mine = lax.dynamic_slice_in_dim(up_weight[0], core * half, half, 1)
    blocks = attention(queries, new_entries, cache_keys, cache_values, lengths, pairs)
    blocks = [to_ffn(block, k) for k, block in enumerate(blocks)]
    fanned = call(fan_kernel, "fan", jax.ShapeDtypeStruct((chips, pairs * 2 * slots, heads), bf16), in_specs=[WHOLE] * pairs + [HELD, HELD], out_specs=WHOLE)(*blocks, pair, gain_theirs)
    near = exchange(fanned, CHIPS).reshape(chips * pairs * 2 * slots, heads)
    far = flip(near, "core")
    own, *parts = call(project_kernel, "project", [jax.ShapeDtypeStruct((2, group // 2, width), bf16)] * pairs, in_specs=[WHOLE] * 4, out_specs=[WHOLE] * pairs)(near, far, out_weight, pair)
    parts = [own] + [turn(part, k + 1) for k, part in enumerate(parts)]
    parts = [part.reshape(group, width) for part in parts]
    stream, copies = call(stream_kernel, "stream", (jax.ShapeDtypeStruct((group, width), jnp.float32), jax.ShapeDtypeStruct((rows, group, width), bf16)), in_specs=[WHOLE] * (pairs + 2), out_specs=(WHOLE, WHOLE))(
        *parts, residual, gain)
    scaled = exchange(copies, HOME).reshape(total, width)
    scaled_theirs = flip(scaled, "core")
    sent = call(gate_up_kernel, "gate_up", jax.ShapeDtypeStruct((total, 2 * half + 128), bf16), in_specs=[WHOLE] * 8, out_specs=WHOLE)(
        scaled, scaled_theirs, gain, gain_theirs, gate_mine, gate_theirs, up_mine, up_theirs)
    sums = exchange(sent.reshape(chips, group, 2 * half + 128), CHIPS)
    hidden = call(hidden_kernel, "hidden", jax.ShapeDtypeStruct((chips, group, half), bf16), in_specs=[WHOLE], out_specs=WHOLE)(sums)
    hidden = exchange(hidden, CHIPS).reshape(total, half)
    down = call(down_kernel, "down", jax.ShapeDtypeStruct((total, width), bf16), in_specs=[WHOLE] * 3, out_specs=WHOLE)(hidden, flip(hidden, "core"), down_weight)
    downs = exchange(down.reshape(rows, group, width), HOME)
    final = call(final_kernel, "final", jax.ShapeDtypeStruct((4 * chips, slots, width), bf16), in_specs=[WHOLE] * 2, out_specs=WHOLE)(downs, stream)
    back = exchange(final, ("side", "core") + CHIPS)
    return call(output_kernel, "output", jax.ShapeDtypeStruct((slots, width * chips), bf16), in_specs=[WHOLE], out_specs=WHOLE)(back)


def solution(mesh):
    sides, rows, cols = mesh.devices.shape
    inner = Mesh(mesh.devices.reshape(sides, rows // 2, 2, cols // 4, 2, 2), ("side",) + ROW + COL)
    in_specs = (
        P(ROW + COL, None),
        P(ROW + COL, None),
        P("side", ROW + COL, None, None),
        P("side", ROW + COL, None, None),
        P(ROW + COL),
        P(None, COL),
        P(COL),
        P("side", ROW, COL),
        P("side", COL, ROW),
        P("side", COL, ROW),
        P("side", ROW, COL),
    )
    return jax.shard_map(local, mesh=inner, in_specs=in_specs, out_specs=P(ROW + COL, "side"), check_vma=False)
```

```python
import functools
import math
import jax
import jax.numpy as jnp
from jax import lax
from jax.experimental import pallas as pl
from jax.experimental.pallas import tpu as pltpu
from jax.sharding import Mesh, PartitionSpec as P

D = 8192
H = 64
KVH = 8
HD = 128
ORIG = 64
PER = H // KVH

rope_theta = 500000.0
stretch_factor = 8.0
eps = 1e-05

CHIPS = ("x", "yl")
COL = ("x", "yl", "core")
ROW = ("rp", "rl")
HOME = ("rl", "rp")
WHOLE = pl.BlockSpec(memory_space=pltpu.VMEM)
HELD = pl.BlockSpec(memory_space=pl.ANY)
SCALARS = pl.BlockSpec(memory_space=pltpu.SMEM)


def swap_halves(v):
    return jnp.concatenate([v[:, HD // 2:], v[:, : HD // 2]], axis=-1)


def attend_kernel(len_ref, q_ref, new_ref, k_lo_ref, k_hi_ref, v_lo_ref, v_hi_ref, *rest):
    o_refs, (q_all, new_all, s_all, acc, out_all, fine_all, coarse_all, at_all) = rest[:-8], rest[-8:]
    slot = pl.program_id(0)
    slots = q_ref.shape[0]
    length = len_ref[slot]
    half = k_lo_ref.shape[2]
    span = 2 * half

    @pl.when(slot == 0)
    def _():
        for h in range(H):
            q_all[:, h, :] = q_ref[:, h * HD:(h + 1) * HD].astype(jnp.float32)
        for h in range(2 * KVH):
            new_all[:, h, :] = new_ref[:, h * HD:(h + 1) * HD].astype(jnp.float32)

    steps = span // 16
    lane = lax.broadcasted_iota(jnp.int32, (1, HD), 1)
    sign = jnp.where(lane < HD // 2, -1.0, 1.0)

    @pl.when(slot == 0)
    def _():
        pair = jnp.where(lane < HD // 2, lane, lane - HD // 2).astype(jnp.float32)
        positions = jnp.concatenate([jnp.full((8, HD), len_ref[j], jnp.int32) for j in range(slots)], axis=0).astype(jnp.float32)
        stretch = jnp.maximum(stretch_factor * (positions + 1.0) / ORIG - (stretch_factor - 1.0), 1.0)
        log_base = math.log(rope_theta) + HD / (HD - 2.0) * jnp.log(stretch)
        freqs = jnp.exp(-(pair * (2.0 / HD)) * log_base)
        low = lax.broadcasted_iota(jnp.int32, (16, HD), 0).astype(jnp.float32)
        high = lax.broadcasted_iota(jnp.int32, (steps, HD), 0).astype(jnp.float32) * 16.0
        each = [freqs[8 * j:8 * j + 1] for j in range(slots)]
        angles = jnp.concatenate([low * f for f in each] + [high * f for f in each] + [positions * freqs], axis=0)
        cosine, sine = jnp.cos(angles), jnp.sin(angles)
        for j in range(slots):
            fine_all[j, 0] = cosine[16 * j:16 * j + 16]
            fine_all[j, 1] = sine[16 * j:16 * j + 16]
            at = 16 * slots + steps * j
            coarse_all[j, 0] = cosine[at:at + steps]
            coarse_all[j, 1] = sine[at:at + steps]
            at = (16 + steps) * slots + 8 * j
            at_all[j, 0] = cosine[at:at + 8]
            at_all[j, 1] = sine[at:at + 8]

    fine_cos, fine_sin = fine_all[slot, 0], fine_all[slot, 1]
    coarse_cos, coarse_sin = coarse_all[slot, 0], coarse_all[slot, 1]

    def tables(first):
        cos_parts, sin_parts = [], []
        for step in range(first, first + steps // 2):
            cc, cs = coarse_cos[step:step + 1], coarse_sin[step:step + 1]
            cos_parts.append(cc * fine_cos - cs * fine_sin)
            sin_parts.append(cs * fine_cos + cc * fine_sin)
        return jnp.concatenate(cos_parts, axis=0), jnp.concatenate(sin_parts, axis=0)

    cos_new = at_all[slot, 0, :1]
    sin_new = at_all[slot, 1, :1] * sign
    q = q_all[slot]
    q_rot = q * cos_new + swap_halves(q) * sin_new
    q_rot = q_rot.astype(jnp.bfloat16).astype(jnp.float32)
    q_both = jnp.concatenate([q_rot, swap_halves(q_rot) * -sign], axis=-1)
    k_new = new_all[slot, :KVH]
    k_new = k_new * cos_new + swap_halves(k_new) * sin_new
    k_new = k_new.astype(jnp.bfloat16).astype(jnp.float32)
    v_new = new_all[slot, KVH:]
    scale = HD ** (-0.5)

    def score(k_ref, first):
        cos_t, sin_t = tables(first)
        for g in range(KVH):
            kg = k_ref[0, 0, :, g * HD:(g + 1) * HD].astype(jnp.float32)
            kk = jnp.concatenate([(kg * cos_t).astype(jnp.bfloat16), (kg * sin_t).astype(jnp.bfloat16)], axis=-1)
            qg = q_both[g * PER:(g + 1) * PER].astype(jnp.bfloat16)
            s_all[g * PER:(g + 1) * PER, first * 16:first * 16 + half] = lax.dot_general(qg, kk, (((1,), (1,)), ((), ())), preferred_element_type=jnp.float32)

    score(k_lo_ref, 0)

    @pl.when(length > half)
    def _():
        score(k_hi_ref, steps // 2)

    @pl.when(length <= half)
    def _():
        s_all[:, half:] = jnp.zeros((H, half), jnp.float32)

    own, fresh = [], []
    for g in range(KVH):
        own.append(jnp.sum(q_rot[g * PER:(g + 1) * PER] * k_new[g:g + 1], axis=-1, keepdims=True))
        fresh.append(jnp.broadcast_to(v_new[g:g + 1], (PER, HD)))
    own_score = jnp.concatenate(own, axis=0) * scale
    valid = lax.broadcasted_iota(jnp.int32, (H, span), 1) < length
    s = jnp.where(valid, s_all[...] * scale, -1e30)
    top = jnp.maximum(jnp.max(s, axis=-1, keepdims=True), own_score)
    w = jnp.where(valid, jnp.exp(s - top), 0.0)
    own_w = jnp.exp(own_score - top)
    total = jnp.sum(w, axis=-1, keepdims=True) + own_w
    w16 = w.astype(jnp.bfloat16)

    def mix(v_ref, weights):
        parts = []
        for p in range(KVH // 2):
            o = jnp.dot(weights[p * 2 * PER:(p + 1) * 2 * PER], v_ref[0, 0, :, p * 2 * HD:(p + 1) * 2 * HD], preferred_element_type=jnp.float32)
            parts += [o[:PER, :HD], o[PER:, HD:]]
        return jnp.concatenate(parts, axis=0)

    acc[...] = mix(v_lo_ref, w16[:, :half]) + own_w * jnp.concatenate(fresh, axis=0)

    @pl.when(length > half)
    def _():
        acc[...] += mix(v_hi_ref, w16[:, half:])

    out = acc[...] / total
    pairs = len(o_refs)
    per_row = H // (2 * pairs)
    for h in range(H):
        at, q_at = h // per_row, h % per_row
        out_all[at // 2, slot, at % 2:at % 2 + 1, q_at * HD:(q_at + 1) * HD] = out[h:h + 1]

    @pl.when(slot == slots - 1)
    def _():
        for k in range(pairs):
            home = lax.rem(lax.axis_index("rp") + k, pairs)
            o_refs[k][...] = jnp.concatenate([out_all[home, j] for j in range(slots)], axis=0).astype(jnp.bfloat16)


def attention(queries, new_entries, cache_keys, cache_values, lengths, pairs):
    slots = queries.shape[0]
    half = cache_keys.shape[2] // 2
    width = KVH * HD
    low = pl.BlockSpec((1, 1, half, width), lambda s, n: (0, s, 0, 0))

    def last_long(s, n):
        at = 0
        for j in range(1, slots):
            at = jnp.where((s >= j) & (n[j] > half), j, at)
        return (0, at, 1, 0)

    high = pl.BlockSpec((1, 1, half, width), last_long)
    heads = H * HD // (2 * pairs)
    grid_spec = pltpu.PrefetchScalarGridSpec(
        num_scalar_prefetch=1, grid=(slots,),
        in_specs=[pl.BlockSpec((slots, H * HD), lambda s, n: (0, 0)), pl.BlockSpec((slots, 2 * width), lambda s, n: (0, 0)), low, high, low, high],
        out_specs=[pl.BlockSpec((2 * slots, heads), lambda s, n: (0, 0))] * pairs,
        scratch_shapes=[
            pltpu.VMEM((slots, H, HD), jnp.float32), pltpu.VMEM((slots, 2 * KVH, HD), jnp.float32),
            pltpu.VMEM((H, 2 * half), jnp.float32), pltpu.VMEM((H, HD), jnp.float32), pltpu.VMEM((pairs, slots, 2, heads), jnp.float32),
            pltpu.VMEM((slots, 2, 16, HD), jnp.float32), pltpu.VMEM((slots, 2, 2 * half // 16, HD), jnp.float32), pltpu.VMEM((slots, 2, 8, HD), jnp.float32)])
    return pl.pallas_call(
        attend_kernel, grid_spec=grid_spec,
        out_shape=[jax.ShapeDtypeStruct((2 * slots, heads), jnp.bfloat16)] * pairs,
        compiler_params=pltpu.CompilerParams(vmem_limit_bytes=60 << 20), name="attend",
    )(lengths, queries, new_entries, cache_keys, cache_keys, cache_values, cache_values)


def flip(value, axis):
    return lax.ppermute(value, axis, [(0, 1), (1, 0)])


def turn(value, steps):
    count = lax.axis_size("rp")
    return lax.ppermute(value, "rp", [(i, (i + steps) % count) for i in range(count)])


def to_ffn(value, steps):
    count = lax.axis_size("rp")
    return lax.ppermute(value, ("side", "rp"), [(i, count + (i + steps) % count) for i in range(count)])


def exchange(value, axes):
    return lax.all_to_all(value, axes, split_axis=0, concat_axis=0, tiled=True)


def matmul(left, right):
    return jnp.dot(left, right, preferred_element_type=jnp.float32)


def call(kernel, name, out_shape, **options):
    limit = options.pop("limit", 24)
    return pl.pallas_call(kernel, out_shape=out_shape, name=name, compiler_params=pltpu.CompilerParams(vmem_limit_bytes=limit << 20), **options)


def fan_kernel(*refs):
    blocks, o_ref = refs[:-3], refs[-1]
    rows = blocks[0].shape[0]
    for i in range(o_ref.shape[0]):
        for k, block in enumerate(blocks):
            o_ref[i, k * rows:(k + 1) * rows] = block[...]


def project_kernel(near_ref, far_ref, own_ref, pair_a_ref, pair_b_ref, *o_refs):
    core, low = lax.axis_index("core"), lax.axis_index("rl")
    pairs, group = len(o_refs), o_refs[0].shape[1]
    slots = near_ref.shape[0] // (2 * pairs * (group // 4))
    rows = pairs * group
    cut = pair_a_ref.shape[0]
    to = lax.broadcasted_iota(jnp.int32, (rows, 2 * rows), 0)
    source = lax.broadcasted_iota(jnp.int32, (rows, 2 * rows), 1)
    block = (pairs - to // group) % pairs
    first = ((to % group) // slots) * (2 * slots * pairs) + block * (2 * slots) + (to % slots) * 2
    pick_own = (source == first + low).astype(jnp.bfloat16)
    pick_pair = (source == first + 1 - low).astype(jnp.bfloat16)
    for left_ref, place in ((near_ref, core), (far_ref, 1 - core)):
        part = matmul(matmul(pick_own, left_ref[...]).astype(jnp.bfloat16), own_ref[0])
        theirs = matmul(pick_pair, left_ref[...]).astype(jnp.bfloat16)
        part = part + matmul(theirs[:, :cut], pair_a_ref[...]) + matmul(theirs[:, cut:], pair_b_ref[...])
        for k in range(pairs):
            o_refs[k][place] = part[k * group:(k + 1) * group].astype(jnp.bfloat16)


def stream_kernel(*refs):
    parts, (residual_ref, gain_ref, stream_ref, copies_ref) = refs[:-4], refs[-4:]
    group = stream_ref.shape[0]
    chips = group // 8
    row = lax.axis_index("rp") * 2 + lax.axis_index("rl")
    to = lax.broadcasted_iota(jnp.int32, (group, group), 0)
    source = lax.broadcasted_iota(jnp.int32, (group, group), 1)
    order = (source == (to // 4 % chips) * 8 + (to // (4 * chips)) * 4 + to % 4).astype(jnp.bfloat16)
    stream = matmul(order, residual_ref[pl.ds(pl.multiple_of(row * group, group), group), :])
    for part_ref in parts:
        stream = stream + part_ref[...].astype(jnp.float32)
    stream_ref[...] = stream
    scaled = (stream * gain_ref[...].astype(jnp.float32)).astype(jnp.bfloat16)
    for i in range(copies_ref.shape[0]):
        copies_ref[i] = scaled


def gate_up_kernel(x_ref, gain_ref, gate_ref, up_ref, *rest):
    other_ref, o_ref = rest if len(rest) == 2 else (None, rest[0])
    half = gate_ref.shape[1]
    x = x_ref[...]
    one = x.astype(jnp.float32) * (1.0 / gain_ref[...].astype(jnp.float32))
    squares = jnp.sum(one * one, axis=1, keepdims=True)
    gate, up = matmul(x, gate_ref[...]), matmul(x, up_ref[...])
    lane = lax.broadcasted_iota(jnp.int32, (x.shape[0], 128), 1)
    if other_ref is not None:
        gate = gate + other_ref[:, :half]
        up = up + other_ref[:, half:2 * half]
        squares = squares + other_ref[:, 2 * half:]
        high = squares.astype(jnp.bfloat16).astype(jnp.float32)
        squares = jnp.where(lane == 0, high, jnp.where(lane == 1, squares - high, 0.0))
    o_ref[:, :half] = gate.astype(o_ref.dtype)
    o_ref[:, half:2 * half] = up.astype(o_ref.dtype)
    o_ref[:, 2 * half:] = jnp.broadcast_to(squares, lane.shape).astype(o_ref.dtype)


def hidden_kernel(parts_ref, copies_ref):
    half = copies_ref.shape[2]
    sums = parts_ref[0].astype(jnp.float32)
    for i in range(1, parts_ref.shape[0]):
        sums = sums + parts_ref[i].astype(jnp.float32)
    squares = sums[:, 2 * half:2 * half + 1] + sums[:, 2 * half + 1:2 * half + 2]
    inv_rms = lax.rsqrt(squares / D + eps)
    gate = sums[:, :half] * inv_rms
    up = sums[:, half:2 * half] * inv_rms
    hidden = (gate / (1.0 + jnp.exp(-gate)) * up).astype(jnp.bfloat16)
    for i in range(copies_ref.shape[0]):
        copies_ref[i] = hidden


def down_kernel(x_ref, weight_ref, *rest):
    other_ref, o_ref = rest if len(rest) == 2 else (None, rest[0])
    half = x_ref.shape[1]
    core = lax.axis_index("core")
    at = core if other_ref is None else 1 - core
    part = matmul(x_ref[...], weight_ref[0, pl.ds(pl.multiple_of(at * half, half), half), :])
    if other_ref is not None:
        part = part + other_ref[...]
    o_ref[...] = part.astype(o_ref.dtype)


def final_kernel(parts_ref, stream_ref, copies_ref):
    total = parts_ref[0].astype(jnp.float32)
    for i in range(1, parts_ref.shape[0]):
        total = total + parts_ref[i].astype(jnp.float32)
    final = stream_ref[...] + total
    count, slots = copies_ref.shape[0] // 2, copies_ref.shape[1]
    for i in range(count):
        block = final[i * slots:(i + 1) * slots].astype(jnp.bfloat16)
        copies_ref[i] = block
        copies_ref[count + i] = block


def output_kernel(back_ref, o_ref):
    width = back_ref.shape[2]
    chips = back_ref.shape[0] // 4
    half = chips // 2
    side = lax.axis_index("side")
    for chip in range(half):
        for core in range(2):
            at = (2 * chip + core) * width
            o_ref[:, at:at + width] = back_ref[(2 + core) * chips + side * half + chip]


def local(queries, new_entries, cache_keys, cache_values, lengths, residual, norm_gain, out_weight, gate_weight, up_weight, down_weight):
    bf16 = jnp.bfloat16
    rows, pairs, chips = lax.axis_size(ROW), lax.axis_size("rp"), lax.axis_size(CHIPS)
    core = lax.axis_index("core")
    slots, width = queries.shape[0], out_weight.shape[2]
    heads = out_weight.shape[1]
    half = gate_weight.shape[2] // 2
    group = chips * 2 * slots
    total = rows * group
    cut = heads // 16 * 7
    pair_a = flip(out_weight[0, :cut], "rl")
    pair_b = flip(out_weight[0, cut:], "rl")
    gain = norm_gain[None, :]
    gain_theirs = flip(norm_gain, "core")
    gate_theirs = flip(lax.dynamic_slice_in_dim(gate_weight[0], (1 - core) * half, half, 1), "core")
    up_theirs = flip(lax.dynamic_slice_in_dim(up_weight[0], (1 - core) * half, half, 1), "core")

    gate_mine = lax.dynamic_slice_in_dim(gate_weight[0], core * half, half, 1)
    up_mine = lax.dynamic_slice_in_dim(up_weight[0], core * half, half, 1)
    blocks = attention(queries, new_entries, cache_keys, cache_values, lengths, pairs)
    blocks = [to_ffn(block, k) for k, block in enumerate(blocks)]
    fanned = call(fan_kernel, "fan", jax.ShapeDtypeStruct((chips, pairs * 2 * slots, heads), bf16), in_specs=[WHOLE] * pairs + [HELD, HELD], out_specs=WHOLE)(*blocks, pair_a, gain_theirs)
    near = exchange(fanned, CHIPS).reshape(chips * pairs * 2 * slots, heads)
    far = flip(near, "core")
    own, *parts = call(project_kernel, "project", [jax.ShapeDtypeStruct((2, group // 2, width), bf16)] * pairs, in_specs=[WHOLE] * 5, out_specs=[WHOLE] * pairs)(near, far, out_weight, pair_a, pair_b)
    parts = [own] + [turn(part, k + 1) for k, part in enumerate(parts)]
    parts = [part.reshape(group, width) for part in parts]
    stream, copies = call(stream_kernel, "stream", (jax.ShapeDtypeStruct((group, width), jnp.float32), jax.ShapeDtypeStruct((rows, group, width), bf16)), in_specs=[WHOLE] * (pairs + 2), out_specs=(WHOLE, WHOLE))(
        *parts, residual, gain)
    scaled = exchange(copies, HOME).reshape(total, width)
    scaled_theirs = flip(scaled, "core")
    wide = 2 * half + 128
    own = call(gate_up_kernel, "gate_up_own", jax.ShapeDtypeStruct((total, wide), jnp.float32), in_specs=[WHOLE] * 4, out_specs=WHOLE)(scaled, gain, gate_mine, up_mine)
    sent = call(gate_up_kernel, "gate_up", jax.ShapeDtypeStruct((total, wide), bf16), in_specs=[WHOLE] * 5, out_specs=WHOLE)(
        scaled_theirs, gain_theirs[None, :], gate_theirs, up_theirs, own)
    sums = exchange(sent.reshape(chips, group, 2 * half + 128), CHIPS)
    hidden = call(hidden_kernel, "hidden", jax.ShapeDtypeStruct((chips, group, half), bf16), in_specs=[WHOLE], out_specs=WHOLE)(sums)
    hidden = exchange(hidden, CHIPS).reshape(total, half)
    hidden_theirs = flip(hidden, "core")
    own = call(down_kernel, "down_own", jax.ShapeDtypeStruct((total, width), jnp.float32), in_specs=[WHOLE] * 2, out_specs=WHOLE)(hidden, down_weight)
    down = call(down_kernel, "down", jax.ShapeDtypeStruct((total, width), bf16), in_specs=[WHOLE] * 3, out_specs=WHOLE)(hidden_theirs, down_weight, own)
    downs = exchange(down.reshape(rows, group, width), HOME)
    final = call(final_kernel, "final", jax.ShapeDtypeStruct((4 * chips, slots, width), bf16), in_specs=[WHOLE] * 2, out_specs=WHOLE)(downs, stream)
    back = exchange(final, ("side", "core") + CHIPS)
    return call(output_kernel, "output", jax.ShapeDtypeStruct((slots, width * chips), bf16), in_specs=[WHOLE], out_specs=WHOLE)(back)


def solution(mesh):
    sides, rows, cols = mesh.devices.shape
    inner = Mesh(mesh.devices.reshape(sides, rows // 2, 2, cols // 4, 2, 2), ("side",) + ROW + COL)
    in_specs = (
        P(ROW + COL, None),
        P(ROW + COL, None),
        P("side", ROW + COL, None, None),
        P("side", ROW + COL, None, None),
        P(ROW + COL),
        P(None, COL),
        P(COL),
        P("side", ROW, COL),
        P("side", COL, ROW),
        P("side", COL, ROW),
        P("side", ROW, COL),
    )
    return jax.shard_map(local, mesh=inner, in_specs=in_specs, out_specs=P(ROW + COL, "side"), check_vma=False)
```

```python
import functools
import math
import jax
import jax.numpy as jnp
from jax import lax
from jax.experimental import pallas as pl
from jax.experimental.pallas import tpu as pltpu
from jax.sharding import Mesh, PartitionSpec as P

D = 8192
H = 64
KVH = 8
HD = 128
ORIG = 64
PER = H // KVH

rope_theta = 500000.0
stretch_factor = 8.0
eps = 1e-05

CHIPS = ("x", "yl")
COL = ("x", "yl", "core")
ROW = ("rp", "rl")
HOME = ("rl", "rp")
WHOLE = pl.BlockSpec(memory_space=pltpu.VMEM)
HELD = pl.BlockSpec(memory_space=pl.ANY)
SCALARS = pl.BlockSpec(memory_space=pltpu.SMEM)


def swap_halves(v):
    return jnp.concatenate([v[:, HD // 2:], v[:, : HD // 2]], axis=-1)


def attend_kernel(len_ref, q_ref, new_ref, k_lo_ref, k_hi_ref, v_lo_ref, v_hi_ref, *rest):
    o_refs, (q_all, new_all, s_all, acc, out_all, fine_all, coarse_all, at_all) = rest[:-8], rest[-8:]
    slot = pl.program_id(0)
    slots = q_ref.shape[0]
    length = len_ref[slot]
    half = k_lo_ref.shape[2]
    span = 2 * half

    @pl.when(slot == 0)
    def _():
        for h in range(H):
            q_all[:, h, :] = q_ref[:, h * HD:(h + 1) * HD].astype(jnp.float32)
        for h in range(2 * KVH):
            new_all[:, h, :] = new_ref[:, h * HD:(h + 1) * HD].astype(jnp.float32)

    steps = span // 16
    lane = lax.broadcasted_iota(jnp.int32, (1, HD), 1)
    sign = jnp.where(lane < HD // 2, -1.0, 1.0)

    @pl.when(slot == 0)
    def _():
        pair = jnp.where(lane < HD // 2, lane, lane - HD // 2).astype(jnp.float32)
        positions = jnp.concatenate([jnp.full((8, HD), len_ref[j], jnp.int32) for j in range(slots)], axis=0).astype(jnp.float32)
        stretch = jnp.maximum(stretch_factor * (positions + 1.0) / ORIG - (stretch_factor - 1.0), 1.0)
        log_base = math.log(rope_theta) + HD / (HD - 2.0) * jnp.log(stretch)
        freqs = jnp.exp(-(pair * (2.0 / HD)) * log_base)
        low = lax.broadcasted_iota(jnp.int32, (16, HD), 0).astype(jnp.float32)
        high = lax.broadcasted_iota(jnp.int32, (steps, HD), 0).astype(jnp.float32) * 16.0
        each = [freqs[8 * j:8 * j + 1] for j in range(slots)]
        angles = jnp.concatenate([low * f for f in each] + [high * f for f in each] + [positions * freqs], axis=0)
        cosine, sine = jnp.cos(angles), jnp.sin(angles)
        for j in range(slots):
            fine_all[j, 0] = cosine[16 * j:16 * j + 16]
            fine_all[j, 1] = sine[16 * j:16 * j + 16]
            at = 16 * slots + steps * j
            coarse_all[j, 0] = cosine[at:at + steps]
            coarse_all[j, 1] = sine[at:at + steps]
            at = (16 + steps) * slots + 8 * j
            at_all[j, 0] = cosine[at:at + 8]
            at_all[j, 1] = sine[at:at + 8]

    fine_cos, fine_sin = fine_all[slot, 0], fine_all[slot, 1]
    coarse_cos, coarse_sin = coarse_all[slot, 0], coarse_all[slot, 1]

    def tables(first):
        cos_parts, sin_parts = [], []
        for step in range(first, first + steps // 2):
            cc, cs = coarse_cos[step:step + 1], coarse_sin[step:step + 1]
            cos_parts.append(cc * fine_cos - cs * fine_sin)
            sin_parts.append(cs * fine_cos + cc * fine_sin)
        return jnp.concatenate(cos_parts, axis=0), jnp.concatenate(sin_parts, axis=0)

    cos_new = at_all[slot, 0, :1]
    sin_new = at_all[slot, 1, :1] * sign
    q = q_all[slot]
    q_rot = q * cos_new + swap_halves(q) * sin_new
    q_rot = q_rot.astype(jnp.bfloat16).astype(jnp.float32)
    q_both = jnp.concatenate([q_rot, swap_halves(q_rot) * -sign], axis=-1)
    k_new = new_all[slot, :KVH]
    k_new = k_new * cos_new + swap_halves(k_new) * sin_new
    k_new = k_new.astype(jnp.bfloat16).astype(jnp.float32)
    v_new = new_all[slot, KVH:]
    scale = HD ** (-0.5)

    def score(k_ref, first):
        cos_t, sin_t = tables(first)
        for g in range(KVH):
            kg = k_ref[0, 0, :, g * HD:(g + 1) * HD].astype(jnp.float32)
            kk = jnp.concatenate([(kg * cos_t).astype(jnp.bfloat16), (kg * sin_t).astype(jnp.bfloat16)], axis=-1)
            qg = q_both[g * PER:(g + 1) * PER].astype(jnp.bfloat16)
            s_all[g * PER:(g + 1) * PER, first * 16:first * 16 + half] = lax.dot_general(qg, kk, (((1,), (1,)), ((), ())), preferred_element_type=jnp.float32)

    score(k_lo_ref, 0)

    @pl.when(length > half)
    def _():
        score(k_hi_ref, steps // 2)

    @pl.when(length <= half)
    def _():
        s_all[:, half:] = jnp.zeros((H, half), jnp.float32)

    own, fresh = [], []
    for g in range(KVH):
        own.append(jnp.sum(q_rot[g * PER:(g + 1) * PER] * k_new[g:g + 1], axis=-1, keepdims=True))
        fresh.append(jnp.broadcast_to(v_new[g:g + 1], (PER, HD)))
    own_score = jnp.concatenate(own, axis=0) * scale
    valid = lax.broadcasted_iota(jnp.int32, (H, span), 1) < length
    s = jnp.where(valid, s_all[...] * scale, -1e30)
    top = jnp.maximum(jnp.max(s, axis=-1, keepdims=True), own_score)
    w = jnp.where(valid, jnp.exp(s - top), 0.0)
    own_w = jnp.exp(own_score - top)
    total = jnp.sum(w, axis=-1, keepdims=True) + own_w
    w16 = w.astype(jnp.bfloat16)

    def mix(v_ref, weights):
        parts = []
        for p in range(KVH // 2):
            o = jnp.dot(weights[p * 2 * PER:(p + 1) * 2 * PER], v_ref[0, 0, :, p * 2 * HD:(p + 1) * 2 * HD], preferred_element_type=jnp.float32)
            parts += [o[:PER, :HD], o[PER:, HD:]]
        return jnp.concatenate(parts, axis=0)

    acc[...] = mix(v_lo_ref, w16[:, :half]) + own_w * jnp.concatenate(fresh, axis=0)

    @pl.when(length > half)
    def _():
        acc[...] += mix(v_hi_ref, w16[:, half:])

    out = acc[...] / total
    pairs = len(o_refs)
    per_row = H // (2 * pairs)
    for h in range(H):
        at, q_at = h // per_row, h % per_row
        out_all[at // 2, slot, at % 2:at % 2 + 1, q_at * HD:(q_at + 1) * HD] = out[h:h + 1]

    @pl.when(slot == slots - 1)
    def _():
        for k in range(pairs):
            home = lax.rem(lax.axis_index("rp") + k, pairs)
            o_refs[k][...] = jnp.concatenate([out_all[home, j] for j in range(slots)], axis=0).astype(jnp.bfloat16)


def attention(queries, new_entries, cache_keys, cache_values, lengths, pairs):
    slots = queries.shape[0]
    half = cache_keys.shape[2] // 2
    width = KVH * HD
    low = pl.BlockSpec((1, 1, half, width), lambda s, n: (0, s, 0, 0))

    def last_long(s, n):
        at = 0
        for j in range(1, slots):
            at = jnp.where((s >= j) & (n[j] > half), j, at)
        return (0, at, 1, 0)

    high = pl.BlockSpec((1, 1, half, width), last_long)
    heads = H * HD // (2 * pairs)
    grid_spec = pltpu.PrefetchScalarGridSpec(
        num_scalar_prefetch=1, grid=(slots,),
        in_specs=[pl.BlockSpec((slots, H * HD), lambda s, n: (0, 0)), pl.BlockSpec((slots, 2 * width), lambda s, n: (0, 0)), low, high, low, high],
        out_specs=[pl.BlockSpec((2 * slots, heads), lambda s, n: (0, 0))] * pairs,
        scratch_shapes=[
            pltpu.VMEM((slots, H, HD), jnp.float32), pltpu.VMEM((slots, 2 * KVH, HD), jnp.float32),
            pltpu.VMEM((H, 2 * half), jnp.float32), pltpu.VMEM((H, HD), jnp.float32), pltpu.VMEM((pairs, slots, 2, heads), jnp.float32),
            pltpu.VMEM((slots, 2, 16, HD), jnp.float32), pltpu.VMEM((slots, 2, 2 * half // 16, HD), jnp.float32), pltpu.VMEM((slots, 2, 8, HD), jnp.float32)])
    return pl.pallas_call(
        attend_kernel, grid_spec=grid_spec,
        out_shape=[jax.ShapeDtypeStruct((2 * slots, heads), jnp.bfloat16)] * pairs,
        compiler_params=pltpu.CompilerParams(vmem_limit_bytes=60 << 20), name="attend",
    )(lengths, queries, new_entries, cache_keys, cache_keys, cache_values, cache_values)


def flip(value, axis):
    return lax.ppermute(value, axis, [(0, 1), (1, 0)])


def turn(value, steps):
    count = lax.axis_size("rp")
    return lax.ppermute(value, "rp", [(i, (i + steps) % count) for i in range(count)])


def to_ffn(value, steps):
    count = lax.axis_size("rp")
    return lax.ppermute(value, ("side", "rp"), [(i, count + (i + steps) % count) for i in range(count)])


def exchange(value, axes):
    return lax.all_to_all(value, axes, split_axis=0, concat_axis=0, tiled=True)


def matmul(left, right):
    return jnp.dot(left, right, preferred_element_type=jnp.float32)


def call(kernel, name, out_shape, **options):
    limit = options.pop("limit", 24)
    return pl.pallas_call(kernel, out_shape=out_shape, name=name, compiler_params=pltpu.CompilerParams(vmem_limit_bytes=limit << 20), **options)


def fan_kernel(*refs):
    blocks, o_ref = refs[:-3], refs[-1]
    rows = blocks[0].shape[0]
    for i in range(o_ref.shape[0]):
        for k, block in enumerate(blocks):
            o_ref[i, k * rows:(k + 1) * rows] = block[...]


def project_kernel(near_ref, far_ref, own_ref, pair_a_ref, pair_b_ref, *o_refs):
    core, low = lax.axis_index("core"), lax.axis_index("rl")
    pairs, group = len(o_refs), o_refs[0].shape[1]
    slots = near_ref.shape[0] // (2 * pairs * (group // 4))
    rows = pairs * group
    cut = pair_a_ref.shape[0]
    to = lax.broadcasted_iota(jnp.int32, (rows, 2 * rows), 0)
    source = lax.broadcasted_iota(jnp.int32, (rows, 2 * rows), 1)
    block = (pairs - to // group) % pairs
    first = ((to % group) // slots) * (2 * slots * pairs) + block * (2 * slots) + (to % slots) * 2
    pick_own = (source == first + low).astype(jnp.bfloat16)
    pick_pair = (source == first + 1 - low).astype(jnp.bfloat16)
    for left_ref, place in ((near_ref, core), (far_ref, 1 - core)):
        part = matmul(matmul(pick_own, left_ref[...]).astype(jnp.bfloat16), own_ref[0])
        theirs = matmul(pick_pair, left_ref[...]).astype(jnp.bfloat16)
        part = part + matmul(theirs[:, :cut], pair_a_ref[...]) + matmul(theirs[:, cut:], pair_b_ref[...])
        for k in range(pairs):
            o_refs[k][place] = part[k * group:(k + 1) * group].astype(jnp.bfloat16)


def stream_kernel(*refs):
    parts, (residual_ref, gain_ref, stream_ref, copies_ref) = refs[:-4], refs[-4:]
    group = stream_ref.shape[0]
    chips = group // 8
    row = lax.axis_index("rp") * 2 + lax.axis_index("rl")
    to = lax.broadcasted_iota(jnp.int32, (group, group), 0)
    source = lax.broadcasted_iota(jnp.int32, (group, group), 1)
    order = (source == (to // 4 % chips) * 8 + (to // (4 * chips)) * 4 + to % 4).astype(jnp.bfloat16)
    stream = matmul(order, residual_ref[pl.ds(pl.multiple_of(row * group, group), group), :])
    for part_ref in parts:
        stream = stream + part_ref[...].astype(jnp.float32)
    stream_ref[...] = stream
    scaled = (stream * gain_ref[...].astype(jnp.float32)).astype(jnp.bfloat16)
    for i in range(copies_ref.shape[0]):
        copies_ref[i] = scaled


def gate_up_kernel(x_ref, gain_ref, gate_ref, up_ref, *rest):
    other_ref, o_ref = rest if len(rest) == 2 else (None, rest[0])
    half = gate_ref.shape[1]
    x = x_ref[...]
    one = x.astype(jnp.float32) * (1.0 / gain_ref[...].astype(jnp.float32))
    squares = jnp.sum(one * one, axis=1, keepdims=True)
    gate, up = matmul(x, gate_ref[...]), matmul(x, up_ref[...])
    lane = lax.broadcasted_iota(jnp.int32, (x.shape[0], 128), 1)
    if other_ref is not None:
        gate = gate + other_ref[:, :half]
        up = up + other_ref[:, half:2 * half]
        squares = squares + other_ref[:, 2 * half:]
        high = squares.astype(jnp.bfloat16).astype(jnp.float32)
        squares = jnp.where(lane == 0, high, jnp.where(lane == 1, squares - high, 0.0))
    o_ref[:, :half] = gate.astype(o_ref.dtype)
    o_ref[:, half:2 * half] = up.astype(o_ref.dtype)
    o_ref[:, 2 * half:] = jnp.broadcast_to(squares, lane.shape).astype(o_ref.dtype)


def hidden_kernel(parts_ref, copies_ref):
    half = copies_ref.shape[2]
    sums = parts_ref[0].astype(jnp.float32)
    for i in range(1, parts_ref.shape[0]):
        sums = sums + parts_ref[i].astype(jnp.float32)
    squares = sums[:, 2 * half:2 * half + 1] + sums[:, 2 * half + 1:2 * half + 2]
    inv_rms = lax.rsqrt(squares / D + eps)
    gate = sums[:, :half] * inv_rms
    up = sums[:, half:2 * half] * inv_rms
    hidden = (gate / (1.0 + jnp.exp(-gate)) * up).astype(jnp.bfloat16)
    for i in range(copies_ref.shape[0]):
        copies_ref[i] = hidden


def down_kernel(x_ref, weight_ref, *rest):
    other_ref, o_ref = rest if len(rest) == 2 else (None, rest[0])
    half = x_ref.shape[1]
    core = lax.axis_index("core")
    at = core if other_ref is None else 1 - core
    part = matmul(x_ref[...], weight_ref[0, pl.ds(pl.multiple_of(at * half, half), half), :])
    if other_ref is not None:
        part = part + other_ref[...]
    o_ref[...] = part.astype(o_ref.dtype)


def final_kernel(parts_ref, stream_ref, copies_ref):
    total = parts_ref[0].astype(jnp.float32)
    for i in range(1, parts_ref.shape[0]):
        total = total + parts_ref[i].astype(jnp.float32)
    final = stream_ref[...] + total
    count, slots = copies_ref.shape[0] // 2, copies_ref.shape[1]
    for i in range(count):
        block = final[i * slots:(i + 1) * slots].astype(jnp.bfloat16)
        copies_ref[i] = block
        copies_ref[count + i] = block


def output_kernel(back_ref, o_ref):
    width = back_ref.shape[2]
    chips = back_ref.shape[0] // 4
    half = chips // 2
    side = lax.axis_index("side")
    for chip in range(half):
        for core in range(2):
            at = (2 * chip + core) * width
            o_ref[:, at:at + width] = back_ref[(2 + core) * chips + side * half + chip]


def local(queries, new_entries, cache_keys, cache_values, lengths, residual, norm_gain, out_weight, gate_weight, up_weight, down_weight):
    bf16 = jnp.bfloat16
    rows, pairs, chips = lax.axis_size(ROW), lax.axis_size("rp"), lax.axis_size(CHIPS)
    core = lax.axis_index("core")
    slots, width = queries.shape[0], out_weight.shape[2]
    heads = out_weight.shape[1]
    half = gate_weight.shape[2] // 2
    group = chips * 2 * slots
    total = rows * group
    cut = heads // 16 * 11
    pair_a = flip(out_weight[0, :cut], "rl")
    pair_b = flip(out_weight[0, cut:], "rl")
    gain = norm_gain[None, :]
    gain_theirs = flip(norm_gain, "core")
    gate_theirs = flip(lax.dynamic_slice_in_dim(gate_weight[0], (1 - core) * half, half, 1), "core")
    up_theirs = flip(lax.dynamic_slice_in_dim(up_weight[0], (1 - core) * half, half, 1), "core")

    gate_mine = lax.dynamic_slice_in_dim(gate_weight[0], core * half, half, 1)
    up_mine = lax.dynamic_slice_in_dim(up_weight[0], core * half, half, 1)
    blocks = attention(queries, new_entries, cache_keys, cache_values, lengths, pairs)
    blocks = [to_ffn(block, k) for k, block in enumerate(blocks)]
    fanned = call(fan_kernel, "fan", jax.ShapeDtypeStruct((chips, pairs * 2 * slots, heads), bf16), in_specs=[WHOLE] * pairs + [HELD, HELD], out_specs=WHOLE)(*blocks, pair_a, gain_theirs)
    near = exchange(fanned, CHIPS).reshape(chips * pairs * 2 * slots, heads)
    far = flip(near, "core")
    own, *parts = call(project_kernel, "project", [jax.ShapeDtypeStruct((2, group // 2, width), bf16)] * pairs, in_specs=[WHOLE] * 5, out_specs=[WHOLE] * pairs)(near, far, out_weight, pair_a, pair_b)
    parts = [own] + [turn(part, k + 1) for k, part in enumerate(parts)]
    parts = [part.reshape(group, width) for part in parts]
    stream, copies = call(stream_kernel, "stream", (jax.ShapeDtypeStruct((group, width), jnp.float32), jax.ShapeDtypeStruct((rows, group, width), bf16)), in_specs=[WHOLE] * (pairs + 2), out_specs=(WHOLE, WHOLE))(
        *parts, residual, gain)
    scaled = exchange(copies, HOME).reshape(total, width)
    scaled_theirs = flip(scaled, "core")
    wide = 2 * half + 128
    own = call(gate_up_kernel, "gate_up_own", jax.ShapeDtypeStruct((total, wide), jnp.float32), in_specs=[WHOLE] * 4, out_specs=WHOLE)(scaled, gain, gate_mine, up_mine)
    sent = call(gate_up_kernel, "gate_up", jax.ShapeDtypeStruct((total, wide), bf16), in_specs=[WHOLE] * 5, out_specs=WHOLE)(
        scaled_theirs, gain_theirs[None, :], gate_theirs, up_theirs, own)
    sums = exchange(sent.reshape(chips, group, 2 * half + 128), CHIPS)
    hidden = call(hidden_kernel, "hidden", jax.ShapeDtypeStruct((chips, group, half), bf16), in_specs=[WHOLE], out_specs=WHOLE)(sums)
    hidden = exchange(hidden, CHIPS).reshape(total, half)
    hidden_theirs = flip(hidden, "core")
    own = call(down_kernel, "down_own", jax.ShapeDtypeStruct((total, width), jnp.float32), in_specs=[WHOLE] * 2, out_specs=WHOLE)(hidden, down_weight)
    down = call(down_kernel, "down", jax.ShapeDtypeStruct((total, width), bf16), in_specs=[WHOLE] * 3, out_specs=WHOLE)(hidden_theirs, down_weight, own)
    downs = exchange(down.reshape(rows, group, width), HOME)
    final = call(final_kernel, "final", jax.ShapeDtypeStruct((4 * chips, slots, width), bf16), in_specs=[WHOLE] * 2, out_specs=WHOLE)(downs, stream)
    back = exchange(final, ("side", "core") + CHIPS)
    return call(output_kernel, "output", jax.ShapeDtypeStruct((slots, width * chips), bf16), in_specs=[WHOLE], out_specs=WHOLE)(back)


def solution(mesh):
    sides, rows, cols = mesh.devices.shape
    inner = Mesh(mesh.devices.reshape(sides, rows // 2, 2, cols // 4, 2, 2), ("side",) + ROW + COL)
    in_specs = (
        P(ROW + COL, None),
        P(ROW + COL, None),
        P("side", ROW + COL, None, None),
        P("side", ROW + COL, None, None),
        P(ROW + COL),
        P(None, COL),
        P(COL),
        P("side", ROW, COL),
        P("side", COL, ROW),
        P("side", COL, ROW),
        P("side", ROW, COL),
    )
    return jax.shard_map(local, mesh=inner, in_specs=in_specs, out_specs=P(ROW + COL, "side"), check_vma=False)
```

```python
import functools
import math
import jax
import jax.numpy as jnp
from jax import lax
from jax.experimental import pallas as pl
from jax.experimental.pallas import tpu as pltpu
from jax.sharding import Mesh, PartitionSpec as P

D = 8192
H = 64
KVH = 8
HD = 128
ORIG = 64
PER = H // KVH

rope_theta = 500000.0
stretch_factor = 8.0
eps = 1e-05

CHIPS = ("x", "yl")
COL = ("x", "yl", "core")
ROW = ("rp", "rl")
HOME = ("rl", "rp")
WHOLE = pl.BlockSpec(memory_space=pltpu.VMEM)
HELD = pl.BlockSpec(memory_space=pl.ANY)
SCALARS = pl.BlockSpec(memory_space=pltpu.SMEM)


def swap_halves(v):
    return jnp.concatenate([v[:, HD // 2:], v[:, : HD // 2]], axis=-1)


def attend_kernel(len_ref, q_ref, new_ref, k_lo_ref, k_hi_ref, v_lo_ref, v_hi_ref, *rest):
    o_refs, (q_all, new_all, s_all, acc, out_all, fine_all, coarse_all, at_all) = rest[:-8], rest[-8:]
    slot = pl.program_id(0)
    slots = q_ref.shape[0]
    length = len_ref[slot]
    half = k_lo_ref.shape[2]
    span = 2 * half

    @pl.when(slot == 0)
    def _():
        for h in range(H):
            q_all[:, h, :] = q_ref[:, h * HD:(h + 1) * HD].astype(jnp.float32)
        for h in range(2 * KVH):
            new_all[:, h, :] = new_ref[:, h * HD:(h + 1) * HD].astype(jnp.float32)

    steps = span // 16
    lane = lax.broadcasted_iota(jnp.int32, (1, HD), 1)
    sign = jnp.where(lane < HD // 2, -1.0, 1.0)

    @pl.when(slot == 0)
    def _():
        pair = jnp.where(lane < HD // 2, lane, lane - HD // 2).astype(jnp.float32)
        positions = jnp.concatenate([jnp.full((8, HD), len_ref[j], jnp.int32) for j in range(slots)], axis=0).astype(jnp.float32)
        stretch = jnp.maximum(stretch_factor * (positions + 1.0) / ORIG - (stretch_factor - 1.0), 1.0)
        log_base = math.log(rope_theta) + HD / (HD - 2.0) * jnp.log(stretch)
        freqs = jnp.exp(-(pair * (2.0 / HD)) * log_base)
        low = lax.broadcasted_iota(jnp.int32, (16, HD), 0).astype(jnp.float32)
        high = lax.broadcasted_iota(jnp.int32, (steps, HD), 0).astype(jnp.float32) * 16.0
        each = [freqs[8 * j:8 * j + 1] for j in range(slots)]
        angles = jnp.concatenate([low * f for f in each] + [high * f for f in each] + [positions * freqs], axis=0)
        cosine, sine = jnp.cos(angles), jnp.sin(angles)
        for j in range(slots):
            fine_all[j, 0] = cosine[16 * j:16 * j + 16]
            fine_all[j, 1] = sine[16 * j:16 * j + 16]
            at = 16 * slots + steps * j
            coarse_all[j, 0] = cosine[at:at + steps]
            coarse_all[j, 1] = sine[at:at + steps]
            at = (16 + steps) * slots + 8 * j
            at_all[j, 0] = cosine[at:at + 8]
            at_all[j, 1] = sine[at:at + 8]

    fine_cos, fine_sin = fine_all[slot, 0], fine_all[slot, 1]
    coarse_cos, coarse_sin = coarse_all[slot, 0], coarse_all[slot, 1]

    def tables(first):
        cos_parts, sin_parts = [], []
        for step in range(first, first + steps // 2):
            cc, cs = coarse_cos[step:step + 1], coarse_sin[step:step + 1]
            cos_parts.append(cc * fine_cos - cs * fine_sin)
            sin_parts.append(cs * fine_cos + cc * fine_sin)
        return jnp.concatenate(cos_parts, axis=0), jnp.concatenate(sin_parts, axis=0)

    cos_new = at_all[slot, 0, :1]
    sin_new = at_all[slot, 1, :1] * sign
    q = q_all[slot]
    q_rot = q * cos_new + swap_halves(q) * sin_new
    q_rot = q_rot.astype(jnp.bfloat16).astype(jnp.float32)
    q_both = jnp.concatenate([q_rot, swap_halves(q_rot) * -sign], axis=-1)
    k_new = new_all[slot, :KVH]
    k_new = k_new * cos_new + swap_halves(k_new) * sin_new
    k_new = k_new.astype(jnp.bfloat16).astype(jnp.float32)
    v_new = new_all[slot, KVH:]
    scale = HD ** (-0.5)

    def score(k_ref, first):
        cos_t, sin_t = tables(first)
        for g in range(KVH):
            kg = k_ref[0, 0, :, g * HD:(g + 1) * HD].astype(jnp.float32)
            kk = jnp.concatenate([(kg * cos_t).astype(jnp.bfloat16), (kg * sin_t).astype(jnp.bfloat16)], axis=-1)
            qg = q_both[g * PER:(g + 1) * PER].astype(jnp.bfloat16)
            s_all[g * PER:(g + 1) * PER, first * 16:first * 16 + half] = lax.dot_general(qg, kk, (((1,), (1,)), ((), ())), preferred_element_type=jnp.float32)

    score(k_lo_ref, 0)

    @pl.when(length > half)
    def _():
        score(k_hi_ref, steps // 2)

    @pl.when(length <= half)
    def _():
        s_all[:, half:] = jnp.zeros((H, half), jnp.float32)

    own, fresh = [], []
    for g in range(KVH):
        own.append(jnp.sum(q_rot[g * PER:(g + 1) * PER] * k_new[g:g + 1], axis=-1, keepdims=True))
        fresh.append(jnp.broadcast_to(v_new[g:g + 1], (PER, HD)))
    own_score = jnp.concatenate(own, axis=0) * scale
    valid = lax.broadcasted_iota(jnp.int32, (H, span), 1) < length
    s = jnp.where(valid, s_all[...] * scale, -1e30)
    top = jnp.maximum(jnp.max(s, axis=-1, keepdims=True), own_score)
    w = jnp.where(valid, jnp.exp(s - top), 0.0)
    own_w = jnp.exp(own_score - top)
    total = jnp.sum(w, axis=-1, keepdims=True) + own_w
    w16 = w.astype(jnp.bfloat16)

    def mix(v_ref, weights):
        parts = []
        for p in range(KVH // 2):
            o = jnp.dot(weights[p * 2 * PER:(p + 1) * 2 * PER], v_ref[0, 0, :, p * 2 * HD:(p + 1) * 2 * HD], preferred_element_type=jnp.float32)
            parts += [o[:PER, :HD], o[PER:, HD:]]
        return jnp.concatenate(parts, axis=0)

    acc[...] = mix(v_lo_ref, w16[:, :half]) + own_w * jnp.concatenate(fresh, axis=0)

    @pl.when(length > half)
    def _():
        acc[...] += mix(v_hi_ref, w16[:, half:])

    out = acc[...] / total
    pairs = len(o_refs)
    per_row = H // (2 * pairs)
    for h in range(H):
        at, q_at = h // per_row, h % per_row
        out_all[at // 2, slot, at % 2:at % 2 + 1, q_at * HD:(q_at + 1) * HD] = out[h:h + 1]

    @pl.when(slot == slots - 1)
    def _():
        for k in range(pairs):
            home = lax.rem(lax.axis_index("rp") + k, pairs)
            o_refs[k][...] = jnp.concatenate([out_all[home, j] for j in range(slots)], axis=0).astype(jnp.bfloat16)


def attention(queries, new_entries, cache_keys, cache_values, lengths, pairs):
    slots = queries.shape[0]
    half = cache_keys.shape[2] // 2
    width = KVH * HD
    low = pl.BlockSpec((1, 1, half, width), lambda s, n: (0, s, 0, 0))

    def last_long(s, n):
        at = 0
        for j in range(1, slots):
            at = jnp.where((s >= j) & (n[j] > half), j, at)
        return (0, at, 1, 0)

    high = pl.BlockSpec((1, 1, half, width), last_long)
    heads = H * HD // (2 * pairs)
    grid_spec = pltpu.PrefetchScalarGridSpec(
        num_scalar_prefetch=1, grid=(slots,),
        in_specs=[pl.BlockSpec((slots, H * HD), lambda s, n: (0, 0)), pl.BlockSpec((slots, 2 * width), lambda s, n: (0, 0)), low, high, low, high],
        out_specs=[pl.BlockSpec((2 * slots, heads), lambda s, n: (0, 0))] * pairs,
        scratch_shapes=[
            pltpu.VMEM((slots, H, HD), jnp.float32), pltpu.VMEM((slots, 2 * KVH, HD), jnp.float32),
            pltpu.VMEM((H, 2 * half), jnp.float32), pltpu.VMEM((H, HD), jnp.float32), pltpu.VMEM((pairs, slots, 2, heads), jnp.float32),
            pltpu.VMEM((slots, 2, 16, HD), jnp.float32), pltpu.VMEM((slots, 2, 2 * half // 16, HD), jnp.float32), pltpu.VMEM((slots, 2, 8, HD), jnp.float32)])
    return pl.pallas_call(
        attend_kernel, grid_spec=grid_spec,
        out_shape=[jax.ShapeDtypeStruct((2 * slots, heads), jnp.bfloat16)] * pairs,
        compiler_params=pltpu.CompilerParams(vmem_limit_bytes=60 << 20), name="attend",
    )(lengths, queries, new_entries, cache_keys, cache_keys, cache_values, cache_values)


def flip(value, axis):
    return lax.ppermute(value, axis, [(0, 1), (1, 0)])


def turn(value, steps):
    count = lax.axis_size("rp")
    return lax.ppermute(value, "rp", [(i, (i + steps) % count) for i in range(count)])


def to_ffn(value, steps):
    count = lax.axis_size("rp")
    return lax.ppermute(value, ("side", "rp"), [(i, count + (i + steps) % count) for i in range(count)])


def exchange(value, axes):
    return lax.all_to_all(value, axes, split_axis=0, concat_axis=0, tiled=True)


def matmul(left, right):
    return jnp.dot(left, right, preferred_element_type=jnp.float32)


def call(kernel, name, out_shape, **options):
    limit = options.pop("limit", 24)
    return pl.pallas_call(kernel, out_shape=out_shape, name=name, compiler_params=pltpu.CompilerParams(vmem_limit_bytes=limit << 20), **options)


def fan_kernel(*refs):
    blocks, o_ref = refs[:-3], refs[-1]
    rows = blocks[0].shape[0]
    for i in range(o_ref.shape[0]):
        for k, block in enumerate(blocks):
            o_ref[i, k * rows:(k + 1) * rows] = block[...]


def project_kernel(pairs, left_ref, own_ref, pair_a_ref, pair_b_ref, *refs):
    near_refs, o_refs = (refs[:pairs], refs[pairs:]) if len(refs) == 2 * pairs else ((), refs[:pairs])
    core, low = lax.axis_index("core"), lax.axis_index("rl")
    group = left_ref.shape[0] // (2 * pairs)
    slots = 4
    rows = pairs * group
    cut = pair_a_ref.shape[0]
    to = lax.broadcasted_iota(jnp.int32, (rows, 2 * rows), 0)
    source = lax.broadcasted_iota(jnp.int32, (rows, 2 * rows), 1)
    block = (pairs - to // group) % pairs
    first = ((to % group) // slots) * (2 * slots * pairs) + block * (2 * slots) + (to % slots) * 2
    pick_own = (source == first + low).astype(jnp.bfloat16)
    pick_pair = (source == first + 1 - low).astype(jnp.bfloat16)
    part = matmul(matmul(pick_own, left_ref[...]).astype(jnp.bfloat16), own_ref[0])
    theirs = matmul(pick_pair, left_ref[...]).astype(jnp.bfloat16)
    part = (part + matmul(theirs[:, :cut], pair_a_ref[...]) + matmul(theirs[:, cut:], pair_b_ref[...])).astype(jnp.bfloat16)
    for k in range(pairs):
        if near_refs:
            o_refs[k][core] = near_refs[k][...]
            o_refs[k][1 - core] = part[k * group:(k + 1) * group]
        else:
            o_refs[k][...] = part[k * group:(k + 1) * group]


def stream_kernel(*refs):
    parts, (residual_ref, gain_ref, stream_ref, copies_ref) = refs[:-4], refs[-4:]
    group = stream_ref.shape[0]
    chips = group // 8
    row = lax.axis_index("rp") * 2 + lax.axis_index("rl")
    to = lax.broadcasted_iota(jnp.int32, (group, group), 0)
    source = lax.broadcasted_iota(jnp.int32, (group, group), 1)
    order = (source == (to // 4 % chips) * 8 + (to // (4 * chips)) * 4 + to % 4).astype(jnp.bfloat16)
    stream = matmul(order, residual_ref[pl.ds(pl.multiple_of(row * group, group), group), :])
    for part_ref in parts:
        stream = stream + part_ref[...].astype(jnp.float32)
    stream_ref[...] = stream
    scaled = (stream * gain_ref[...].astype(jnp.float32)).astype(jnp.bfloat16)
    for i in range(copies_ref.shape[0]):
        copies_ref[i] = scaled


def gate_up_kernel(x_ref, gain_ref, gate_ref, up_ref, *rest):
    other_ref, o_ref = rest if len(rest) == 2 else (None, rest[0])
    half = gate_ref.shape[1]
    x = x_ref[...]
    one = x.astype(jnp.float32) * (1.0 / gain_ref[...].astype(jnp.float32))
    squares = jnp.sum(one * one, axis=1, keepdims=True)
    gate, up = matmul(x, gate_ref[...]), matmul(x, up_ref[...])
    lane = lax.broadcasted_iota(jnp.int32, (x.shape[0], 128), 1)
    if other_ref is not None:
        gate = gate + other_ref[:, :half]
        up = up + other_ref[:, half:2 * half]
        squares = squares + other_ref[:, 2 * half:]
        high = squares.astype(jnp.bfloat16).astype(jnp.float32)
        squares = jnp.where(lane == 0, high, jnp.where(lane == 1, squares - high, 0.0))
    o_ref[:, :half] = gate.astype(o_ref.dtype)
    o_ref[:, half:2 * half] = up.astype(o_ref.dtype)
    o_ref[:, 2 * half:] = jnp.broadcast_to(squares, lane.shape).astype(o_ref.dtype)


def hidden_kernel(parts_ref, copies_ref):
    half = copies_ref.shape[2]
    sums = parts_ref[0].astype(jnp.float32)
    for i in range(1, parts_ref.shape[0]):
        sums = sums + parts_ref[i].astype(jnp.float32)
    squares = sums[:, 2 * half:2 * half + 1] + sums[:, 2 * half + 1:2 * half + 2]
    inv_rms = lax.rsqrt(squares / D + eps)
    gate = sums[:, :half] * inv_rms
    up = sums[:, half:2 * half] * inv_rms
    hidden = (gate / (1.0 + jnp.exp(-gate)) * up).astype(jnp.bfloat16)
    for i in range(copies_ref.shape[0]):
        copies_ref[i] = hidden


def down_kernel(x_ref, weight_ref, *rest):
    other_ref, o_ref = rest if len(rest) == 2 else (None, rest[0])
    half = x_ref.shape[1]
    core = lax.axis_index("core")
    at = core if other_ref is None else 1 - core
    part = matmul(x_ref[...], weight_ref[0, pl.ds(pl.multiple_of(at * half, half), half), :])
    if other_ref is not None:
        part = part + other_ref[...]
    o_ref[...] = part.astype(o_ref.dtype)


def final_kernel(parts_ref, stream_ref, copies_ref):
    total = parts_ref[0].astype(jnp.float32)
    for i in range(1, parts_ref.shape[0]):
        total = total + parts_ref[i].astype(jnp.float32)
    final = stream_ref[...] + total
    count, slots = copies_ref.shape[0] // 2, copies_ref.shape[1]
    for i in range(count):
        block = final[i * slots:(i + 1) * slots].astype(jnp.bfloat16)
        copies_ref[i] = block
        copies_ref[count + i] = block


def output_kernel(back_ref, o_ref):
    width = back_ref.shape[2]
    chips = back_ref.shape[0] // 4
    half = chips // 2
    side = lax.axis_index("side")
    for chip in range(half):
        for core in range(2):
            at = (2 * chip + core) * width
            o_ref[:, at:at + width] = back_ref[(2 + core) * chips + side * half + chip]


def local(queries, new_entries, cache_keys, cache_values, lengths, residual, norm_gain, out_weight, gate_weight, up_weight, down_weight):
    bf16 = jnp.bfloat16
    rows, pairs, chips = lax.axis_size(ROW), lax.axis_size("rp"), lax.axis_size(CHIPS)
    core = lax.axis_index("core")
    slots, width = queries.shape[0], out_weight.shape[2]
    heads = out_weight.shape[1]
    half = gate_weight.shape[2] // 2
    group = chips * 2 * slots
    total = rows * group
    cut = heads // 16 * 11
    pair_a = flip(out_weight[0, :cut], "rl")
    pair_b = flip(out_weight[0, cut:], "rl")
    gain = norm_gain[None, :]
    gain_theirs = flip(norm_gain, "core")
    gate_theirs = flip(lax.dynamic_slice_in_dim(gate_weight[0], (1 - core) * half, half, 1), "core")
    up_theirs = flip(lax.dynamic_slice_in_dim(up_weight[0], (1 - core) * half, half, 1), "core")

    gate_mine = lax.dynamic_slice_in_dim(gate_weight[0], core * half, half, 1)
    up_mine = lax.dynamic_slice_in_dim(up_weight[0], core * half, half, 1)
    blocks = attention(queries, new_entries, cache_keys, cache_values, lengths, pairs)
    blocks = [to_ffn(block, k) for k, block in enumerate(blocks)]
    fanned = call(fan_kernel, "fan", jax.ShapeDtypeStruct((chips, pairs * 2 * slots, heads), bf16), in_specs=[WHOLE] * pairs + [HELD, HELD], out_specs=WHOLE)(*blocks, pair_a, gain_theirs)
    near = exchange(fanned, CHIPS).reshape(chips * pairs * 2 * slots, heads)
    near_parts = call(functools.partial(project_kernel, pairs), "project_near", [jax.ShapeDtypeStruct((group // 2, width), bf16)] * pairs + [jax.ShapeDtypeStruct(near.shape, bf16)], in_specs=[WHOLE] * 4, out_specs=[WHOLE] * pairs + [HELD],
        input_output_aliases={0: pairs})(near, out_weight, pair_a, pair_b)
    *near_parts, near = near_parts
    far = flip(near, "core")
    own, *parts = call(functools.partial(project_kernel, pairs), "project", [jax.ShapeDtypeStruct((2, group // 2, width), bf16)] * pairs, in_specs=[WHOLE] * (4 + pairs), out_specs=[WHOLE] * pairs)(
        far, out_weight, pair_a, pair_b, *near_parts)
    parts = [own] + [turn(part, k + 1) for k, part in enumerate(parts)]
    parts = [part.reshape(group, width) for part in parts]
    stream, copies = call(stream_kernel, "stream", (jax.ShapeDtypeStruct((group, width), jnp.float32), jax.ShapeDtypeStruct((rows, group, width), bf16)), in_specs=[WHOLE] * (pairs + 2), out_specs=(WHOLE, WHOLE))(
        *parts, residual, gain)
    scaled = exchange(copies, HOME).reshape(total, width)
    scaled_theirs = flip(scaled, "core")
    wide = 2 * half + 128
    own = call(gate_up_kernel, "gate_up_own", jax.ShapeDtypeStruct((total, wide), jnp.float32), in_specs=[WHOLE] * 4, out_specs=WHOLE)(scaled, gain, gate_mine, up_mine)
    sent = call(gate_up_kernel, "gate_up", jax.ShapeDtypeStruct((total, wide), bf16), in_specs=[WHOLE] * 5, out_specs=WHOLE)(
        scaled_theirs, gain_theirs[None, :], gate_theirs, up_theirs, own)
    sums = exchange(sent.reshape(chips, group, 2 * half + 128), CHIPS)
    hidden = call(hidden_kernel, "hidden", jax.ShapeDtypeStruct((chips, group, half), bf16), in_specs=[WHOLE], out_specs=WHOLE)(sums)
    hidden = exchange(hidden, CHIPS).reshape(total, half)
    hidden_theirs = flip(hidden, "core")
    own = call(down_kernel, "down_own", jax.ShapeDtypeStruct((total, width), jnp.float32), in_specs=[WHOLE] * 2, out_specs=WHOLE)(hidden, down_weight)
    down = call(down_kernel, "down", jax.ShapeDtypeStruct((total, width), bf16), in_specs=[WHOLE] * 3, out_specs=WHOLE)(hidden_theirs, down_weight, own)
    downs = exchange(down.reshape(rows, group, width), HOME)
    final = call(final_kernel, "final", jax.ShapeDtypeStruct((4 * chips, slots, width), bf16), in_specs=[WHOLE] * 2, out_specs=WHOLE)(downs, stream)
    back = exchange(final, ("side", "core") + CHIPS)
    return call(output_kernel, "output", jax.ShapeDtypeStruct((slots, width * chips), bf16), in_specs=[WHOLE], out_specs=WHOLE)(back)


def solution(mesh):
    sides, rows, cols = mesh.devices.shape
    inner = Mesh(mesh.devices.reshape(sides, rows // 2, 2, cols // 4, 2, 2), ("side",) + ROW + COL)
    in_specs = (
        P(ROW + COL, None),
        P(ROW + COL, None),
        P("side", ROW + COL, None, None),
        P("side", ROW + COL, None, None),
        P(ROW + COL),
        P(None, COL),
        P(COL),
        P("side", ROW, COL),
        P("side", COL, ROW),
        P("side", COL, ROW),
        P("side", ROW, COL),
    )
    return jax.shard_map(local, mesh=inner, in_specs=in_specs, out_specs=P(ROW + COL, "side"), check_vma=False)
```

```python
import functools
import math
import jax
import jax.numpy as jnp
from jax import lax
from jax.experimental import pallas as pl
from jax.experimental.pallas import tpu as pltpu
from jax.sharding import Mesh, PartitionSpec as P

D = 8192
H = 64
KVH = 8
HD = 128
ORIG = 64
PER = H // KVH

rope_theta = 500000.0
stretch_factor = 8.0
eps = 1e-05

CHIPS = ("x", "yl")
COL = ("x", "yl", "core")
ROW = ("rp", "rl")
HOME = ("rl", "rp")
WHOLE = pl.BlockSpec(memory_space=pltpu.VMEM)
HELD = pl.BlockSpec(memory_space=pl.ANY)
SCALARS = pl.BlockSpec(memory_space=pltpu.SMEM)


def swap_halves(v):
    return jnp.concatenate([v[:, HD // 2:], v[:, : HD // 2]], axis=-1)


def attend_kernel(len_ref, q_ref, new_ref, k_lo_ref, k_hi_ref, v_lo_ref, v_hi_ref, *rest):
    o_ref, q_all, new_all, s_all, acc, out_all, fine_all, coarse_all, at_all = rest
    slot = pl.program_id(0)
    slots = q_ref.shape[0]
    length = len_ref[slot]
    half = k_lo_ref.shape[2]
    span = 2 * half

    @pl.when(slot == 0)
    def _():
        for h in range(H):
            q_all[:, h, :] = q_ref[:, h * HD:(h + 1) * HD].astype(jnp.float32)
        for h in range(2 * KVH):
            new_all[:, h, :] = new_ref[:, h * HD:(h + 1) * HD].astype(jnp.float32)

    steps = span // 16
    lane = lax.broadcasted_iota(jnp.int32, (1, HD), 1)
    sign = jnp.where(lane < HD // 2, -1.0, 1.0)

    @pl.when(slot == 0)
    def _():
        pair = jnp.where(lane < HD // 2, lane, lane - HD // 2).astype(jnp.float32)
        positions = jnp.concatenate([jnp.full((8, HD), len_ref[j], jnp.int32) for j in range(slots)], axis=0).astype(jnp.float32)
        stretch = jnp.maximum(stretch_factor * (positions + 1.0) / ORIG - (stretch_factor - 1.0), 1.0)
        log_base = math.log(rope_theta) + HD / (HD - 2.0) * jnp.log(stretch)
        freqs = jnp.exp(-(pair * (2.0 / HD)) * log_base)
        low = lax.broadcasted_iota(jnp.int32, (16, HD), 0).astype(jnp.float32)
        high = lax.broadcasted_iota(jnp.int32, (steps, HD), 0).astype(jnp.float32) * 16.0
        each = [freqs[8 * j:8 * j + 1] for j in range(slots)]
        angles = jnp.concatenate([low * f for f in each] + [high * f for f in each] + [positions * freqs], axis=0)
        cosine, sine = jnp.cos(angles), jnp.sin(angles)
        for j in range(slots):
            fine_all[j, 0] = cosine[16 * j:16 * j + 16]
            fine_all[j, 1] = sine[16 * j:16 * j + 16]
            at = 16 * slots + steps * j
            coarse_all[j, 0] = cosine[at:at + steps]
            coarse_all[j, 1] = sine[at:at + steps]
            at = (16 + steps) * slots + 8 * j
            at_all[j, 0] = cosine[at:at + 8]
            at_all[j, 1] = sine[at:at + 8]

    fine_cos, fine_sin = fine_all[slot, 0], fine_all[slot, 1]
    coarse_cos, coarse_sin = coarse_all[slot, 0], coarse_all[slot, 1]

    def tables(first):
        cos_parts, sin_parts = [], []
        for step in range(first, first + steps // 2):
            cc, cs = coarse_cos[step:step + 1], coarse_sin[step:step + 1]
            cos_parts.append(cc * fine_cos - cs * fine_sin)
            sin_parts.append(cs * fine_cos + cc * fine_sin)
        return jnp.concatenate(cos_parts, axis=0), jnp.concatenate(sin_parts, axis=0)

    cos_new = at_all[slot, 0, :1]
    sin_new = at_all[slot, 1, :1] * sign
    q = q_all[slot]
    q_rot = q * cos_new + swap_halves(q) * sin_new
    q_rot = q_rot.astype(jnp.bfloat16).astype(jnp.float32)
    q_both = jnp.concatenate([q_rot, swap_halves(q_rot) * -sign], axis=-1)
    k_new = new_all[slot, :KVH]
    k_new = k_new * cos_new + swap_halves(k_new) * sin_new
    k_new = k_new.astype(jnp.bfloat16).astype(jnp.float32)
    v_new = new_all[slot, KVH:]
    scale = HD ** (-0.5)

    def score(k_ref, first):
        cos_t, sin_t = tables(first)
        for g in range(KVH):
            kg = k_ref[0, 0, :, g * HD:(g + 1) * HD].astype(jnp.float32)
            kk = jnp.concatenate([(kg * cos_t).astype(jnp.bfloat16), (kg * sin_t).astype(jnp.bfloat16)], axis=-1)
            qg = q_both[g * PER:(g + 1) * PER].astype(jnp.bfloat16)
            s_all[g * PER:(g + 1) * PER, first * 16:first * 16 + half] = lax.dot_general(qg, kk, (((1,), (1,)), ((), ())), preferred_element_type=jnp.float32)

    score(k_lo_ref, 0)

    @pl.when(length > half)
    def _():
        score(k_hi_ref, steps // 2)

    @pl.when(length <= half)
    def _():
        s_all[:, half:] = jnp.zeros((H, half), jnp.float32)

    own, fresh = [], []
    for g in range(KVH):
        own.append(jnp.sum(q_rot[g * PER:(g + 1) * PER] * k_new[g:g + 1], axis=-1, keepdims=True))
        fresh.append(jnp.broadcast_to(v_new[g:g + 1], (PER, HD)))
    own_score = jnp.concatenate(own, axis=0) * scale
    valid = lax.broadcasted_iota(jnp.int32, (H, span), 1) < length
    s = jnp.where(valid, s_all[...] * scale, -1e30)
    top = jnp.maximum(jnp.max(s, axis=-1, keepdims=True), own_score)
    w = jnp.where(valid, jnp.exp(s - top), 0.0)
    own_w = jnp.exp(own_score - top)
    total = jnp.sum(w, axis=-1, keepdims=True) + own_w
    w16 = w.astype(jnp.bfloat16)

    def mix(v_ref, weights):
        parts = []
        for p in range(KVH // 2):
            o = jnp.dot(weights[p * 2 * PER:(p + 1) * 2 * PER], v_ref[0, 0, :, p * 2 * HD:(p + 1) * 2 * HD], preferred_element_type=jnp.float32)
            parts += [o[:PER, :HD], o[PER:, HD:]]
        return jnp.concatenate(parts, axis=0)

    acc[...] = mix(v_lo_ref, w16[:, :half]) + own_w * jnp.concatenate(fresh, axis=0)

    @pl.when(length > half)
    def _():
        acc[...] += mix(v_hi_ref, w16[:, half:])

    out = acc[...] / total
    pairs = o_ref.shape[0]
    per_row = H // (2 * pairs)
    for h in range(H):
        at, q_at = h // per_row, h % per_row
        out_all[at // 2, slot, at % 2:at % 2 + 1, q_at * HD:(q_at + 1) * HD] = out[h:h + 1]

    @pl.when(slot == slots - 1)
    def _():
        for k in range(pairs):
            o_ref[k] = jnp.concatenate([out_all[k, j] for j in range(slots)], axis=0).astype(jnp.bfloat16)


def attention(queries, new_entries, cache_keys, cache_values, lengths, pairs):
    slots = queries.shape[0]
    half = cache_keys.shape[2] // 2
    width = KVH * HD
    low = pl.BlockSpec((1, 1, half, width), lambda s, n: (0, s, 0, 0))

    def last_long(s, n):
        at = 0
        for j in range(1, slots):
            at = jnp.where((s >= j) & (n[j] > half), j, at)
        return (0, at, 1, 0)

    high = pl.BlockSpec((1, 1, half, width), last_long)
    heads = H * HD // (2 * pairs)
    grid_spec = pltpu.PrefetchScalarGridSpec(
        num_scalar_prefetch=1, grid=(slots,),
        in_specs=[pl.BlockSpec((slots, H * HD), lambda s, n: (0, 0)), pl.BlockSpec((slots, 2 * width), lambda s, n: (0, 0)), low, high, low, high],
        out_specs=pl.BlockSpec((pairs, 2 * slots, heads), lambda s, n: (0, 0, 0)),
        scratch_shapes=[
            pltpu.VMEM((slots, H, HD), jnp.float32), pltpu.VMEM((slots, 2 * KVH, HD), jnp.float32),
            pltpu.VMEM((H, 2 * half), jnp.float32), pltpu.VMEM((H, HD), jnp.float32), pltpu.VMEM((pairs, slots, 2, heads), jnp.float32),
            pltpu.VMEM((slots, 2, 16, HD), jnp.float32), pltpu.VMEM((slots, 2, 2 * half // 16, HD), jnp.float32), pltpu.VMEM((slots, 2, 8, HD), jnp.float32)])
    return pl.pallas_call(
        attend_kernel, grid_spec=grid_spec,
        out_shape=jax.ShapeDtypeStruct((pairs, 2 * slots, heads), jnp.bfloat16),
        compiler_params=pltpu.CompilerParams(vmem_limit_bytes=60 << 20), name="attend",
    )(lengths, queries, new_entries, cache_keys, cache_keys, cache_values, cache_values)


def flip(value, axis):
    return lax.ppermute(value, axis, [(0, 1), (1, 0)])


def turn(value, steps):
    count = lax.axis_size("rp")
    return lax.ppermute(value, "rp", [(i, (i + steps) % count) for i in range(count)])


def to_ffn(value, steps):
    count = lax.axis_size("rp")
    return lax.ppermute(value, ("side", "rp"), [(i, count + (i + steps) % count) for i in range(count)])


def exchange(value, axes):
    return lax.all_to_all(value, axes, split_axis=0, concat_axis=0, tiled=True)


def matmul(left, right):
    return jnp.dot(left, right, preferred_element_type=jnp.float32)


def call(kernel, name, out_shape, **options):
    limit = options.pop("limit", 24)
    return pl.pallas_call(kernel, out_shape=out_shape, name=name, compiler_params=pltpu.CompilerParams(vmem_limit_bytes=limit << 20), **options)


def fan_kernel(block_ref, held_ref, also_held_ref, o_ref):
    rows = block_ref.shape[1]
    for i in range(o_ref.shape[0]):
        for k in range(block_ref.shape[0]):
            o_ref[i, k * rows:(k + 1) * rows] = block_ref[k]


def project_kernel(pairs, left_ref, own_ref, pair_a_ref, pair_b_ref, *refs):
    near_refs, o_refs = (refs[:pairs], refs[pairs:]) if len(refs) == 2 * pairs else ((), refs[:pairs])
    core, low = lax.axis_index("core"), lax.axis_index("rl")
    group = left_ref.shape[0] // (2 * pairs)
    slots = 4
    rows = pairs * group
    cut = pair_a_ref.shape[0]
    to = lax.broadcasted_iota(jnp.int32, (rows, 2 * rows), 0)
    source = lax.broadcasted_iota(jnp.int32, (rows, 2 * rows), 1)
    block = (lax.axis_index("rp") + to // group) % pairs
    first = ((to % group) // slots) * (2 * slots * pairs) + block * (2 * slots) + (to % slots) * 2
    pick_own = (source == first + low).astype(jnp.bfloat16)
    pick_pair = (source == first + 1 - low).astype(jnp.bfloat16)
    part = matmul(matmul(pick_own, left_ref[...]).astype(jnp.bfloat16), own_ref[0])
    theirs = matmul(pick_pair, left_ref[...]).astype(jnp.bfloat16)
    part = (part + matmul(theirs[:, :cut], pair_a_ref[...]) + matmul(theirs[:, cut:], pair_b_ref[...])).astype(jnp.bfloat16)
    for k in range(pairs):
        if near_refs:
            o_refs[k][core] = near_refs[k][...]
            o_refs[k][1 - core] = part[k * group:(k + 1) * group]
        else:
            o_refs[k][...] = part[k * group:(k + 1) * group]


def stream_kernel(*refs):
    parts, (residual_ref, gain_ref, stream_ref, copies_ref) = refs[:-4], refs[-4:]
    group = stream_ref.shape[0]
    chips = group // 8
    row = lax.axis_index("rp") * 2 + lax.axis_index("rl")
    to = lax.broadcasted_iota(jnp.int32, (group, group), 0)
    source = lax.broadcasted_iota(jnp.int32, (group, group), 1)
    order = (source == (to // 4 % chips) * 8 + (to // (4 * chips)) * 4 + to % 4).astype(jnp.bfloat16)
    stream = matmul(order, residual_ref[pl.ds(pl.multiple_of(row * group, group), group), :])
    for part_ref in parts:
        stream = stream + part_ref[...].astype(jnp.float32)
    stream_ref[...] = stream
    scaled = (stream * gain_ref[...].astype(jnp.float32)).astype(jnp.bfloat16)
    for i in range(copies_ref.shape[0]):
        copies_ref[i] = scaled


def gate_up_kernel(x_ref, gain_ref, gate_ref, up_ref, *rest):
    other_ref, o_ref = rest if len(rest) == 2 else (None, rest[0])
    half = gate_ref.shape[1]
    x = x_ref[...]
    one = x.astype(jnp.float32) * (1.0 / gain_ref[...].astype(jnp.float32))
    squares = jnp.sum(one * one, axis=1, keepdims=True)
    gate, up = matmul(x, gate_ref[...]), matmul(x, up_ref[...])
    lane = lax.broadcasted_iota(jnp.int32, (x.shape[0], 128), 1)
    if other_ref is not None:
        gate = gate + other_ref[:, :half]
        up = up + other_ref[:, half:2 * half]
        squares = squares + other_ref[:, 2 * half:]
        high = squares.astype(jnp.bfloat16).astype(jnp.float32)
        squares = jnp.where(lane == 0, high, jnp.where(lane == 1, squares - high, 0.0))
    o_ref[:, :half] = gate.astype(o_ref.dtype)
    o_ref[:, half:2 * half] = up.astype(o_ref.dtype)
    o_ref[:, 2 * half:] = jnp.broadcast_to(squares, lane.shape).astype(o_ref.dtype)


def hidden_kernel(parts_ref, copies_ref):
    half = copies_ref.shape[2]
    sums = parts_ref[0].astype(jnp.float32)
    for i in range(1, parts_ref.shape[0]):
        sums = sums + parts_ref[i].astype(jnp.float32)
    squares = sums[:, 2 * half:2 * half + 1] + sums[:, 2 * half + 1:2 * half + 2]
    inv_rms = lax.rsqrt(squares / D + eps)
    gate = sums[:, :half] * inv_rms
    up = sums[:, half:2 * half] * inv_rms
    hidden = (gate / (1.0 + jnp.exp(-gate)) * up).astype(jnp.bfloat16)
    for i in range(copies_ref.shape[0]):
        copies_ref[i] = hidden


def down_kernel(x_ref, weight_ref, *rest):
    other_ref, o_ref = rest if len(rest) == 2 else (None, rest[0])
    half = x_ref.shape[1]
    core = lax.axis_index("core")
    at = core if other_ref is None else 1 - core
    part = matmul(x_ref[...], weight_ref[0, pl.ds(pl.multiple_of(at * half, half), half), :])
    if other_ref is not None:
        part = part + other_ref[...]
    o_ref[...] = part.astype(o_ref.dtype)


def final_kernel(parts_ref, stream_ref, copies_ref):
    total = parts_ref[0].astype(jnp.float32)
    for i in range(1, parts_ref.shape[0]):
        total = total + parts_ref[i].astype(jnp.float32)
    final = stream_ref[...] + total
    count, slots = copies_ref.shape[0] // 2, copies_ref.shape[1]
    for i in range(count):
        block = final[i * slots:(i + 1) * slots].astype(jnp.bfloat16)
        copies_ref[i] = block
        copies_ref[count + i] = block


def output_kernel(back_ref, o_ref):
    width = back_ref.shape[2]
    chips = back_ref.shape[0] // 4
    half = chips // 2
    side = lax.axis_index("side")
    for chip in range(half):
        for core in range(2):
            at = (2 * chip + core) * width
            o_ref[:, at:at + width] = back_ref[(2 + core) * chips + side * half + chip]


def local(queries, new_entries, cache_keys, cache_values, lengths, residual, norm_gain, out_weight, gate_weight, up_weight, down_weight):
    bf16 = jnp.bfloat16
    rows, pairs, chips = lax.axis_size(ROW), lax.axis_size("rp"), lax.axis_size(CHIPS)
    core = lax.axis_index("core")
    slots, width = queries.shape[0], out_weight.shape[2]
    heads = out_weight.shape[1]
    half = gate_weight.shape[2] // 2
    group = chips * 2 * slots
    total = rows * group
    cut = heads // 16 * 11
    pair_a = flip(out_weight[0, :cut], "rl")
    pair_b = flip(out_weight[0, cut:], "rl")
    gain = norm_gain[None, :]
    gain_theirs = flip(norm_gain, "core")
    gate_theirs = flip(lax.dynamic_slice_in_dim(gate_weight[0], (1 - core) * half, half, 1), "core")
    up_theirs = flip(lax.dynamic_slice_in_dim(up_weight[0], (1 - core) * half, half, 1), "core")

    gate_mine = lax.dynamic_slice_in_dim(gate_weight[0], core * half, half, 1)
    up_mine = lax.dynamic_slice_in_dim(up_weight[0], core * half, half, 1)
    blocks = attention(queries, new_entries, cache_keys, cache_values, lengths, pairs)
    blocks = exchange(lax.ppermute(blocks, "side", [(0, 1)]), "rp")
    fanned = call(fan_kernel, "fan", jax.ShapeDtypeStruct((chips, pairs * 2 * slots, heads), bf16), in_specs=[WHOLE, HELD, HELD], out_specs=WHOLE)(blocks, pair_a, gain_theirs)
    near = exchange(fanned, CHIPS).reshape(chips * pairs * 2 * slots, heads)
    near_parts = call(functools.partial(project_kernel, pairs), "project_near", [jax.ShapeDtypeStruct((group // 2, width), bf16)] * pairs + [jax.ShapeDtypeStruct(near.shape, bf16)], in_specs=[WHOLE] * 4, out_specs=[WHOLE] * pairs + [HELD],
        input_output_aliases={0: pairs})(near, out_weight, pair_a, pair_b)
    *near_parts, near = near_parts
    far = flip(near, "core")
    own, *parts = call(functools.partial(project_kernel, pairs), "project", [jax.ShapeDtypeStruct((2, group // 2, width), bf16)] * pairs, in_specs=[WHOLE] * (4 + pairs), out_specs=[WHOLE] * pairs)(
        far, out_weight, pair_a, pair_b, *near_parts)
    parts = [own] + [turn(part, k + 1) for k, part in enumerate(parts)]
    parts = [part.reshape(group, width) for part in parts]
    stream, copies = call(stream_kernel, "stream", (jax.ShapeDtypeStruct((group, width), jnp.float32), jax.ShapeDtypeStruct((rows, group, width), bf16)), in_specs=[WHOLE] * (pairs + 2), out_specs=(WHOLE, WHOLE))(
        *parts, residual, gain)
    scaled = exchange(copies, HOME).reshape(total, width)
    scaled_theirs = flip(scaled, "core")
    wide = 2 * half + 128
    own = call(gate_up_kernel, "gate_up_own", jax.ShapeDtypeStruct((total, wide), jnp.float32), in_specs=[WHOLE] * 4, out_specs=WHOLE)(scaled, gain, gate_mine, up_mine)
    sent = call(gate_up_kernel, "gate_up", jax.ShapeDtypeStruct((total, wide), bf16), in_specs=[WHOLE] * 5, out_specs=WHOLE)(
        scaled_theirs, gain_theirs[None, :], gate_theirs, up_theirs, own)
    sums = exchange(sent.reshape(chips, group, 2 * half + 128), CHIPS)
    hidden = call(hidden_kernel, "hidden", jax.ShapeDtypeStruct((chips, group, half), bf16), in_specs=[WHOLE], out_specs=WHOLE)(sums)
    hidden = exchange(hidden, CHIPS).reshape(total, half)
    hidden_theirs = flip(hidden, "core")
    own = call(down_kernel, "down_own", jax.ShapeDtypeStruct((total, width), jnp.float32), in_specs=[WHOLE] * 2, out_specs=WHOLE)(hidden, down_weight)
    down = call(down_kernel, "down", jax.ShapeDtypeStruct((total, width), bf16), in_specs=[WHOLE] * 3, out_specs=WHOLE)(hidden_theirs, down_weight, own)
    downs = exchange(down.reshape(rows, group, width), HOME)
    final = call(final_kernel, "final", jax.ShapeDtypeStruct((4 * chips, slots, width), bf16), in_specs=[WHOLE] * 2, out_specs=WHOLE)(downs, stream)
    back = exchange(final, ("side", "core") + CHIPS)
    return call(output_kernel, "output", jax.ShapeDtypeStruct((slots, width * chips), bf16), in_specs=[WHOLE], out_specs=WHOLE)(back)


def solution(mesh):
    sides, rows, cols = mesh.devices.shape
    inner = Mesh(mesh.devices.reshape(sides, rows // 2, 2, cols // 4, 2, 2), ("side",) + ROW + COL)
    in_specs = (
        P(ROW + COL, None),
        P(ROW + COL, None),
        P("side", ROW + COL, None, None),
        P("side", ROW + COL, None, None),
        P(ROW + COL),
        P(None, COL),
        P(COL),
        P("side", ROW, COL),
        P("side", COL, ROW),
        P("side", COL, ROW),
        P("side", ROW, COL),
    )
    return jax.shard_map(local, mesh=inner, in_specs=in_specs, out_specs=P(ROW + COL, "side"), check_vma=False)
```
